512 devices in a mesh: tm: 64 (over y, z), rows: 8 (over x, core).
Axes of the slice: x: 4, y: 4, z: 16, core: 2. Of those that a mesh axis runs over, the one named last changes fastest.
Arguments:
- states: float32 [128, 64, 640], P('tm'), may hold values from -6 to 6
- ancestors: int32 [128, 640], P('tm'), may hold values from 0 to 639
- tracer_obs: float32 [128, 32], P('tm'), may hold values from -6 to 6
- jitter: float32 [128], P('tm'), may hold values from 0.00390625 to 0.0390625
- fingerprints: float32 [64, 32], replicated, may hold values from -0.75 to 0.75
- tracer_scale: float32 [32], replicated, may hold values from 0.15 to 0.45
- prior_weights: float32 [640], replicated, may hold values from 0.25 to 4
Outputs:
- filtered: float32 [128, 640], P('tm', 'rows')
The draws below stay inside these ranges and needn't reach their ends.
All inputs are finite; a program needn't handle non-finite values.
Results may differ from the reference program's by a relative error of at most 0.0003.
Values sent between devices are 32-bit elements; how exact they have to be, the bound alone decides.
A program may use at most 64 MiB of HBM per device.

```python
import math
import jax
import jax.numpy as jnp
from jax import lax

PARTICLES = 640
STATES = 64
TRACERS = 32
TSTEPS = 128


def with_ends(result, rng, smallest, high):
    extent = result.shape
    index_at = [jax.random.randint(jax.random.fold_in(rng, axis), (), 0, extent[axis]) for axis in range(len(extent))]
    result = result.at[tuple(index_at)].set(smallest)
    longest = extent.index(max(extent))
    index_at[longest] = (index_at[longest] + 1) % extent[longest]
    return result.at[tuple(index_at)].set(high)


def block_scale(stream_key, shape, cuts, low, top_value):
    def one(axis_at, shards_of):
        heights = jax.random.uniform(jax.random.fold_in(jax.random.fold_in(stream_key, 6), axis_at), (shards_of,), jnp.float32, low / len(cuts), top_value / len(cuts))
        return jnp.repeat(jnp.exp(heights), shape[axis_at] // shards_of).reshape((-1,) + (1,) * (len(shape) - axis_at - 1))

    level = one(*cuts[0])
    for cut in cuts[1:]:
        level = level * one(*cut)
    return level


def centred(stream_key, shape, deviation, most, shards=(), kind=jnp.bfloat16):
    loudness = block_scale(stream_key, shape, shards, -0.22, 0.18) if shards else 1.0
    entries = jax.random.normal(stream_key, shape, jnp.float32) * deviation * loudness
    return jnp.minimum(jnp.maximum(entries, -most), most).astype(kind)


def setup_inputs(seed: int = 0) -> dict:
    seeds = jax.random.split(jax.random.key(seed), 8)
    return {
        "states": centred(seeds[0], (TSTEPS, STATES, PARTICLES), 1.0, 6.0, ((0, 64),), jnp.float32),
        "ancestors": with_ends(jax.random.randint(seeds[1], (TSTEPS, PARTICLES), 0, PARTICLES), jax.random.fold_in(seeds[1], 1), 0, PARTICLES - 1).astype(jnp.int32),
        "tracer_obs": centred(seeds[2], (TSTEPS, TRACERS), 1.0, 6.0, ((0, 64),), jnp.float32),
        "jitter": jnp.clip(jnp.exp(math.log(0.0390625) - 2.3025851 * jax.random.uniform(seeds[3], (TSTEPS,), jnp.float32) ** block_scale(seeds[3], (TSTEPS,), ((0, 64),), -0.2, 0.2)), 0.00390625, 0.0390625),
        "fingerprints": centred(seeds[4], (STATES, TRACERS), STATES ** -0.5, 0.75, (), jnp.float32),
        "tracer_scale": jnp.clip(jnp.exp(jax.random.uniform(seeds[5], (TRACERS,), jnp.float32, math.log(0.15), math.log(0.45))), 0.15, 0.45),
        "prior_weights": jnp.clip(jnp.exp(jax.random.uniform(seeds[6], (PARTICLES,), jnp.float32, math.log(0.25), math.log(4.0))), 0.25, 4.0),
    }


def transition(previous, current, parent_ids, observed, mixing, fingerprints, tracer_scale):
    count = current.shape[1]
    highest = lax.Precision.HIGHEST
    inner_prod = lax.dot_general(previous, current, (((0,), (0,)), ((), ())), precision=highest, preferred_element_type=jnp.float32)
    distance = jnp.sum(previous * previous, axis=0)[:, None] + jnp.sum(current * current, axis=0)[None, :] - 2.0 * inner_prod
    kernel = jnp.exp(-2.0 * distance / current.shape[0])
    predicted = lax.dot_general(fingerprints, current, (((0,), (0,)), ((), ())), precision=highest, preferred_element_type=jnp.float32)
    misfit = tracer_scale[:, None] * (observed[:, None] - predicted)
    likelihood = jnp.exp(-0.5 * jnp.sum(misfit * misfit, axis=0))
    parent = (parent_ids[None, :] == jnp.arange(count, dtype=jnp.int32)[:, None]).astype(jnp.float32)
    weight = likelihood[None, :] * (parent + mixing * kernel)
    return weight * (count / jnp.sum(weight))


def reference(states, ancestors, tracer_obs, jitter, fingerprints, tracer_scale, prior_weights):
    count = states.shape[2]
    start = prior_weights / jnp.sum(prior_weights)

    def advance(carry, inputs):
        weights_now, previous = carry
        current, parent_ids, observed, mixing = inputs
        matrix = transition(previous, current, parent_ids, observed, mixing, fingerprints, tracer_scale)
        moved = jnp.dot(weights_now, matrix, precision=lax.Precision.HIGHEST, preferred_element_type=jnp.float32)
        moved = moved / jnp.sum(moved)
        return (moved, current), count * moved

    initial = (start, jnp.zeros_like(states[0]))
    unused, filtered = lax.scan(advance, initial, (states, ancestors, tracer_obs, jitter))
    return filtered
```

```python
import functools

import jax
import jax.numpy as jnp
from jax import lax
from jax.experimental import pallas as pl
from jax.experimental.pallas import tpu as pltpu
from jax.sharding import PartitionSpec as P

MESH = pl.DeviceIdType.MESH


def shifted(block, axis, distance):
    devices = range(lax.axis_size(axis))
    route = [(i - distance, i) for i in devices if i - distance in devices]
    return lax.ppermute(block, axis, route)


def transition(previous, current, parent_ids, observed, mixing, fingerprints, tracer_scale):
    count = current.shape[1]
    highest = lax.Precision.HIGHEST
    inner_prod = lax.dot_general(
        previous,
        current,
        (((0,), (0,)), ((), ())),
        precision=highest,
        preferred_element_type=jnp.float32,
    )
    distance = (
        jnp.sum(previous * previous, axis=0)[:, None]
        + jnp.sum(current * current, axis=0)[None, :]
        - 2.0 * inner_prod
    )
    kernel = jnp.exp(-2.0 * distance / current.shape[0])
    predicted = lax.dot_general(
        fingerprints,
        current,
        (((0,), (0,)), ((), ())),
        precision=highest,
        preferred_element_type=jnp.float32,
    )
    misfit = tracer_scale[:, None] * (observed[:, None] - predicted)
    likelihood = jnp.exp(-0.5 * jnp.sum(misfit * misfit, axis=0))
    parent = (parent_ids[None, :] == jnp.arange(count, dtype=jnp.int32)[:, None]).astype(
        jnp.float32
    )
    weight = likelihood[None, :] * (parent + mixing * kernel)
    return weight * (count / jnp.sum(weight))


def vec_mat(u_row, mat):
    n = mat.shape[0]
    u_col = jnp.transpose(jnp.broadcast_to(u_row[0:1, :], (128, n)))
    parts = []
    for g in range(n // 128):
        block = mat[:, g * 128:(g + 1) * 128]
        parts.append(jnp.sum(block * u_col, axis=0, keepdims=True))
    return jnp.concatenate(parts, axis=1)


def chain_kernel(steps, b_ref, start_ref, out_ref, recv_buf, send_buf, send_sem, recv_sem):
    me = lax.axis_index("tm")
    row = lax.axis_index("rows")
    last = steps - 1

    barrier = pltpu.get_barrier_semaphore()

    @pl.when(me > 0)
    def _():
        pl.semaphore_signal(barrier, 1, device_id=(me - 1, row), device_id_type=MESH)

    @pl.when(me < last)
    def _():
        pl.semaphore_signal(barrier, 1, device_id=(me + 1, row), device_id_type=MESH)

    @pl.when(jnp.logical_or(me == 0, me == last))
    def _():
        pl.semaphore_wait(barrier, 1)

    @pl.when(jnp.logical_and(me > 0, me < last))
    def _():
        pl.semaphore_wait(barrier, 2)

    copy = pltpu.make_async_remote_copy(
        src_ref=send_buf,
        dst_ref=recv_buf,
        send_sem=send_sem,
        recv_sem=recv_sem,
        device_id=(jnp.minimum(me + 1, last), row),
        device_id_type=MESH,
    )

    @pl.when(me == 0)
    def _():
        out_ref[...] = start_ref[...]

    @pl.when(me > 0)
    def _():
        copy.wait_recv()
        out_ref[...] = recv_buf[...]

    @pl.when(me < last)
    def _():
        v = vec_mat(out_ref[...], b_ref[...])
        v = v / jnp.sum(v)
        send_buf[...] = jnp.broadcast_to(v, send_buf.shape)
        copy.start()
        copy.wait_send()


def chain(block, start, steps):
    count = block.shape[0]
    return pl.pallas_call(
        functools.partial(chain_kernel, steps),
        out_shape=jax.ShapeDtypeStruct((8, count), jnp.float32),
        in_specs=[pl.BlockSpec(memory_space=pltpu.VMEM)] * 2,
        out_specs=pl.BlockSpec(memory_space=pltpu.VMEM),
        scratch_shapes=[
            pltpu.VMEM((8, count), jnp.float32),
            pltpu.VMEM((8, count), jnp.float32),
            pltpu.SemaphoreType.DMA,
            pltpu.SemaphoreType.DMA,
        ],
        compiler_params=pltpu.CompilerParams(collective_id=0, has_side_effects=True),
    )(block, start)


def shards(states, ancestors, tracer_obs, jitter, fingerprints, tracer_scale, prior_weights):
    highest = lax.Precision.HIGHEST
    count = states.shape[2]
    own_rows = count // lax.axis_size("rows")
    row_start = lax.axis_index("rows") * own_rows
    steps = lax.axis_size("tm")
    rim = shifted(states[-1], "tm", 1)

    previous = jnp.concatenate([rim[None], states[:-1]], axis=0)
    matrices = [
        transition(
            previous[s], states[s], ancestors[s], tracer_obs[s], jitter[s], fingerprints, tracer_scale
        )
        for s in range(states.shape[0])
    ]
    block = matrices[0]
    for matrix in matrices[1:]:
        block = jnp.dot(block, matrix, precision=highest, preferred_element_type=jnp.float32)

    start = prior_weights / jnp.sum(prior_weights)
    start8 = jnp.broadcast_to(start[None, :], (8, count))
    incoming = chain(block, start8, steps)[0]

    weights_now = incoming
    rows_out = []
    for matrix in matrices:
        moved = jnp.dot(weights_now, matrix, precision=highest, preferred_element_type=jnp.float32)
        moved = moved / jnp.sum(moved)
        weights_now = moved
        rows_out.append(count * lax.dynamic_slice_in_dim(moved, row_start, own_rows, 0))
    return jnp.stack(rows_out, axis=0)


def solution(mesh):
    return jax.shard_map(
        shards,
        mesh=mesh,
        in_specs=(P("tm", None, None), P("tm", None), P("tm", None), P("tm"), P(), P(), P()),
        out_specs=P("tm", "rows"),
        check_vma=False,
    )
```

```python
import functools

import jax
import jax.numpy as jnp
from jax import lax
from jax.experimental import pallas as pl
from jax.experimental.pallas import tpu as pltpu
from jax.sharding import PartitionSpec as P

MESH = pl.DeviceIdType.MESH


def shifted(block, axis, distance):
    devices = range(lax.axis_size(axis))
    route = [(i - distance, i) for i in devices if i - distance in devices]
    return lax.ppermute(block, axis, route)


def transition(previous, current, parent_ids, observed, mixing, fingerprints, tracer_scale):
    count = current.shape[1]
    highest = lax.Precision.HIGHEST
    inner_prod = lax.dot_general(
        previous,
        current,
        (((0,), (0,)), ((), ())),
        precision=highest,
        preferred_element_type=jnp.float32,
    )
    distance = (
        jnp.sum(previous * previous, axis=0)[:, None]
        + jnp.sum(current * current, axis=0)[None, :]
        - 2.0 * inner_prod
    )
    kernel = jnp.exp(-2.0 * distance / current.shape[0])
    predicted = lax.dot_general(
        fingerprints,
        current,
        (((0,), (0,)), ((), ())),
        precision=highest,
        preferred_element_type=jnp.float32,
    )
    misfit = tracer_scale[:, None] * (observed[:, None] - predicted)
    likelihood = jnp.exp(-0.5 * jnp.sum(misfit * misfit, axis=0))
    parent = (parent_ids[None, :] == jnp.arange(count, dtype=jnp.int32)[:, None]).astype(
        jnp.float32
    )
    weight = likelihood[None, :] * (parent + mixing * kernel)
    return weight * (count / jnp.sum(weight))


def vec_mat(u_row, mat):
    n = mat.shape[0]
    u_col = jnp.transpose(jnp.broadcast_to(u_row[0:1, :], (128, n)))
    parts = []
    for g in range(n // 128):
        block = mat[:, g * 128:(g + 1) * 128]
        parts.append(jnp.sum(block * u_col, axis=0, keepdims=True))
    return jnp.concatenate(parts, axis=1)


def normalized(v):
    return v / jnp.sum(v)


def chain_kernel(
    steps, before_ref, block_ref, first_ref, second_ref, start_ref,
    out_ref, recv_buf, send_buf, send_sem, recv_sem,
):
    me = lax.axis_index("tm")
    row = lax.axis_index("rows")
    last = steps - 1
    even = me % 2 == 0

    barrier = pltpu.get_barrier_semaphore()

    def greet(other):
        pl.semaphore_signal(barrier, 1, device_id=(other, row), device_id_type=MESH)

    @pl.when(even)
    def _():
        greet(me + 1)

        @pl.when(me + 2 <= last)
        def _():
            greet(me + 2)

        @pl.when(me >= 2)
        def _():
            greet(me - 2)

    @pl.when(jnp.logical_not(even))
    def _():
        greet(me - 1)

    partners = jnp.where(
        even, 1 + (me + 2 <= last).astype(jnp.int32) + (me >= 2).astype(jnp.int32), 1
    )

    @pl.when(partners == 1)
    def _():
        pl.semaphore_wait(barrier, 1)

    @pl.when(partners == 2)
    def _():
        pl.semaphore_wait(barrier, 2)

    @pl.when(partners == 3)
    def _():
        pl.semaphore_wait(barrier, 3)

    def copy_to(other, slot):
        return pltpu.make_async_remote_copy(
            src_ref=send_buf,
            dst_ref=recv_buf,
            send_sem=send_sem.at[slot],
            recv_sem=recv_sem,
            device_id=(other, row),
            device_id_type=MESH,
        )

    near = copy_to(jnp.minimum(me + 1, last), 0)
    far = copy_to(jnp.minimum(me + 2, last), 1)

    @pl.when(me == 0)
    def _():
        out_ref[...] = start_ref[...]

    @pl.when(jnp.logical_and(even, me > 0))
    def _():
        near.wait_recv()
        u = normalized(vec_mat(recv_buf[...], before_ref[...]))
        out_ref[...] = jnp.broadcast_to(u, out_ref.shape)

    @pl.when(jnp.logical_not(even))
    def _():
        near.wait_recv()
        out_ref[...] = recv_buf[...]

    @pl.when(even)
    def _():
        v = normalized(vec_mat(out_ref[...], block_ref[...]))
        send_buf[...] = jnp.broadcast_to(v, send_buf.shape)
        near.start()

        @pl.when(me + 2 <= last)
        def _():
            far.start()

    incoming = out_ref[...]
    w_first = normalized(vec_mat(incoming, first_ref[...]))
    w_second = normalized(vec_mat(jnp.broadcast_to(w_first, incoming.shape), second_ref[...]))
    out_ref[...] = jnp.concatenate(
        [w_first, w_second, jnp.zeros((incoming.shape[0] - 2, incoming.shape[1]), jnp.float32)],
        axis=0,
    )

    @pl.when(even)
    def _():
        near.wait_send()

        @pl.when(me + 2 <= last)
        def _():
            far.wait_send()


def chain(before, block, first, second, start, steps):
    count = block.shape[0]
    return pl.pallas_call(
        functools.partial(chain_kernel, steps),
        out_shape=jax.ShapeDtypeStruct((8, count), jnp.float32),
        in_specs=[pl.BlockSpec(memory_space=pltpu.VMEM)] * 5,
        out_specs=pl.BlockSpec(memory_space=pltpu.VMEM),
        scratch_shapes=[
            pltpu.VMEM((8, count), jnp.float32),
            pltpu.VMEM((8, count), jnp.float32),
            pltpu.SemaphoreType.DMA((2,)),
            pltpu.SemaphoreType.DMA,
        ],
        compiler_params=pltpu.CompilerParams(collective_id=0, has_side_effects=True),
    )(before, block, first, second, start)


def block_product(matrices):
    block = matrices[0]
    for matrix in matrices[1:]:
        block = jnp.dot(
            block, matrix, precision=lax.Precision.HIGHEST, preferred_element_type=jnp.float32
        )
    return block


def shards(states, ancestors, tracer_obs, jitter, fingerprints, tracer_scale, prior_weights):
    count = states.shape[2]
    own_rows = count // lax.axis_size("rows")
    row_start = lax.axis_index("rows") * own_rows
    steps = lax.axis_size("tm")
    local = states.shape[0]

    states_before = shifted(states, "tm", 1)
    ancestors_before = shifted(ancestors, "tm", 1)
    obs_before = shifted(tracer_obs, "tm", 1)
    jitter_before = shifted(jitter, "tm", 1)
    rim_before = shifted(states[-1], "tm", 2)

    def matrices_of(rim, block_states, parents, observed, mixing):
        previous = jnp.concatenate([rim[None], block_states[:-1]], axis=0)
        return [
            transition(
                previous[s], block_states[s], parents[s], observed[s], mixing[s],
                fingerprints, tracer_scale,
            )
            for s in range(local)
        ]

    own = matrices_of(states_before[-1], states, ancestors, tracer_obs, jitter)
    before = matrices_of(rim_before, states_before, ancestors_before, obs_before, jitter_before)

    start = prior_weights / jnp.sum(prior_weights)
    start8 = jnp.broadcast_to(start[None, :], (8, count))
    weights = chain(block_product(before), block_product(own), own[0], own[1], start8, steps)
    mine = lax.dynamic_slice_in_dim(weights[:local], row_start, own_rows, 1)
    return count * mine


def solution(mesh):
    return jax.shard_map(
        shards,
        mesh=mesh,
        in_specs=(P("tm", None, None), P("tm", None), P("tm", None), P("tm"), P(), P(), P()),
        out_specs=P("tm", "rows"),
        check_vma=False,
    )
```

```python
import functools

import jax
import jax.numpy as jnp
from jax import lax
from jax.experimental import pallas as pl
from jax.experimental.pallas import tpu as pltpu
from jax.sharding import PartitionSpec as P

MESH = pl.DeviceIdType.MESH


def shifted(block, axis, distance):
    devices = range(lax.axis_size(axis))
    route = [(i - distance, i) for i in devices if i - distance in devices]
    return lax.ppermute(block, axis, route)


def transition(previous, current, parent_ids, observed, mixing, fingerprints, tracer_scale):
    count = current.shape[1]
    highest = lax.Precision.HIGHEST
    inner_prod = lax.dot_general(
        previous,
        current,
        (((0,), (0,)), ((), ())),
        precision=highest,
        preferred_element_type=jnp.float32,
    )
    distance = (
        jnp.sum(previous * previous, axis=0)[:, None]
        + jnp.sum(current * current, axis=0)[None, :]
        - 2.0 * inner_prod
    )
    kernel = jnp.exp(-2.0 * distance / current.shape[0])
    predicted = lax.dot_general(
        fingerprints,
        current,
        (((0,), (0,)), ((), ())),
        precision=highest,
        preferred_element_type=jnp.float32,
    )
    misfit = tracer_scale[:, None] * (observed[:, None] - predicted)
    likelihood = jnp.exp(-0.5 * jnp.sum(misfit * misfit, axis=0))
    parent = (parent_ids[None, :] == jnp.arange(count, dtype=jnp.int32)[:, None]).astype(
        jnp.float32
    )
    weight = likelihood[None, :] * (parent + mixing * kernel)
    return weight * (count / jnp.sum(weight))


def vec_mat(u_row, mat):
    n = mat.shape[0]
    u_col = jnp.transpose(jnp.broadcast_to(u_row[0:1, :], (128, n)))
    parts = []
    for g in range(n // 128):
        block = mat[:, g * 128:(g + 1) * 128]
        parts.append(jnp.sum(block * u_col, axis=0, keepdims=True))
    return jnp.concatenate(parts, axis=1)


def normalized(v):
    return v / jnp.sum(v)


def chain_kernel(
    steps, before_ref, block_ref, combined_ref, first_ref, second_ref, start_ref,
    out_ref, recv_buf, send_buf, send_sem, recv_sem,
):
    me = lax.axis_index("tm")
    row = lax.axis_index("rows")
    last = steps - 1
    even = me % 2 == 0

    barrier = pltpu.get_barrier_semaphore()

    def greet(other):
        pl.semaphore_signal(barrier, 1, device_id=(other, row), device_id_type=MESH)

    @pl.when(even)
    def _():
        greet(me + 1)

        @pl.when(me + 2 <= last)
        def _():
            greet(me + 2)

        @pl.when(me >= 2)
        def _():
            greet(me - 2)

    @pl.when(jnp.logical_not(even))
    def _():
        greet(me - 1)

    partners = jnp.where(
        even, 1 + (me + 2 <= last).astype(jnp.int32) + (me >= 2).astype(jnp.int32), 1
    )

    @pl.when(partners == 1)
    def _():
        pl.semaphore_wait(barrier, 1)

    @pl.when(partners == 2)
    def _():
        pl.semaphore_wait(barrier, 2)

    @pl.when(partners == 3)
    def _():
        pl.semaphore_wait(barrier, 3)

    def copy_to(other, slot):
        return pltpu.make_async_remote_copy(
            src_ref=send_buf,
            dst_ref=recv_buf,
            send_sem=send_sem.at[slot],
            recv_sem=recv_sem,
            device_id=(other, row),
            device_id_type=MESH,
        )

    near = copy_to(jnp.minimum(me + 1, last), 0)
    far = copy_to(jnp.minimum(me + 2, last), 1)

    @pl.when(me == 0)
    def _():
        out_ref[...] = start_ref[...]
        v = normalized(vec_mat(start_ref[...], block_ref[...]))
        send_buf[...] = jnp.broadcast_to(v, send_buf.shape)
        near.start()
        far.start()

    @pl.when(jnp.logical_and(even, me > 0))
    def _():
        near.wait_recv()
        received = recv_buf[...]
        v = normalized(vec_mat(received, combined_ref[...]))
        send_buf[...] = jnp.broadcast_to(v, send_buf.shape)
        near.start()

        @pl.when(me + 2 <= last)
        def _():
            far.start()

        u = normalized(vec_mat(received, before_ref[...]))
        out_ref[...] = jnp.broadcast_to(u, out_ref.shape)

    @pl.when(jnp.logical_not(even))
    def _():
        near.wait_recv()
        out_ref[...] = recv_buf[...]

    incoming = out_ref[...]
    w_first = normalized(vec_mat(incoming, first_ref[...]))
    w_second = normalized(vec_mat(jnp.broadcast_to(w_first, incoming.shape), second_ref[...]))
    out_ref[...] = jnp.concatenate(
        [w_first, w_second, jnp.zeros((incoming.shape[0] - 2, incoming.shape[1]), jnp.float32)],
        axis=0,
    )

    @pl.when(even)
    def _():
        near.wait_send()

        @pl.when(me + 2 <= last)
        def _():
            far.wait_send()


def chain(before, block, combined, first, second, start, steps):
    count = block.shape[0]
    return pl.pallas_call(
        functools.partial(chain_kernel, steps),
        out_shape=jax.ShapeDtypeStruct((8, count), jnp.float32),
        in_specs=[pl.BlockSpec(memory_space=pltpu.VMEM)] * 6,
        out_specs=pl.BlockSpec(memory_space=pltpu.VMEM),
        scratch_shapes=[
            pltpu.VMEM((8, count), jnp.float32),
            pltpu.VMEM((8, count), jnp.float32),
            pltpu.SemaphoreType.DMA((2,)),
            pltpu.SemaphoreType.DMA,
        ],
        compiler_params=pltpu.CompilerParams(collective_id=0, has_side_effects=True),
    )(before, block, combined, first, second, start)


def block_product(matrices):
    block = matrices[0]
    for matrix in matrices[1:]:
        block = jnp.dot(
            block, matrix, precision=lax.Precision.HIGH, preferred_element_type=jnp.float32
        )
    return block


def shards(states, ancestors, tracer_obs, jitter, fingerprints, tracer_scale, prior_weights):
    count = states.shape[2]
    own_rows = count // lax.axis_size("rows")
    row_start = lax.axis_index("rows") * own_rows
    steps = lax.axis_size("tm")
    local = states.shape[0]

    count_pad = jnp.zeros((local, count - tracer_obs.shape[1] - 1), jnp.float32)
    extra = jnp.concatenate(
        [
            ancestors.astype(jnp.float32)[:, None, :],
            jnp.concatenate([tracer_obs, jitter[:, None], count_pad], axis=1)[:, None, :],
        ],
        axis=1,
    )
    packed_before = shifted(jnp.concatenate([states, extra], axis=1), "tm", 1)
    dims = states.shape[1]
    states_before = packed_before[:, :dims, :]
    ancestors_before = packed_before[:, dims, :].astype(jnp.int32)
    obs_before = packed_before[:, dims + 1, : tracer_obs.shape[1]]
    jitter_before = packed_before[:, dims + 1, tracer_obs.shape[1]]
    rim_before = shifted(states[-1], "tm", 2)

    def matrices_of(rim, block_states, parents, observed, mixing):
        previous = jnp.concatenate([rim[None], block_states[:-1]], axis=0)
        return [
            transition(
                previous[s], block_states[s], parents[s], observed[s], mixing[s],
                fingerprints, tracer_scale,
            )
            for s in range(local)
        ]

    own = matrices_of(states_before[-1], states, ancestors, tracer_obs, jitter)
    before = matrices_of(rim_before, states_before, ancestors_before, obs_before, jitter_before)

    start = prior_weights / jnp.sum(prior_weights)
    start8 = jnp.broadcast_to(start[None, :], (8, count))
    block_before = block_product(before)
    block_own = block_product(own)
    combined = block_product([block_before, block_own])
    weights = chain(block_before, block_own, combined, own[0], own[1], start8, steps)
    mine = lax.dynamic_slice_in_dim(weights[:local], row_start, own_rows, 1)
    return count * mine


def solution(mesh):
    return jax.shard_map(
        shards,
        mesh=mesh,
        in_specs=(P("tm", None, None), P("tm", None), P("tm", None), P("tm"), P(), P(), P()),
        out_specs=P("tm", "rows"),
        check_vma=False,
    )
```

```python
import functools

import jax
import jax.numpy as jnp
from jax import lax
from jax.experimental import pallas as pl
from jax.experimental.pallas import tpu as pltpu
from jax.sharding import PartitionSpec as P

MESH = pl.DeviceIdType.MESH
STRIDE = 3


def shifted(block, axis, distance):
    devices = range(lax.axis_size(axis))
    route = [(i - distance, i) for i in devices if i - distance in devices]
    return lax.ppermute(block, axis, route)


def transition(previous, current, parent_ids, observed, mixing, fingerprints, tracer_scale):
    count = current.shape[1]
    highest = lax.Precision.HIGHEST
    inner_prod = lax.dot_general(
        previous,
        current,
        (((0,), (0,)), ((), ())),
        precision=highest,
        preferred_element_type=jnp.float32,
    )
    distance = (
        jnp.sum(previous * previous, axis=0)[:, None]
        + jnp.sum(current * current, axis=0)[None, :]
        - 2.0 * inner_prod
    )
    kernel = jnp.exp(-2.0 * distance / current.shape[0])
    predicted = lax.dot_general(
        fingerprints,
        current,
        (((0,), (0,)), ((), ())),
        precision=highest,
        preferred_element_type=jnp.float32,
    )
    misfit = tracer_scale[:, None] * (observed[:, None] - predicted)
    likelihood = jnp.exp(-0.5 * jnp.sum(misfit * misfit, axis=0))
    likelihood = likelihood / jnp.max(likelihood)
    parent = (parent_ids[None, :] == jnp.arange(count, dtype=jnp.int32)[:, None]).astype(
        jnp.float32
    )
    return likelihood[None, :] * (parent + mixing * kernel)


def vec_mat(u_row, mat):
    n = mat.shape[0]
    u_col = jnp.transpose(jnp.broadcast_to(u_row[0:1, :], (128, n)))
    parts = []
    for g in range(n // 128):
        block = mat[:, g * 128:(g + 1) * 128]
        parts.append(jnp.sum(block * u_col, axis=0, keepdims=True))
    return jnp.concatenate(parts, axis=1)


def normalized(v):
    return v / jnp.sum(v)


def spread(v, like):
    return jnp.broadcast_to(v, like.shape)


def chain_kernel(
    steps, stride, before_ref, block_ref, combined_ref, first_ref, second_ref, start_ref,
    out_ref, recv_buf, send_buf, send_sem, recv_sem,
):
    me = lax.axis_index("tm")
    row = lax.axis_index("rows")
    last = steps - 1
    phase = me % stride
    node = phase == 0

    barrier = pltpu.get_barrier_semaphore()

    def greet(other):
        pl.semaphore_signal(barrier, 1, device_id=(other, row), device_id_type=MESH)

    @pl.when(node)
    def _():
        for d in range(1, stride + 1):
            @pl.when(me + d <= last)
            def _():
                greet(me + d)

        @pl.when(me >= stride)
        def _():
            greet(me - stride)

    @pl.when(jnp.logical_not(node))
    def _():
        greet(me - phase)

    partners = jnp.where(
        node,
        jnp.minimum(last - me, stride) + (me >= stride).astype(jnp.int32),
        1,
    )
    for amount in range(1, stride + 2):
        @pl.when(partners == amount)
        def _():
            pl.semaphore_wait(barrier, amount)

    def copy_to(d):
        return pltpu.make_async_remote_copy(
            src_ref=send_buf,
            dst_ref=recv_buf,
            send_sem=send_sem.at[d - 1],
            recv_sem=recv_sem,
            device_id=(jnp.minimum(me + d, last), row),
            device_id_type=MESH,
        )

    copies = [copy_to(d) for d in range(1, stride + 1)]

    def send_all(v):
        send_buf[...] = spread(v, send_buf)
        for d in range(1, stride + 1):
            @pl.when(me + d <= last)
            def _():
                copies[d - 1].start()

    @pl.when(me == 0)
    def _():
        out_ref[...] = start_ref[...]
        send_all(normalized(vec_mat(start_ref[...], block_ref[...])))

    @pl.when(me > 0)
    def _():
        copies[0].wait_recv()
        out_ref[...] = recv_buf[...]

    @pl.when(jnp.logical_and(node, me > 0))
    def _():
        send_all(normalized(vec_mat(out_ref[...], combined_ref[...])))

    lag = jnp.where(node, jnp.where(me > 0, stride - 1, 0), phase - 1)
    for amount in range(1, stride):
        @pl.when(lag == amount)
        def _():
            u = out_ref[...]
            for d in range(amount, 0, -1):
                u = spread(normalized(vec_mat(u, before_ref[d - 1])), out_ref)
            out_ref[...] = u

    incoming = out_ref[...]
    w_first = normalized(vec_mat(incoming, first_ref[...]))
    w_second = normalized(vec_mat(spread(w_first, incoming), second_ref[...]))
    out_ref[...] = jnp.concatenate(
        [w_first, w_second, jnp.zeros((incoming.shape[0] - 2, incoming.shape[1]), jnp.float32)],
        axis=0,
    )

    @pl.when(node)
    def _():
        for d in range(1, stride + 1):
            @pl.when(me + d <= last)
            def _():
                copies[d - 1].wait_send()


def chain(befores, block, combined, first, second, start, steps, stride):
    count = block.shape[0]
    return pl.pallas_call(
        functools.partial(chain_kernel, steps, stride),
        out_shape=jax.ShapeDtypeStruct((8, count), jnp.float32),
        in_specs=[pl.BlockSpec(memory_space=pltpu.VMEM)] * 6,
        out_specs=pl.BlockSpec(memory_space=pltpu.VMEM),
        scratch_shapes=[
            pltpu.VMEM((8, count), jnp.float32),
            pltpu.VMEM((8, count), jnp.float32),
            pltpu.SemaphoreType.DMA((stride,)),
            pltpu.SemaphoreType.DMA,
        ],
        compiler_params=pltpu.CompilerParams(
            collective_id=0, has_side_effects=True, vmem_limit_bytes=48 * 1024 * 1024
        ),
    )(befores, block, combined, first, second, start)


def block_product(matrices):
    block = matrices[0]
    for matrix in matrices[1:]:
        block = jnp.dot(
            block, matrix, precision=lax.Precision.HIGH, preferred_element_type=jnp.float32
        )
    return block


def shards(states, ancestors, tracer_obs, jitter, fingerprints, tracer_scale, prior_weights):
    count = states.shape[2]
    own_rows = count // lax.axis_size("rows")
    row_start = lax.axis_index("rows") * own_rows
    steps = lax.axis_size("tm")
    stride = STRIDE
    local = states.shape[0]
    dims = states.shape[1]
    tracers = tracer_obs.shape[1]

    count_pad = jnp.zeros((local, count - tracers - 1), jnp.float32)
    extra = jnp.concatenate(
        [
            ancestors.astype(jnp.float32)[:, None, :],
            jnp.concatenate([tracer_obs, jitter[:, None], count_pad], axis=1)[:, None, :],
        ],
        axis=1,
    )
    packed = jnp.concatenate([states, extra], axis=1)
    packs = [packed] + [shifted(packed, "tm", d) for d in range(1, stride)]
    rims = [pack[-1, :dims, :] for pack in packs[1:]] + [shifted(states[-1], "tm", stride)]

    def matrices_of(rim, pack):
        block_states = pack[:, :dims, :]
        parents = pack[:, dims, :].astype(jnp.int32)
        observed = pack[:, dims + 1, :tracers]
        mixing = pack[:, dims + 1, tracers]
        previous = jnp.concatenate([rim[None], block_states[:-1]], axis=0)
        return [
            transition(
                previous[s], block_states[s], parents[s], observed[s], mixing[s],
                fingerprints, tracer_scale,
            )
            for s in range(local)
        ]

    own = matrices_of(rims[0], packs[0])
    blocks = [block_product(own)] + [
        block_product(matrices_of(rims[d], packs[d])) for d in range(1, stride)
    ]
    combined = block_product(blocks[::-1])
    befores = jnp.stack(blocks[1:], axis=0)

    start = prior_weights / jnp.sum(prior_weights)
    start8 = jnp.broadcast_to(start[None, :], (8, count))
    weights = chain(befores, blocks[0], combined, own[0], own[1], start8, steps, stride)
    mine = lax.dynamic_slice_in_dim(weights[:local], row_start, own_rows, 1)
    return count * mine


def solution(mesh):
    return jax.shard_map(
        shards,
        mesh=mesh,
        in_specs=(P("tm", None, None), P("tm", None), P("tm", None), P("tm"), P(), P(), P()),
        out_specs=P("tm", "rows"),
        check_vma=False,
    )
```

```python
import functools

import jax
import jax.numpy as jnp
from jax import lax
from jax.experimental import pallas as pl
from jax.experimental.pallas import tpu as pltpu
from jax.sharding import PartitionSpec as P

MESH = pl.DeviceIdType.MESH
STRIDE = 3


def shifted(block, axis, distance):
    devices = range(lax.axis_size(axis))
    route = [(i - distance, i) for i in devices if i - distance in devices]
    return lax.ppermute(block, axis, route)


def transition(previous, current, parent_ids, observed, mixing, fingerprints, tracer_scale):
    count = current.shape[1]
    highest = lax.Precision.HIGHEST
    inner_prod = lax.dot_general(
        previous,
        current,
        (((0,), (0,)), ((), ())),
        precision=highest,
        preferred_element_type=jnp.float32,
    )
    distance = (
        jnp.sum(previous * previous, axis=0)[:, None]
        + jnp.sum(current * current, axis=0)[None, :]
        - 2.0 * inner_prod
    )
    kernel = jnp.exp(-2.0 * distance / current.shape[0])
    predicted = lax.dot_general(
        fingerprints,
        current,
        (((0,), (0,)), ((), ())),
        precision=highest,
        preferred_element_type=jnp.float32,
    )
    misfit = tracer_scale[:, None] * (observed[:, None] - predicted)
    likelihood = jnp.exp(-0.5 * jnp.sum(misfit * misfit, axis=0))
    likelihood = likelihood / jnp.max(likelihood)
    parent = (parent_ids[None, :] == jnp.arange(count, dtype=jnp.int32)[:, None]).astype(
        jnp.float32
    )
    return likelihood[None, :] * (parent + mixing * kernel)


def vec_mat(u_row, mat):
    n = mat.shape[0]
    u_col = jnp.transpose(jnp.broadcast_to(u_row[0:1, :], (128, n)))
    parts = []
    for g in range(n // 128):
        block = mat[:, g * 128:(g + 1) * 128]
        parts.append(jnp.sum(block * u_col, axis=0, keepdims=True))
    return jnp.concatenate(parts, axis=1)


def normalized(v):
    return v / jnp.sum(v)


def spread(v, like):
    return jnp.broadcast_to(v, like.shape)


def chain_kernel(
    steps, stride, *refs,
):
    n_in = stride + 4
    hbm = refs[:n_in - 1]
    start_ref = refs[n_in - 1]
    out_ref, recv_buf, send_buf, send_sem, recv_sem, load_sem = refs[n_in:n_in + 6]
    local = refs[n_in + 6:]
    me = lax.axis_index("tm")
    row = lax.axis_index("rows")
    last = steps - 1
    phase = me % stride
    node = phase == 0

    loads = [
        pltpu.make_async_copy(hbm[i], local[i], load_sem.at[i]) for i in range(len(hbm))
    ]
    for load in loads:
        load.start()
    block_ref, combined_ref, first_ref, second_ref = local[:4]
    befores = local[4:]

    barrier = pltpu.get_barrier_semaphore()

    def greet(other):
        pl.semaphore_signal(barrier, 1, device_id=(other, row), device_id_type=MESH)

    @pl.when(node)
    def _():
        for d in range(1, stride + 1):
            @pl.when(me + d <= last)
            def _():
                greet(me + d)

        @pl.when(me >= stride)
        def _():
            greet(me - stride)

    @pl.when(jnp.logical_not(node))
    def _():
        greet(me - phase)

    partners = jnp.where(
        node,
        jnp.minimum(last - me, stride) + (me >= stride).astype(jnp.int32),
        1,
    )
    for amount in range(1, stride + 2):
        @pl.when(partners == amount)
        def _():
            pl.semaphore_wait(barrier, amount)

    def copy_to(d):
        return pltpu.make_async_remote_copy(
            src_ref=send_buf,
            dst_ref=recv_buf,
            send_sem=send_sem.at[d - 1],
            recv_sem=recv_sem,
            device_id=(jnp.minimum(me + d, last), row),
            device_id_type=MESH,
        )

    copies = [copy_to(d) for d in range(1, stride + 1)]

    def send_all(v):
        send_buf[...] = v
        for d in range(1, stride + 1):
            @pl.when(me + d <= last)
            def _():
                copies[d - 1].start()

    loads[0].wait()
    loads[1].wait()

    @pl.when(me == 0)
    def _():
        out_ref[...] = start_ref[...]
        send_all(normalized(vec_mat(start_ref[...], block_ref[...])))

    @pl.when(me > 0)
    def _():
        copies[0].wait_recv()
        out_ref[...] = spread(recv_buf[...], out_ref)

    @pl.when(jnp.logical_and(node, me > 0))
    def _():
        send_all(normalized(vec_mat(out_ref[...], combined_ref[...])))

    for load in loads[4:]:
        load.wait()
    lag = jnp.where(node, jnp.where(me > 0, stride - 1, 0), phase - 1)
    for amount in range(1, stride):
        @pl.when(lag == amount)
        def _():
            u = out_ref[...]
            for d in range(amount, 0, -1):
                u = spread(normalized(vec_mat(u, befores[d - 1][...])), out_ref)
            out_ref[...] = u

    loads[2].wait()
    loads[3].wait()
    incoming = out_ref[...]
    w_first = normalized(vec_mat(incoming, first_ref[...]))
    w_second = normalized(vec_mat(spread(w_first, incoming), second_ref[...]))
    out_ref[...] = jnp.concatenate(
        [w_first, w_second, jnp.zeros((incoming.shape[0] - 2, incoming.shape[1]), jnp.float32)],
        axis=0,
    )

    @pl.when(node)
    def _():
        for d in range(1, stride + 1):
            @pl.when(me + d <= last)
            def _():
                copies[d - 1].wait_send()


def chain(block, combined, first, second, befores, start, steps, stride):
    count = block.shape[0]
    matrices = [block, combined, first, second] + list(befores)
    return pl.pallas_call(
        functools.partial(chain_kernel, steps, stride),
        out_shape=jax.ShapeDtypeStruct((8, count), jnp.float32),
        in_specs=[pl.BlockSpec(memory_space=pl.ANY)] * len(matrices)
        + [pl.BlockSpec(memory_space=pltpu.VMEM)],
        out_specs=pl.BlockSpec(memory_space=pltpu.VMEM),
        scratch_shapes=[
            pltpu.VMEM((1, count), jnp.float32),
            pltpu.VMEM((1, count), jnp.float32),
            pltpu.SemaphoreType.DMA((stride,)),
            pltpu.SemaphoreType.DMA,
            pltpu.SemaphoreType.DMA((len(matrices),)),
        ]
        + [pltpu.VMEM((count, count), jnp.float32) for _ in matrices],
        compiler_params=pltpu.CompilerParams(
            collective_id=0, has_side_effects=True, vmem_limit_bytes=48 * 1024 * 1024
        ),
    )(*matrices, start)


def block_product(matrices):
    block = matrices[0]
    for matrix in matrices[1:]:
        block = jnp.dot(
            block, matrix, precision=lax.Precision.HIGH, preferred_element_type=jnp.float32
        )
    return block


def shards(states, ancestors, tracer_obs, jitter, fingerprints, tracer_scale, prior_weights):
    count = states.shape[2]
    own_rows = count // lax.axis_size("rows")
    row_start = lax.axis_index("rows") * own_rows
    steps = lax.axis_size("tm")
    stride = STRIDE
    local = states.shape[0]
    dims = states.shape[1]
    tracers = tracer_obs.shape[1]

    count_pad = jnp.zeros((local, count - tracers - 1), jnp.float32)
    extra = jnp.concatenate(
        [
            ancestors.astype(jnp.float32)[:, None, :],
            jnp.concatenate([tracer_obs, jitter[:, None], count_pad], axis=1)[:, None, :],
        ],
        axis=1,
    )
    packed = jnp.concatenate([states, extra], axis=1)
    packs = [packed] + [shifted(packed, "tm", d) for d in range(1, stride)]
    rims = [pack[-1, :dims, :] for pack in packs[1:]] + [shifted(states[-1], "tm", stride)]

    def matrices_of(rim, pack):
        block_states = pack[:, :dims, :]
        parents = pack[:, dims, :].astype(jnp.int32)
        observed = pack[:, dims + 1, :tracers]
        mixing = pack[:, dims + 1, tracers]
        previous = jnp.concatenate([rim[None], block_states[:-1]], axis=0)
        return [
            transition(
                previous[s], block_states[s], parents[s], observed[s], mixing[s],
                fingerprints, tracer_scale,
            )
            for s in range(local)
        ]

    own = matrices_of(rims[0], packs[0])
    blocks = [block_product(own)] + [
        block_product(matrices_of(rims[d], packs[d])) for d in range(1, stride)
    ]
    combined = block_product(blocks[::-1])

    start = prior_weights / jnp.sum(prior_weights)
    start8 = jnp.broadcast_to(start[None, :], (8, count))
    weights = chain(blocks[0], combined, own[0], own[1], blocks[1:], start8, steps, stride)
    mine = lax.dynamic_slice_in_dim(weights[:local], row_start, own_rows, 1)
    return count * mine


def solution(mesh):
    return jax.shard_map(
        shards,
        mesh=mesh,
        in_specs=(P("tm", None, None), P("tm", None), P("tm", None), P("tm"), P(), P(), P()),
        out_specs=P("tm", "rows"),
        check_vma=False,
    )
```

```python
import functools

import jax
import jax.numpy as jnp
from jax import lax
from jax.experimental import pallas as pl
from jax.experimental.pallas import tpu as pltpu
from jax.sharding import PartitionSpec as P

MESH = pl.DeviceIdType.MESH
STRIDE = 3


def shifted(block, axis, distance):
    devices = range(lax.axis_size(axis))
    route = [(i - distance, i) for i in devices if i - distance in devices]
    return lax.ppermute(block, axis, route)


def transition(previous, current, parent_ids, observed, mixing, fingerprints, tracer_scale):
    count = current.shape[1]
    highest = lax.Precision.HIGHEST
    inner_prod = lax.dot_general(
        previous,
        current,
        (((0,), (0,)), ((), ())),
        precision=highest,
        preferred_element_type=jnp.float32,
    )
    distance = (
        jnp.sum(previous * previous, axis=0)[:, None]
        + jnp.sum(current * current, axis=0)[None, :]
        - 2.0 * inner_prod
    )
    kernel = jnp.exp(-2.0 * distance / current.shape[0])
    predicted = lax.dot_general(
        fingerprints,
        current,
        (((0,), (0,)), ((), ())),
        precision=highest,
        preferred_element_type=jnp.float32,
    )
    misfit = tracer_scale[:, None] * (observed[:, None] - predicted)
    likelihood = jnp.exp(-0.5 * jnp.sum(misfit * misfit, axis=0))
    likelihood = likelihood / jnp.max(likelihood)
    parent = (parent_ids[None, :] == jnp.arange(count, dtype=jnp.int32)[:, None]).astype(
        jnp.float32
    )
    return likelihood[None, :] * (parent + mixing * kernel)


def vec_mat(u_row, mat):
    n = mat.shape[0]
    u_col = jnp.transpose(jnp.broadcast_to(u_row[0:1, :], (128, n)))
    parts = []
    for g in range(n // 128):
        block = mat[:, g * 128:(g + 1) * 128]
        parts.append(jnp.sum(block * u_col, axis=0, keepdims=True))
    return jnp.concatenate(parts, axis=1)


def normalized(v):
    return v / jnp.sum(v)


def spread(v, like):
    return jnp.broadcast_to(v, like.shape)


def chain_kernel(
    steps, stride, *refs,
):
    n_in = stride + 4
    hbm = refs[:n_in - 1]
    start_ref = refs[n_in - 1]
    out_ref, recv_buf, send_buf, send_sem, recv_sem, load_sem = refs[n_in:n_in + 6]
    local = refs[n_in + 6:]
    me = lax.axis_index("tm")
    row = lax.axis_index("rows")
    last = steps - 1
    phase = me % stride
    node = phase == 0

    loads = [
        pltpu.make_async_copy(hbm[i], local[i], load_sem.at[i]) for i in range(len(hbm))
    ]
    for load in loads:
        load.start()
    block_ref, combined_ref, first_ref, second_ref = local[:4]
    befores = local[4:]

    barrier = pltpu.get_barrier_semaphore()

    def greet(other):
        pl.semaphore_signal(barrier, 1, device_id=(other, row), device_id_type=MESH)

    @pl.when(node)
    def _():
        for d in range(1, stride + 1):
            @pl.when(me + d <= last)
            def _():
                greet(me + d)

        @pl.when(me >= stride)
        def _():
            greet(me - stride)

    @pl.when(jnp.logical_not(node))
    def _():
        greet(me - phase)

    partners = jnp.where(
        node,
        jnp.minimum(last - me, stride) + (me >= stride).astype(jnp.int32),
        1,
    )
    for amount in range(1, stride + 2):
        @pl.when(partners == amount)
        def _():
            pl.semaphore_wait(barrier, amount)

    def copy_to(d):
        return pltpu.make_async_remote_copy(
            src_ref=send_buf,
            dst_ref=recv_buf,
            send_sem=send_sem.at[d - 1],
            recv_sem=recv_sem,
            device_id=(jnp.minimum(me + d, last), row),
            device_id_type=MESH,
        )

    copies = [copy_to(d) for d in range(1, stride + 1)]

    def send_all(v):
        send_buf[...] = v
        for d in range(1, stride + 1):
            @pl.when(me + d <= last)
            def _():
                copies[d - 1].start()

    loads[0].wait()
    loads[1].wait()

    @pl.when(me == 0)
    def _():
        out_ref[...] = start_ref[...]
        send_all(normalized(vec_mat(start_ref[...], block_ref[...])))

    @pl.when(me > 0)
    def _():
        copies[0].wait_recv()
        out_ref[...] = spread(recv_buf[...], out_ref)

    @pl.when(jnp.logical_and(node, me > 0))
    def _():
        send_all(normalized(vec_mat(out_ref[...], combined_ref[...])))

    for load in loads[4:]:
        load.wait()
    lag = jnp.where(node, jnp.where(me > 0, stride - 1, 0), phase - 1)
    for amount in range(1, stride):
        @pl.when(lag == amount)
        def _():
            u = out_ref[...]
            for d in range(amount, 0, -1):
                u = spread(normalized(vec_mat(u, befores[d - 1][...])), out_ref)
            out_ref[...] = u

    loads[2].wait()
    loads[3].wait()
    incoming = out_ref[...]
    w_first = normalized(vec_mat(incoming, first_ref[...]))
    w_second = normalized(vec_mat(spread(w_first, incoming), second_ref[...]))
    out_ref[...] = jnp.concatenate(
        [w_first, w_second, jnp.zeros((incoming.shape[0] - 2, incoming.shape[1]), jnp.float32)],
        axis=0,
    )

    @pl.when(node)
    def _():
        for d in range(1, stride + 1):
            @pl.when(me + d <= last)
            def _():
                copies[d - 1].wait_send()


def chain(block, combined, first, second, befores, start, steps, stride):
    count = block.shape[0]
    matrices = [block, combined, first, second] + list(befores)
    return pl.pallas_call(
        functools.partial(chain_kernel, steps, stride),
        out_shape=jax.ShapeDtypeStruct((8, count), jnp.float32),
        in_specs=[pl.BlockSpec(memory_space=pl.ANY)] * len(matrices)
        + [pl.BlockSpec(memory_space=pltpu.VMEM)],
        out_specs=pl.BlockSpec(memory_space=pltpu.VMEM),
        scratch_shapes=[
            pltpu.VMEM((1, count), jnp.float32),
            pltpu.VMEM((1, count), jnp.float32),
            pltpu.SemaphoreType.DMA((stride,)),
            pltpu.SemaphoreType.DMA,
            pltpu.SemaphoreType.DMA((len(matrices),)),
        ]
        + [pltpu.VMEM((count, count), jnp.float32) for _ in matrices],
        compiler_params=pltpu.CompilerParams(
            collective_id=0, has_side_effects=True, vmem_limit_bytes=48 * 1024 * 1024
        ),
    )(*matrices, start)


def block_product(matrices):
    block = matrices[0]
    for matrix in matrices[1:]:
        block = jnp.dot(
            block, matrix, precision=lax.Precision.HIGH, preferred_element_type=jnp.float32
        )
    return block


def shards(states, ancestors, tracer_obs, jitter, fingerprints, tracer_scale, prior_weights):
    count = states.shape[2]
    own_rows = count // lax.axis_size("rows")
    row_start = lax.axis_index("rows") * own_rows
    steps = lax.axis_size("tm")
    stride = STRIDE
    local = states.shape[0]
    dims = states.shape[1]
    tracers = tracer_obs.shape[1]

    count_pad = jnp.zeros((local, count - tracers - 1), jnp.float32)
    extra = jnp.concatenate(
        [
            ancestors.astype(jnp.float32)[:, None, :],
            jnp.concatenate([tracer_obs, jitter[:, None], count_pad], axis=1)[:, None, :],
        ],
        axis=1,
    )
    packed = jnp.concatenate([states, extra], axis=1)

    def need(k):
        if k % stride == 0:
            return stride - 1 if k > 0 else 0
        return k % stride - 1

    devices = range(steps)

    def sent(block, distance, wanted):
        route = [(i - distance, i) for i in devices if i - distance >= 0 and wanted(i)]
        return lax.ppermute(block, "tm", route)

    core = lax.axis_index("rows") % 2
    half_rows = dims // 2
    packed_half = lax.dynamic_index_in_dim(packed, core, 0, keepdims=False)
    rim_half = lax.dynamic_slice_in_dim(states[-1], core * half_rows, half_rows, 0)
    fetched = [sent(packed_half, d, lambda i, d=d: need(i) >= d) for d in range(1, stride)]
    fetched += [sent(rim_half, e, lambda i, e=e: need(i) + 1 == e) for e in range(1, stride + 1)]
    bundle = jnp.concatenate(fetched, axis=0)
    pairs = [(r, r ^ 1) for r in range(lax.axis_size("rows"))]
    other = lax.ppermute(bundle, "rows", pairs)
    first_half = jnp.where(core == 0, bundle, other)
    second_half = jnp.where(core == 0, other, bundle)
    rows_of = [f.shape[0] for f in fetched]
    offsets = [sum(rows_of[:i]) for i in range(len(rows_of) + 1)]

    def joined(i):
        lo, hi = offsets[i], offsets[i + 1]
        return jnp.concatenate([first_half[lo:hi], second_half[lo:hi]], axis=0)

    packs = [packed] + [joined(i).reshape(packed.shape) for i in range(stride - 1)]
    rim_parts = [joined(stride - 1 + i) for i in range(stride)]
    rims = [
        (packs[d + 1][-1, :dims, :] if d + 1 < stride else 0.0) + rim_parts[d]
        for d in range(stride)
    ]

    def matrices_of(rim, pack):
        block_states = pack[:, :dims, :]
        parents = pack[:, dims, :].astype(jnp.int32)
        observed = pack[:, dims + 1, :tracers]
        mixing = pack[:, dims + 1, tracers]
        previous = jnp.concatenate([rim[None], block_states[:-1]], axis=0)
        return [
            transition(
                previous[s], block_states[s], parents[s], observed[s], mixing[s],
                fingerprints, tracer_scale,
            )
            for s in range(local)
        ]

    own = matrices_of(rims[0], packs[0])
    blocks = [block_product(own)] + [
        block_product(matrices_of(rims[d], packs[d])) for d in range(1, stride)
    ]
    combined = block_product(blocks[::-1])

    start = prior_weights / jnp.sum(prior_weights)
    start8 = jnp.broadcast_to(start[None, :], (8, count))
    weights = chain(blocks[0], combined, own[0], own[1], blocks[1:], start8, steps, stride)
    mine = lax.dynamic_slice_in_dim(weights[:local], row_start, own_rows, 1)
    return count * mine


def solution(mesh):
    return jax.shard_map(
        shards,
        mesh=mesh,
        in_specs=(P("tm", None, None), P("tm", None), P("tm", None), P("tm"), P(), P(), P()),
        out_specs=P("tm", "rows"),
        check_vma=False,
    )
```

```python
import functools

import jax
import jax.numpy as jnp
from jax import lax
from jax.experimental import pallas as pl
from jax.experimental.pallas import tpu as pltpu
from jax.sharding import PartitionSpec as P

MESH = pl.DeviceIdType.MESH
STRIDE = 3


def shifted(block, axis, distance):
    devices = range(lax.axis_size(axis))
    route = [(i - distance, i) for i in devices if i - distance in devices]
    return lax.ppermute(block, axis, route)


def transition(previous, current, parent_ids, observed, mixing, fingerprints, tracer_scale):
    count = current.shape[1]
    highest = lax.Precision.HIGHEST
    inner_prod = lax.dot_general(
        previous,
        current,
        (((0,), (0,)), ((), ())),
        precision=highest,
        preferred_element_type=jnp.float32,
    )
    distance = (
        jnp.sum(previous * previous, axis=0)[:, None]
        + jnp.sum(current * current, axis=0)[None, :]
        - 2.0 * inner_prod
    )
    kernel = jnp.exp(-2.0 * distance / current.shape[0])
    predicted = lax.dot_general(
        fingerprints,
        current,
        (((0,), (0,)), ((), ())),
        precision=highest,
        preferred_element_type=jnp.float32,
    )
    misfit = tracer_scale[:, None] * (observed[:, None] - predicted)
    likelihood = jnp.exp(-0.5 * jnp.sum(misfit * misfit, axis=0))
    likelihood = likelihood / jnp.max(likelihood)
    parent = (parent_ids[None, :] == jnp.arange(count, dtype=jnp.int32)[:, None]).astype(
        jnp.float32
    )
    return likelihood[None, :] * (parent + mixing * kernel)


def vec_mat(u_row, mat):
    n = mat.shape[0]
    u_col = jnp.transpose(jnp.broadcast_to(u_row[0:1, :], (128, n)))
    parts = []
    for g in range(n // 128):
        block = mat[:, g * 128:(g + 1) * 128]
        parts.append(jnp.sum(block * u_col, axis=0, keepdims=True))
    return jnp.concatenate(parts, axis=1)


def normalized(v):
    return v / jnp.sum(v)


def spread(v, like):
    return jnp.broadcast_to(v, like.shape)


def chain_kernel(
    steps, stride, *refs,
):
    n_in = stride + 4
    hbm = refs[:n_in - 1]
    start_ref = refs[n_in - 1]
    out_ref, recv_buf, send_buf, send_sem, recv_sem, load_sem = refs[n_in:n_in + 6]
    local = refs[n_in + 6:]
    me = lax.axis_index("tm")
    row = lax.axis_index("rows")
    last = steps - 1
    phase = me % stride
    node = phase == 0

    loads = [
        pltpu.make_async_copy(hbm[i], local[i], load_sem.at[i]) for i in range(len(hbm))
    ]
    for load in loads:
        load.start()
    block_ref, combined_ref, first_ref, second_ref = local[:4]
    befores = local[4:]

    barrier = pltpu.get_barrier_semaphore()

    def greet(other):
        pl.semaphore_signal(barrier, 1, device_id=(other, row), device_id_type=MESH)

    @pl.when(node)
    def _():
        for d in range(1, stride + 1):
            @pl.when(me + d <= last)
            def _():
                greet(me + d)

        @pl.when(me >= stride)
        def _():
            greet(me - stride)

    @pl.when(jnp.logical_not(node))
    def _():
        greet(me - phase)

    partners = jnp.where(
        node,
        jnp.minimum(last - me, stride) + (me >= stride).astype(jnp.int32),
        1,
    )
    for amount in range(1, stride + 2):
        @pl.when(partners == amount)
        def _():
            pl.semaphore_wait(barrier, amount)

    def copy_to(d):
        return pltpu.make_async_remote_copy(
            src_ref=send_buf,
            dst_ref=recv_buf,
            send_sem=send_sem.at[d - 1],
            recv_sem=recv_sem,
            device_id=(jnp.minimum(me + d, last), row),
            device_id_type=MESH,
        )

    copies = [copy_to(d) for d in range(1, stride + 1)]

    def send_all(v):
        send_buf[...] = v
        for d in range(1, stride + 1):
            @pl.when(me + d <= last)
            def _():
                copies[d - 1].start()

    loads[0].wait()
    loads[1].wait()

    @pl.when(me == 0)
    def _():
        out_ref[...] = start_ref[...]
        send_all(normalized(vec_mat(start_ref[...], block_ref[...])))

    @pl.when(me > 0)
    def _():
        copies[0].wait_recv()
        out_ref[...] = spread(recv_buf[...], out_ref)

    @pl.when(jnp.logical_and(node, me > 0))
    def _():
        send_all(normalized(vec_mat(out_ref[...], combined_ref[...])))

    for load in loads[4:]:
        load.wait()
    lag = jnp.where(node, jnp.where(me > 0, stride - 1, 0), phase - 1)
    for amount in range(1, stride):
        @pl.when(lag == amount)
        def _():
            u = out_ref[...]
            for d in range(amount, 0, -1):
                u = spread(normalized(vec_mat(u, befores[d - 1][...])), out_ref)
            out_ref[...] = u

    loads[2].wait()
    loads[3].wait()
    incoming = out_ref[...]
    w_first = normalized(vec_mat(incoming, first_ref[...]))
    w_second = normalized(vec_mat(spread(w_first, incoming), second_ref[...]))
    out_ref[...] = jnp.concatenate(
        [w_first, w_second, jnp.zeros((incoming.shape[0] - 2, incoming.shape[1]), jnp.float32)],
        axis=0,
    )

    @pl.when(node)
    def _():
        for d in range(1, stride + 1):
            @pl.when(me + d <= last)
            def _():
                copies[d - 1].wait_send()


def chain(block, combined, first, second, befores, start, steps, stride):
    count = block.shape[0]
    matrices = [block, combined, first, second] + list(befores)
    return pl.pallas_call(
        functools.partial(chain_kernel, steps, stride),
        out_shape=jax.ShapeDtypeStruct((8, count), jnp.float32),
        in_specs=[pl.BlockSpec(memory_space=pl.ANY)] * len(matrices)
        + [pl.BlockSpec(memory_space=pltpu.VMEM)],
        out_specs=pl.BlockSpec(memory_space=pltpu.VMEM),
        scratch_shapes=[
            pltpu.VMEM((1, count), jnp.float32),
            pltpu.VMEM((1, count), jnp.float32),
            pltpu.SemaphoreType.DMA((stride,)),
            pltpu.SemaphoreType.DMA,
            pltpu.SemaphoreType.DMA((len(matrices),)),
        ]
        + [pltpu.VMEM((count, count), jnp.float32) for _ in matrices],
        compiler_params=pltpu.CompilerParams(
            collective_id=0, has_side_effects=True, vmem_limit_bytes=48 * 1024 * 1024
        ),
    )(*matrices, start)


def block_product(matrices):
    block = matrices[0]
    for matrix in matrices[1:]:
        block = jnp.dot(
            block, matrix, precision=lax.Precision.HIGH, preferred_element_type=jnp.float32
        )
    return block


def shards(states, ancestors, tracer_obs, jitter, fingerprints, tracer_scale, prior_weights):
    count = states.shape[2]
    own_rows = count // lax.axis_size("rows")
    row_start = lax.axis_index("rows") * own_rows
    steps = lax.axis_size("tm")
    stride = STRIDE
    local = states.shape[0]
    dims = states.shape[1]
    tracers = tracer_obs.shape[1]

    count_pad = jnp.zeros((local, count - tracers - 1), jnp.float32)
    extra = jnp.concatenate(
        [
            ancestors.astype(jnp.float32)[:, None, :],
            jnp.concatenate([tracer_obs, jitter[:, None], count_pad], axis=1)[:, None, :],
        ],
        axis=1,
    )
    packed = jnp.concatenate([states, extra], axis=1)

    def need(k):
        if k % stride == 0:
            return stride - 1 if k > 0 else 0
        return k % stride - 1

    devices = range(steps)

    def sent(block, distance, wanted):
        route = [(i - distance, i) for i in devices if i - distance >= 0 and wanted(i)]
        return lax.ppermute(block, "tm", route)

    core = lax.axis_index("rows") % 2
    half_rows = dims // 2
    packed_half = lax.dynamic_index_in_dim(packed, core, 0, keepdims=False)
    rim_half = lax.dynamic_slice_in_dim(states[-1], core * half_rows, half_rows, 0)
    fetched = [sent(packed_half, d, lambda i, d=d: need(i) >= d) for d in range(1, stride)]
    fetched += [sent(rim_half, e, lambda i, e=e: need(i) + 1 == e) for e in range(1, stride + 1)]
    bundle = jnp.concatenate(fetched, axis=0)
    pairs = [(r, r ^ 1) for r in range(lax.axis_size("rows"))]
    other = lax.ppermute(bundle, "rows", pairs)
    first_half = jnp.where(core == 0, bundle, other)
    second_half = jnp.where(core == 0, other, bundle)
    rows_of = [f.shape[0] for f in fetched]
    offsets = [sum(rows_of[:i]) for i in range(len(rows_of) + 1)]

    def joined(i):
        lo, hi = offsets[i], offsets[i + 1]
        return jnp.concatenate([first_half[lo:hi], second_half[lo:hi]], axis=0)

    packs = [packed] + [joined(i).reshape(packed.shape) for i in range(stride - 1)]
    rim_parts = [joined(stride - 1 + i) for i in range(stride)]
    rims = [
        (packs[d + 1][-1, :dims, :] if d + 1 < stride else 0.0) + rim_parts[d]
        for d in range(stride)
    ]

    previous = []
    current = []
    parents = []
    observed = []
    mixing = []
    for d in range(stride):
        block_states = packs[d][:, :dims, :]
        previous += [rims[d], block_states[0]]
        current += [block_states[0], block_states[1]]
        parents.append(packs[d][:, dims, :])
        observed.append(packs[d][:, dims + 1, :tracers])
        mixing.append(packs[d][:, dims + 1, tracers])
    weights_all = jax.vmap(transition, in_axes=(0, 0, 0, 0, 0, None, None))(
        jnp.stack(previous),
        jnp.stack(current),
        jnp.concatenate(parents).astype(jnp.int32),
        jnp.concatenate(observed),
        jnp.concatenate(mixing),
        fingerprints,
        tracer_scale,
    )
    products = lax.dot_general(
        weights_all[0::2],
        weights_all[1::2],
        (((2,), (1,)), ((0,), (0,))),
        precision=lax.Precision.HIGH,
        preferred_element_type=jnp.float32,
    )
    blocks = [products[d] for d in range(stride)]
    combined = block_product(blocks[::-1])
    own = [weights_all[0], weights_all[1]]

    start = prior_weights / jnp.sum(prior_weights)
    start8 = jnp.broadcast_to(start[None, :], (8, count))
    weights = chain(blocks[0], combined, own[0], own[1], blocks[1:], start8, steps, stride)
    mine = lax.dynamic_slice_in_dim(weights[:local], row_start, own_rows, 1)
    return count * mine


def solution(mesh):
    return jax.shard_map(
        shards,
        mesh=mesh,
        in_specs=(P("tm", None, None), P("tm", None), P("tm", None), P("tm"), P(), P(), P()),
        out_specs=P("tm", "rows"),
        check_vma=False,
    )
```

```python
import functools

import jax
import jax.numpy as jnp
from jax import lax
from jax.experimental import pallas as pl
from jax.experimental.pallas import tpu as pltpu
from jax.sharding import PartitionSpec as P

MESH = pl.DeviceIdType.MESH
STRIDE = 3


def shifted(block, axis, distance):
    devices = range(lax.axis_size(axis))
    route = [(i - distance, i) for i in devices if i - distance in devices]
    return lax.ppermute(block, axis, route)


def transition(previous, current, parent_ids, observed, mixing, fingerprints, tracer_scale):
    count = current.shape[1]
    highest = lax.Precision.HIGHEST
    inner_prod = lax.dot_general(
        previous,
        current,
        (((0,), (0,)), ((), ())),
        precision=highest,
        preferred_element_type=jnp.float32,
    )
    distance = (
        jnp.sum(previous * previous, axis=0)[:, None]
        + jnp.sum(current * current, axis=0)[None, :]
        - 2.0 * inner_prod
    )
    kernel = jnp.exp(-2.0 * distance / current.shape[0])
    predicted = lax.dot_general(
        fingerprints,
        current,
        (((0,), (0,)), ((), ())),
        precision=highest,
        preferred_element_type=jnp.float32,
    )
    misfit = tracer_scale[:, None] * (observed[:, None] - predicted)
    likelihood = jnp.exp(-0.5 * jnp.sum(misfit * misfit, axis=0))
    likelihood = likelihood / jnp.max(likelihood)
    parent = (parent_ids[None, :] == jnp.arange(count, dtype=jnp.int32)[:, None]).astype(
        jnp.float32
    )
    return likelihood[None, :] * (parent + mixing * kernel)


def vec_mat(u_row, mat):
    n = mat.shape[0]
    u_col = jnp.transpose(jnp.broadcast_to(u_row[0:1, :], (128, n)))
    parts = []
    for g in range(n // 128):
        block = mat[:, g * 128:(g + 1) * 128]
        parts.append(jnp.sum(block * u_col, axis=0, keepdims=True))
    return jnp.concatenate(parts, axis=1)


def normalized(v):
    return v / jnp.sum(v)


def spread(v, like):
    return jnp.broadcast_to(v, like.shape)


def chain_kernel(
    steps, stride, *refs,
):
    weights_hbm, products_hbm, combined_hbm, prior_ref = refs[:4]
    out_ref, recv_buf, send_buf, send_sem, recv_sem, load_sem = refs[4:10]
    local = refs[10:]
    me = lax.axis_index("tm")
    row = lax.axis_index("rows")
    last = steps - 1
    phase = me % stride
    node = phase == 0

    sources = [products_hbm.at[0], combined_hbm, weights_hbm.at[0], weights_hbm.at[1]]
    sources += [products_hbm.at[d] for d in range(1, stride)]
    loads = [
        pltpu.make_async_copy(sources[i], local[i], load_sem.at[i]) for i in range(len(sources))
    ]
    for load in loads:
        load.start()
    block_ref, combined_ref, first_ref, second_ref = local[:4]
    befores = local[4:]

    barrier = pltpu.get_barrier_semaphore()

    def greet(other):
        pl.semaphore_signal(barrier, 1, device_id=(other, row), device_id_type=MESH)

    @pl.when(node)
    def _():
        for d in range(1, stride + 1):
            @pl.when(me + d <= last)
            def _():
                greet(me + d)

        @pl.when(me >= stride)
        def _():
            greet(me - stride)

    @pl.when(jnp.logical_not(node))
    def _():
        greet(me - phase)

    partners = jnp.where(
        node,
        jnp.minimum(last - me, stride) + (me >= stride).astype(jnp.int32),
        1,
    )
    for amount in range(1, stride + 2):
        @pl.when(partners == amount)
        def _():
            pl.semaphore_wait(barrier, amount)

    def copy_to(d):
        return pltpu.make_async_remote_copy(
            src_ref=send_buf,
            dst_ref=recv_buf,
            send_sem=send_sem.at[d - 1],
            recv_sem=recv_sem,
            device_id=(jnp.minimum(me + d, last), row),
            device_id_type=MESH,
        )

    copies = [copy_to(d) for d in range(1, stride + 1)]

    def send_all(v):
        send_buf[...] = v
        for d in range(1, stride + 1):
            @pl.when(me + d <= last)
            def _():
                copies[d - 1].start()

    loads[0].wait()
    loads[1].wait()

    @pl.when(me == 0)
    def _():
        start = spread(normalized(prior_ref[0:1, :]), out_ref)
        out_ref[...] = start
        send_all(normalized(vec_mat(start, block_ref[...])))

    @pl.when(me > 0)
    def _():
        copies[0].wait_recv()
        out_ref[...] = spread(recv_buf[...], out_ref)

    @pl.when(jnp.logical_and(node, me > 0))
    def _():
        send_all(normalized(vec_mat(out_ref[...], combined_ref[...])))

    for load in loads[4:]:
        load.wait()
    lag = jnp.where(node, jnp.where(me > 0, stride - 1, 0), phase - 1)
    for amount in range(1, stride):
        @pl.when(lag == amount)
        def _():
            u = out_ref[...]
            for d in range(amount, 0, -1):
                u = spread(normalized(vec_mat(u, befores[d - 1][...])), out_ref)
            out_ref[...] = u

    loads[2].wait()
    loads[3].wait()
    incoming = out_ref[...]
    w_first = normalized(vec_mat(incoming, first_ref[...]))
    w_second = normalized(vec_mat(spread(w_first, incoming), second_ref[...]))
    out_ref[...] = jnp.concatenate(
        [w_first, w_second, jnp.zeros((incoming.shape[0] - 2, incoming.shape[1]), jnp.float32)],
        axis=0,
    )

    @pl.when(node)
    def _():
        for d in range(1, stride + 1):
            @pl.when(me + d <= last)
            def _():
                copies[d - 1].wait_send()


def chain(weights_all, products, combined, prior, steps, stride):
    count = combined.shape[0]
    loaded = stride + 3
    return pl.pallas_call(
        functools.partial(chain_kernel, steps, stride),
        out_shape=jax.ShapeDtypeStruct((8, count), jnp.float32),
        in_specs=[pl.BlockSpec(memory_space=pl.ANY)] * 3
        + [pl.BlockSpec(memory_space=pltpu.VMEM)],
        out_specs=pl.BlockSpec(memory_space=pltpu.VMEM),
        scratch_shapes=[
            pltpu.VMEM((1, count), jnp.float32),
            pltpu.VMEM((1, count), jnp.float32),
            pltpu.SemaphoreType.DMA((stride,)),
            pltpu.SemaphoreType.DMA,
            pltpu.SemaphoreType.DMA((loaded,)),
        ]
        + [pltpu.VMEM((count, count), jnp.float32) for _ in range(loaded)],
        compiler_params=pltpu.CompilerParams(
            collective_id=0, has_side_effects=True, vmem_limit_bytes=48 * 1024 * 1024
        ),
    )(weights_all, products, combined, prior)


def block_product(matrices):
    block = matrices[0]
    for matrix in matrices[1:]:
        block = jnp.dot(
            block, matrix, precision=lax.Precision.HIGH, preferred_element_type=jnp.float32
        )
    return block


def shards(states, ancestors, tracer_obs, jitter, fingerprints, tracer_scale, prior_weights):
    count = states.shape[2]
    own_rows = count // lax.axis_size("rows")
    row_start = lax.axis_index("rows") * own_rows
    steps = lax.axis_size("tm")
    stride = STRIDE
    local = states.shape[0]
    dims = states.shape[1]
    tracers = tracer_obs.shape[1]

    count_pad = jnp.zeros((local, count - tracers - 1), jnp.float32)
    extra = jnp.concatenate(
        [
            ancestors.astype(jnp.float32)[:, None, :],
            jnp.concatenate([tracer_obs, jitter[:, None], count_pad], axis=1)[:, None, :],
        ],
        axis=1,
    )
    packed = jnp.concatenate([states, extra], axis=1)

    def need(k):
        if k % stride == 0:
            return stride - 1 if k > 0 else 0
        return k % stride - 1

    devices = range(steps)

    def sent(block, distance, wanted):
        route = [(i - distance, i) for i in devices if i - distance >= 0 and wanted(i)]
        return lax.ppermute(block, "tm", route)

    core = lax.axis_index("rows") % 2
    half_rows = dims // 2
    packed_half = lax.dynamic_index_in_dim(packed, core, 0, keepdims=False)
    rim_half = lax.dynamic_slice_in_dim(states[-1], core * half_rows, half_rows, 0)
    fetched = [sent(packed_half, d, lambda i, d=d: need(i) >= d) for d in range(1, stride)]
    fetched += [sent(rim_half, e, lambda i, e=e: need(i) + 1 == e) for e in range(1, stride + 1)]
    bundle = jnp.concatenate(fetched, axis=0)
    pairs = [(r, r ^ 1) for r in range(lax.axis_size("rows"))]
    other = lax.ppermute(bundle, "rows", pairs)
    first_half = jnp.where(core == 0, bundle, other)
    second_half = jnp.where(core == 0, other, bundle)
    rows_of = [f.shape[0] for f in fetched]
    offsets = [sum(rows_of[:i]) for i in range(len(rows_of) + 1)]

    def joined(i):
        lo, hi = offsets[i], offsets[i + 1]
        return jnp.concatenate([first_half[lo:hi], second_half[lo:hi]], axis=0)

    packs = [packed] + [joined(i).reshape(packed.shape) for i in range(stride - 1)]
    rim_parts = [joined(stride - 1 + i) for i in range(stride)]
    rims = [
        (packs[d + 1][-1, :dims, :] if d + 1 < stride else 0.0) + rim_parts[d]
        for d in range(stride)
    ]

    previous = []
    current = []
    parents = []
    observed = []
    mixing = []
    for d in range(stride):
        block_states = packs[d][:, :dims, :]
        previous += [rims[d], block_states[0]]
        current += [block_states[0], block_states[1]]
        parents.append(packs[d][:, dims, :])
        observed.append(packs[d][:, dims + 1, :tracers])
        mixing.append(packs[d][:, dims + 1, tracers])
    weights_all = jax.vmap(transition, in_axes=(0, 0, 0, 0, 0, None, None))(
        jnp.stack(previous),
        jnp.stack(current),
        jnp.concatenate(parents).astype(jnp.int32),
        jnp.concatenate(observed),
        jnp.concatenate(mixing),
        fingerprints,
        tracer_scale,
    )
    products = lax.dot_general(
        weights_all[0::2],
        weights_all[1::2],
        (((2,), (1,)), ((0,), (0,))),
        precision=lax.Precision.HIGH,
        preferred_element_type=jnp.float32,
    )
    combined = block_product([products[d] for d in range(stride - 1, -1, -1)])

    prior8 = jnp.broadcast_to(prior_weights[None, :], (8, count))
    weights = chain(weights_all, products, combined, prior8, steps, stride)
    mine = lax.dynamic_slice_in_dim(weights[:local], row_start, own_rows, 1)
    return count * mine


def solution(mesh):
    return jax.shard_map(
        shards,
        mesh=mesh,
        in_specs=(P("tm", None, None), P("tm", None), P("tm", None), P("tm"), P(), P(), P()),
        out_specs=P("tm", "rows"),
        check_vma=False,
    )
```

```python
import functools

import jax
import jax.numpy as jnp
from jax import lax
from jax.experimental import pallas as pl
from jax.experimental.pallas import tpu as pltpu
from jax.sharding import PartitionSpec as P

MESH = pl.DeviceIdType.MESH
STRIDE = 3
HEAD = 10


def shifted(block, axis, distance):
    devices = range(lax.axis_size(axis))
    route = [(i - distance, i) for i in devices if i - distance in devices]
    return lax.ppermute(block, axis, route)


def transition(previous, current, parent_ids, observed, mixing, fingerprints, tracer_scale):
    count = current.shape[1]
    highest = lax.Precision.HIGHEST
    inner_prod = lax.dot_general(
        previous,
        current,
        (((0,), (0,)), ((), ())),
        precision=highest,
        preferred_element_type=jnp.float32,
    )
    distance = (
        jnp.sum(previous * previous, axis=0)[:, None]
        + jnp.sum(current * current, axis=0)[None, :]
        - 2.0 * inner_prod
    )
    kernel = jnp.exp(-2.0 * distance / current.shape[0])
    predicted = lax.dot_general(
        fingerprints,
        current,
        (((0,), (0,)), ((), ())),
        precision=highest,
        preferred_element_type=jnp.float32,
    )
    misfit = tracer_scale[:, None] * (observed[:, None] - predicted)
    likelihood = jnp.exp(-0.5 * jnp.sum(misfit * misfit, axis=0))
    likelihood = likelihood / jnp.max(likelihood)
    parent = (parent_ids[None, :] == jnp.arange(count, dtype=jnp.int32)[:, None]).astype(
        jnp.float32
    )
    return likelihood[None, :] * (parent + mixing * kernel)


def vec_mat(u_row, mat):
    n = mat.shape[0]
    u_col = jnp.transpose(jnp.broadcast_to(u_row[0:1, :], (128, n)))
    parts = []
    for g in range(n // 128):
        block = mat[:, g * 128:(g + 1) * 128]
        parts.append(jnp.sum(block * u_col, axis=0, keepdims=True))
    return jnp.concatenate(parts, axis=1)


def normalized(v):
    return v / jnp.sum(v)


def spread(v, like):
    return jnp.broadcast_to(v, like.shape)


def chain_kernel(steps, stride, head, *refs):
    weights_hbm, block_hbm, befores_hbm, combined_hbm, prior_ref = refs[:5]
    out_ref, recv_buf, send_buf, send_sem, recv_sem, load_sem = refs[5:11]
    local = refs[11:]
    me = lax.axis_index("tm")
    row = lax.axis_index("rows")
    last = steps - 1
    offset = me - head
    phase = jnp.maximum(offset, 0) % stride
    tail = me > head
    tail_node = jnp.logical_and(tail, phase == 0)
    fans = jnp.logical_or(me == head, tail_node)

    sources = [block_hbm, combined_hbm, weights_hbm.at[0], weights_hbm.at[1]]
    sources += [befores_hbm.at[d] for d in range(stride - 1)]
    loads = [
        pltpu.make_async_copy(sources[i], local[i], load_sem.at[i]) for i in range(len(sources))
    ]
    for load in loads:
        load.start()
    block_ref, combined_ref, first_ref, second_ref = local[:4]
    befores = local[4:]

    source_gap = jnp.where(me <= head, 1, jnp.where(phase == 0, stride, phase))
    sends = jnp.where(me < head, 1, jnp.where(fans, jnp.minimum(last - me, stride), 0))

    barrier = pltpu.get_barrier_semaphore()

    def greet(other):
        pl.semaphore_signal(barrier, 1, device_id=(other, row), device_id_type=MESH)

    @pl.when(me > 0)
    def _():
        greet(me - source_gap)

    for d in range(1, stride + 1):
        @pl.when(d <= sends)
        def _():
            greet(me + d)

    partners = sends + (me > 0).astype(jnp.int32)
    for amount in range(1, stride + 2):
        @pl.when(partners == amount)
        def _():
            pl.semaphore_wait(barrier, amount)

    def copy_to(d):
        return pltpu.make_async_remote_copy(
            src_ref=send_buf,
            dst_ref=recv_buf,
            send_sem=send_sem.at[d - 1],
            recv_sem=recv_sem,
            device_id=(jnp.minimum(me + d, last), row),
            device_id_type=MESH,
        )

    copies = [copy_to(d) for d in range(1, stride + 1)]

    def send_all(v):
        send_buf[...] = v
        for d in range(1, stride + 1):
            @pl.when(d <= sends)
            def _():
                copies[d - 1].start()

    loads[0].wait()
    loads[1].wait()

    @pl.when(me == 0)
    def _():
        out_ref[...] = spread(normalized(prior_ref[0:1, :]), out_ref)

    @pl.when(me > 0)
    def _():
        copies[0].wait_recv()
        out_ref[...] = spread(recv_buf[...], out_ref)

    @pl.when(me <= head)
    def _():
        send_all(normalized(vec_mat(out_ref[...], block_ref[...])))

    @pl.when(tail_node)
    def _():
        send_all(normalized(vec_mat(out_ref[...], combined_ref[...])))

    for load in loads[4:]:
        load.wait()
    lag = jnp.where(tail_node, stride - 1, jnp.where(tail, phase - 1, 0))
    for amount in range(1, stride):
        @pl.when(lag == amount)
        def _():
            u = out_ref[...]
            for d in range(amount, 0, -1):
                u = spread(normalized(vec_mat(u, befores[d - 1][...])), out_ref)
            out_ref[...] = u

    loads[2].wait()
    loads[3].wait()
    incoming = out_ref[...]
    w_first = normalized(vec_mat(incoming, first_ref[...]))
    w_second = normalized(vec_mat(spread(w_first, incoming), second_ref[...]))
    out_ref[...] = jnp.concatenate(
        [w_first, w_second, jnp.zeros((incoming.shape[0] - 2, incoming.shape[1]), jnp.float32)],
        axis=0,
    )

    for d in range(1, stride + 1):
        @pl.when(d <= sends)
        def _():
            copies[d - 1].wait_send()


def chain(weights_own, block, befores, combined, prior, steps, stride, head):
    count = combined.shape[0]
    loaded = stride + 3
    return pl.pallas_call(
        functools.partial(chain_kernel, steps, stride, head),
        out_shape=jax.ShapeDtypeStruct((8, count), jnp.float32),
        in_specs=[pl.BlockSpec(memory_space=pl.ANY)] * 4
        + [pl.BlockSpec(memory_space=pltpu.VMEM)],
        out_specs=pl.BlockSpec(memory_space=pltpu.VMEM),
        scratch_shapes=[
            pltpu.VMEM((1, count), jnp.float32),
            pltpu.VMEM((1, count), jnp.float32),
            pltpu.SemaphoreType.DMA((stride,)),
            pltpu.SemaphoreType.DMA,
            pltpu.SemaphoreType.DMA((loaded,)),
        ]
        + [pltpu.VMEM((count, count), jnp.float32) for _ in range(loaded)],
        compiler_params=pltpu.CompilerParams(
            collective_id=0, has_side_effects=True, vmem_limit_bytes=48 * 1024 * 1024
        ),
    )(weights_own, block, befores, combined, prior)


def block_product(matrices):
    block = matrices[0]
    for matrix in matrices[1:]:
        block = jnp.dot(
            block, matrix, precision=lax.Precision.HIGH, preferred_element_type=jnp.float32
        )
    return block


def shards(states, ancestors, tracer_obs, jitter, fingerprints, tracer_scale, prior_weights):
    count = states.shape[2]
    own_rows = count // lax.axis_size("rows")
    row_start = lax.axis_index("rows") * own_rows
    steps = lax.axis_size("tm")
    stride = STRIDE
    head = min(HEAD, steps - 1)
    local = states.shape[0]
    dims = states.shape[1]
    tracers = tracer_obs.shape[1]
    me = lax.axis_index("tm")

    count_pad = jnp.zeros((local, count - tracers - 1), jnp.float32)
    extra = jnp.concatenate(
        [
            ancestors.astype(jnp.float32)[:, None, :],
            jnp.concatenate([tracer_obs, jitter[:, None], count_pad], axis=1)[:, None, :],
        ],
        axis=1,
    )
    packed = jnp.concatenate([states, extra], axis=1)

    def need(k):
        if k <= head:
            return 0
        phase = (k - head) % stride
        return stride - 1 if phase == 0 else phase - 1

    devices = range(steps)

    def sent(block, distance, wanted):
        route = [(i - distance, i) for i in devices if i - distance >= 0 and wanted(i)]
        return lax.ppermute(block, "tm", route)

    rim_own = sent(states[-1], 1, lambda i: True)

    core = lax.axis_index("rows") % 2
    half_rows = dims // 2
    packed_half = lax.dynamic_index_in_dim(packed, core, 0, keepdims=False)
    rim_half = lax.dynamic_slice_in_dim(states[-1], core * half_rows, half_rows, 0)
    fetched = [sent(packed_half, d, lambda i, d=d: need(i) >= d) for d in range(1, stride)]
    fetched += [sent(rim_half, e, lambda i, e=e: need(i) + 1 == e) for e in range(2, stride + 1)]
    bundle = jnp.concatenate(fetched, axis=0)
    pairs = [(r, r ^ 1) for r in range(lax.axis_size("rows"))]
    other = lax.ppermute(bundle, "rows", pairs)

    def own_matrices():
        return jax.vmap(transition, in_axes=(0, 0, 0, 0, 0, None, None))(
            jnp.stack([rim_own, states[0]]),
            states,
            ancestors,
            tracer_obs,
            jitter,
            fingerprints,
            tracer_scale,
        )

    weights_own = own_matrices()
    block_own = block_product([weights_own[0], weights_own[1]])

    def earlier(bundle, other):
        first_half = jnp.where(core == 0, bundle, other)
        second_half = jnp.where(core == 0, other, bundle)
        rows_of = [f.shape[0] for f in fetched]
        offsets = [sum(rows_of[:i]) for i in range(len(rows_of) + 1)]

        def joined(i):
            lo, hi = offsets[i], offsets[i + 1]
            return jnp.concatenate([first_half[lo:hi], second_half[lo:hi]], axis=0)

        packs = [packed] + [joined(i).reshape(packed.shape) for i in range(stride - 1)]
        rim_parts = [joined(stride - 1 + i) for i in range(stride - 1)]
        rims = [None] + [
            (packs[d + 1][-1, :dims, :] if d + 1 < stride else 0.0) + rim_parts[d - 1]
            for d in range(1, stride)
        ]
        previous = []
        current = []
        parents = []
        observed = []
        mixing = []
        for d in range(1, stride):
            block_states = packs[d][:, :dims, :]
            previous += [rims[d], block_states[0]]
            current += [block_states[0], block_states[1]]
            parents.append(packs[d][:, dims, :])
            observed.append(packs[d][:, dims + 1, :tracers])
            mixing.append(packs[d][:, dims + 1, tracers])
        weights_all = jax.vmap(transition, in_axes=(0, 0, 0, 0, 0, None, None))(
            jnp.stack(previous),
            jnp.stack(current),
            jnp.concatenate(parents).astype(jnp.int32),
            jnp.concatenate(observed),
            jnp.concatenate(mixing),
            fingerprints,
            tracer_scale,
        )
        products = lax.dot_general(
            weights_all[0::2],
            weights_all[1::2],
            (((2,), (1,)), ((0,), (0,))),
            precision=lax.Precision.HIGH,
            preferred_element_type=jnp.float32,
        )
        combined = block_product([products[d] for d in range(stride - 2, -1, -1)] + [block_own])
        return products, combined

    def skipped(bundle, other):
        return (
            jnp.zeros((stride - 1, count, count), jnp.float32),
            jnp.zeros((count, count), jnp.float32),
        )

    befores, combined = lax.cond(me > head, earlier, skipped, bundle, other)

    prior8 = jnp.broadcast_to(prior_weights[None, :], (8, count))
    weights = chain(weights_own, block_own, befores, combined, prior8, steps, stride, head)
    mine = lax.dynamic_slice_in_dim(weights[:local], row_start, own_rows, 1)
    return count * mine


def solution(mesh):
    return jax.shard_map(
        shards,
        mesh=mesh,
        in_specs=(P("tm", None, None), P("tm", None), P("tm", None), P("tm"), P(), P(), P()),
        out_specs=P("tm", "rows"),
        check_vma=False,
    )
```

```python
import functools

import jax
import jax.numpy as jnp
from jax import lax
from jax.experimental import pallas as pl
from jax.experimental.pallas import tpu as pltpu
from jax.sharding import PartitionSpec as P

MESH = pl.DeviceIdType.MESH
STRIDE = 3
HEAD = 13


def shifted(block, axis, distance):
    devices = range(lax.axis_size(axis))
    route = [(i - distance, i) for i in devices if i - distance in devices]
    return lax.ppermute(block, axis, route)


def transition(previous, current, parent_ids, observed, mixing, fingerprints, tracer_scale):
    count = current.shape[1]
    highest = lax.Precision.HIGHEST
    inner_prod = lax.dot_general(
        previous,
        current,
        (((0,), (0,)), ((), ())),
        precision=highest,
        preferred_element_type=jnp.float32,
    )
    distance = (
        jnp.sum(previous * previous, axis=0)[:, None]
        + jnp.sum(current * current, axis=0)[None, :]
        - 2.0 * inner_prod
    )
    kernel = jnp.exp(-2.0 * distance / current.shape[0])
    predicted = lax.dot_general(
        fingerprints,
        current,
        (((0,), (0,)), ((), ())),
        precision=highest,
        preferred_element_type=jnp.float32,
    )
    misfit = tracer_scale[:, None] * (observed[:, None] - predicted)
    likelihood = jnp.exp(-0.5 * jnp.sum(misfit * misfit, axis=0))
    likelihood = likelihood / jnp.max(likelihood)
    parent = (parent_ids[None, :] == jnp.arange(count, dtype=jnp.int32)[:, None]).astype(
        jnp.float32
    )
    return likelihood[None, :] * (parent + mixing * kernel)


def vec_mat(u_row, mat):
    n = mat.shape[0]
    u_col = jnp.transpose(jnp.broadcast_to(u_row[0:1, :], (128, n)))
    parts = []
    for g in range(n // 128):
        block = mat[:, g * 128:(g + 1) * 128]
        parts.append(jnp.sum(block * u_col, axis=0, keepdims=True))
    return jnp.concatenate(parts, axis=1)


def normalized(v):
    return v / jnp.sum(v)


def spread(v, like):
    return jnp.broadcast_to(v, like.shape)


def chain_kernel(steps, stride, head, *refs):
    weights_hbm, block_hbm, befores_hbm, combined_hbm, prior_ref = refs[:5]
    out_ref, recv_buf, send_buf, send_sem, recv_sem, load_sem = refs[5:11]
    local = refs[11:]
    me = lax.axis_index("tm")
    row = lax.axis_index("rows")
    last = steps - 1
    offset = me - head
    phase = jnp.maximum(offset, 0) % stride
    tail = me > head
    tail_node = jnp.logical_and(tail, phase == 0)
    fans = jnp.logical_or(me == head, tail_node)

    sources = [block_hbm, combined_hbm, weights_hbm.at[0], weights_hbm.at[1]]
    sources += [befores_hbm.at[d] for d in range(stride - 1)]
    loads = [
        pltpu.make_async_copy(sources[i], local[i], load_sem.at[i]) for i in range(len(sources))
    ]
    for load in loads:
        load.start()
    block_ref, combined_ref, first_ref, second_ref = local[:4]
    befores = local[4:]

    source_gap = jnp.where(me <= head, 1, jnp.where(phase == 0, stride, phase))
    sends = jnp.where(me < head, 1, jnp.where(fans, jnp.minimum(last - me, stride), 0))

    barrier = pltpu.get_barrier_semaphore()

    def greet(other):
        pl.semaphore_signal(barrier, 1, device_id=(other, row), device_id_type=MESH)

    @pl.when(me > 0)
    def _():
        greet(me - source_gap)

    for d in range(1, stride + 1):
        @pl.when(d <= sends)
        def _():
            greet(me + d)

    partners = sends + (me > 0).astype(jnp.int32)
    for amount in range(1, stride + 2):
        @pl.when(partners == amount)
        def _():
            pl.semaphore_wait(barrier, amount)

    def copy_to(d):
        return pltpu.make_async_remote_copy(
            src_ref=send_buf,
            dst_ref=recv_buf,
            send_sem=send_sem.at[d - 1],
            recv_sem=recv_sem,
            device_id=(jnp.minimum(me + d, last), row),
            device_id_type=MESH,
        )

    copies = [copy_to(d) for d in range(1, stride + 1)]

    def send_all(v):
        send_buf[...] = v
        for d in range(1, stride + 1):
            @pl.when(d <= sends)
            def _():
                copies[d - 1].start()

    loads[0].wait()
    loads[1].wait()

    @pl.when(me == 0)
    def _():
        out_ref[...] = spread(normalized(prior_ref[0:1, :]), out_ref)

    @pl.when(me > 0)
    def _():
        copies[0].wait_recv()
        out_ref[...] = spread(recv_buf[...], out_ref)

    @pl.when(me <= head)
    def _():
        send_all(normalized(vec_mat(out_ref[...], block_ref[...])))

    @pl.when(tail_node)
    def _():
        send_all(normalized(vec_mat(out_ref[...], combined_ref[...])))

    for load in loads[4:]:
        load.wait()
    lag = jnp.where(tail_node, stride - 1, jnp.where(tail, phase - 1, 0))
    for amount in range(1, stride):
        @pl.when(lag == amount)
        def _():
            u = out_ref[...]
            for d in range(amount, 0, -1):
                u = spread(normalized(vec_mat(u, befores[d - 1][...])), out_ref)
            out_ref[...] = u

    loads[2].wait()
    loads[3].wait()
    incoming = out_ref[...]
    w_first = normalized(vec_mat(incoming, first_ref[...]))
    w_second = normalized(vec_mat(spread(w_first, incoming), second_ref[...]))
    out_ref[...] = jnp.concatenate(
        [w_first, w_second, jnp.zeros((incoming.shape[0] - 2, incoming.shape[1]), jnp.float32)],
        axis=0,
    )

    for d in range(1, stride + 1):
        @pl.when(d <= sends)
        def _():
            copies[d - 1].wait_send()


def chain(weights_own, block, befores, combined, prior, steps, stride, head):
    count = combined.shape[0]
    loaded = stride + 3
    return pl.pallas_call(
        functools.partial(chain_kernel, steps, stride, head),
        out_shape=jax.ShapeDtypeStruct((8, count), jnp.float32),
        in_specs=[pl.BlockSpec(memory_space=pl.ANY)] * 4
        + [pl.BlockSpec(memory_space=pltpu.VMEM)],
        out_specs=pl.BlockSpec(memory_space=pltpu.VMEM),
        scratch_shapes=[
            pltpu.VMEM((1, count), jnp.float32),
            pltpu.VMEM((1, count), jnp.float32),
            pltpu.SemaphoreType.DMA((stride,)),
            pltpu.SemaphoreType.DMA,
            pltpu.SemaphoreType.DMA((loaded,)),
        ]
        + [pltpu.VMEM((count, count), jnp.float32) for _ in range(loaded)],
        compiler_params=pltpu.CompilerParams(
            collective_id=0, has_side_effects=True, vmem_limit_bytes=48 * 1024 * 1024
        ),
    )(weights_own, block, befores, combined, prior)


def block_product(matrices):
    block = matrices[0]
    for matrix in matrices[1:]:
        block = jnp.dot(
            block, matrix, precision=lax.Precision.HIGH, preferred_element_type=jnp.float32
        )
    return block


def shards(states, ancestors, tracer_obs, jitter, fingerprints, tracer_scale, prior_weights):
    count = states.shape[2]
    own_rows = count // lax.axis_size("rows")
    row_start = lax.axis_index("rows") * own_rows
    steps = lax.axis_size("tm")
    stride = STRIDE
    head = min(HEAD, steps - 1)
    local = states.shape[0]
    dims = states.shape[1]
    tracers = tracer_obs.shape[1]
    me = lax.axis_index("tm")

    count_pad = jnp.zeros((local, count - tracers - 1), jnp.float32)
    extra = jnp.concatenate(
        [
            ancestors.astype(jnp.float32)[:, None, :],
            jnp.concatenate([tracer_obs, jitter[:, None], count_pad], axis=1)[:, None, :],
            jnp.zeros((local, 6, count), jnp.float32),
        ],
        axis=1,
    )
    packed = jnp.concatenate([states, extra], axis=1)

    def need(k):
        if k <= head:
            return 0
        phase = (k - head) % stride
        return stride - 1 if phase == 0 else phase - 1

    devices = range(steps)

    def sent(block, distance, wanted):
        route = [(i - distance, i) for i in devices if i - distance >= 0 and wanted(i)]
        return lax.ppermute(block, "tm", route)

    rim_own = sent(states[-1], 1, lambda i: True)

    core = lax.axis_index("rows") % 2
    half_rows = dims // 2
    packed_half = lax.dynamic_index_in_dim(packed, core, 0, keepdims=False)
    rim_half = lax.dynamic_slice_in_dim(states[-1], core * half_rows, half_rows, 0)
    fetched = [sent(packed_half, d, lambda i, d=d: need(i) >= d) for d in range(1, stride)]
    fetched += [sent(rim_half, e, lambda i, e=e: need(i) + 1 == e) for e in range(2, stride + 1)]
    bundle = jnp.concatenate(fetched, axis=0)
    pairs = [(r, r ^ 1) for r in range(lax.axis_size("rows"))]
    other = lax.ppermute(bundle, "rows", pairs)

    def own_matrices():
        return jax.vmap(transition, in_axes=(0, 0, 0, 0, 0, None, None))(
            jnp.stack([rim_own, states[0]]),
            states,
            ancestors,
            tracer_obs,
            jitter,
            fingerprints,
            tracer_scale,
        )

    weights_own = own_matrices()
    block_own = block_product([weights_own[0], weights_own[1]])

    def earlier(bundle, other):
        first_half = jnp.where(core == 0, bundle, other)
        second_half = jnp.where(core == 0, other, bundle)
        rows_of = [f.shape[0] for f in fetched]
        offsets = [sum(rows_of[:i]) for i in range(len(rows_of) + 1)]

        def joined(i):
            lo, hi = offsets[i], offsets[i + 1]
            return jnp.concatenate([first_half[lo:hi], second_half[lo:hi]], axis=0)

        packs = [packed] + [joined(i).reshape(packed.shape) for i in range(stride - 1)]
        rim_parts = [joined(stride - 1 + i) for i in range(stride - 1)]
        rims = [None] + [
            (packs[d + 1][-1, :dims, :] if d + 1 < stride else 0.0) + rim_parts[d - 1]
            for d in range(1, stride)
        ]
        previous = []
        current = []
        parents = []
        observed = []
        mixing = []
        for d in range(1, stride):
            block_states = packs[d][:, :dims, :]
            previous += [rims[d], block_states[0]]
            current += [block_states[0], block_states[1]]
            parents.append(packs[d][:, dims, :])
            observed.append(packs[d][:, dims + 1, :tracers])
            mixing.append(packs[d][:, dims + 1, tracers])
        weights_all = jax.vmap(transition, in_axes=(0, 0, 0, 0, 0, None, None))(
            jnp.stack(previous),
            jnp.stack(current),
            jnp.concatenate(parents).astype(jnp.int32),
            jnp.concatenate(observed),
            jnp.concatenate(mixing),
            fingerprints,
            tracer_scale,
        )
        products = lax.dot_general(
            weights_all[0::2],
            weights_all[1::2],
            (((2,), (1,)), ((0,), (0,))),
            precision=lax.Precision.HIGH,
            preferred_element_type=jnp.float32,
        )
        combined = block_product([products[d] for d in range(stride - 2, -1, -1)] + [block_own])
        return products, combined

    def skipped(bundle, other):
        return (
            jnp.zeros((stride - 1, count, count), jnp.float32),
            jnp.zeros((count, count), jnp.float32),
        )

    befores, combined = lax.cond(me > head, earlier, skipped, bundle, other)

    prior8 = jnp.broadcast_to(prior_weights[None, :], (8, count))
    weights = chain(weights_own, block_own, befores, combined, prior8, steps, stride, head)
    mine = lax.dynamic_slice_in_dim(weights[:local], row_start, own_rows, 1)
    return count * mine


def solution(mesh):
    return jax.shard_map(
        shards,
        mesh=mesh,
        in_specs=(P("tm", None, None), P("tm", None), P("tm", None), P("tm"), P(), P(), P()),
        out_specs=P("tm", "rows"),
        check_vma=False,
    )
```

```python
import functools

import jax
import jax.numpy as jnp
from jax import lax
from jax.experimental import pallas as pl
from jax.experimental.pallas import tpu as pltpu
from jax.sharding import PartitionSpec as P

MESH = pl.DeviceIdType.MESH
STRIDE = 3
HEAD = 13


def shifted(block, axis, distance):
    devices = range(lax.axis_size(axis))
    route = [(i - distance, i) for i in devices if i - distance in devices]
    return lax.ppermute(block, axis, route)


def transition(previous, current, parent_ids, observed, mixing, fingerprints, tracer_scale):
    count = current.shape[1]
    highest = lax.Precision.HIGHEST
    inner_prod = lax.dot_general(
        previous,
        current,
        (((0,), (0,)), ((), ())),
        precision=highest,
        preferred_element_type=jnp.float32,
    )
    distance = (
        jnp.sum(previous * previous, axis=0)[:, None]
        + jnp.sum(current * current, axis=0)[None, :]
        - 2.0 * inner_prod
    )
    kernel = jnp.exp(-2.0 * distance / current.shape[0])
    predicted = lax.dot_general(
        fingerprints,
        current,
        (((0,), (0,)), ((), ())),
        precision=highest,
        preferred_element_type=jnp.float32,
    )
    misfit = tracer_scale[:, None] * (observed[:, None] - predicted)
    likelihood = jnp.exp(-0.5 * jnp.sum(misfit * misfit, axis=0))
    likelihood = likelihood / jnp.max(likelihood)
    parent = (parent_ids[None, :] == jnp.arange(count, dtype=jnp.int32)[:, None]).astype(
        jnp.float32
    )
    return likelihood[None, :] * (parent + mixing * kernel)


def vec_mat(u_row, mat):
    n = mat.shape[0]
    u_col = jnp.transpose(jnp.broadcast_to(u_row[0:1, :], (128, n)))
    parts = []
    for g in range(n // 128):
        block = mat[:, g * 128:(g + 1) * 128]
        parts.append(jnp.sum(block * u_col, axis=0, keepdims=True))
    return jnp.concatenate(parts, axis=1)


def normalized(v):
    return v / jnp.sum(v)


def spread(v, like):
    return jnp.broadcast_to(v, like.shape)


def chain_kernel(steps, stride, head, *refs):
    weights_hbm, block_hbm, befores_hbm, combined_hbm, prior_ref = refs[:5]
    out_ref, recv_buf, send_buf, send_sem, recv_sem, load_sem = refs[5:11]
    local = refs[11:]
    me = lax.axis_index("tm")
    row = lax.axis_index("rows")
    last = steps - 1
    offset = me - head
    phase = jnp.maximum(offset, 0) % stride
    tail = me > head
    tail_node = jnp.logical_and(tail, phase == 0)
    fans = jnp.logical_or(me == head, tail_node)

    sources = [block_hbm, combined_hbm, weights_hbm.at[0], weights_hbm.at[1]]
    sources += [befores_hbm.at[d] for d in range(stride - 1)]
    loads = [
        pltpu.make_async_copy(sources[i], local[i], load_sem.at[i]) for i in range(len(sources))
    ]
    for load in loads:
        load.start()
    block_ref, combined_ref, first_ref, second_ref = local[:4]
    befores = local[4:]

    source_gap = jnp.where(me <= head, 1, jnp.where(phase == 0, stride, phase))
    sends = jnp.where(me < head, 1, jnp.where(fans, jnp.minimum(last - me, stride), 0))

    barrier = pltpu.get_barrier_semaphore()

    def greet(other):
        pl.semaphore_signal(barrier, 1, device_id=(other, row), device_id_type=MESH)

    @pl.when(me > 0)
    def _():
        greet(me - source_gap)

    for d in range(1, stride + 1):
        @pl.when(d <= sends)
        def _():
            greet(me + d)

    partners = sends + (me > 0).astype(jnp.int32)
    for amount in range(1, stride + 2):
        @pl.when(partners == amount)
        def _():
            pl.semaphore_wait(barrier, amount)

    def copy_to(d):
        return pltpu.make_async_remote_copy(
            src_ref=send_buf,
            dst_ref=recv_buf,
            send_sem=send_sem.at[d - 1],
            recv_sem=recv_sem,
            device_id=(jnp.minimum(me + d, last), row),
            device_id_type=MESH,
        )

    copies = [copy_to(d) for d in range(1, stride + 1)]

    def send_all(v):
        send_buf[...] = v
        for d in range(1, stride + 1):
            @pl.when(d <= sends)
            def _():
                copies[d - 1].start()

    loads[0].wait()
    loads[1].wait()

    @pl.when(me == 0)
    def _():
        out_ref[...] = spread(normalized(prior_ref[0:1, :]), out_ref)

    @pl.when(me > 0)
    def _():
        copies[0].wait_recv()
        out_ref[...] = spread(recv_buf[...], out_ref)

    @pl.when(me <= head)
    def _():
        send_all(normalized(vec_mat(out_ref[...], block_ref[...])))

    @pl.when(tail_node)
    def _():
        send_all(normalized(vec_mat(out_ref[...], combined_ref[...])))

    for load in loads[4:]:
        load.wait()
    lag = jnp.where(tail_node, stride - 1, jnp.where(tail, phase - 1, 0))
    for amount in range(1, stride):
        @pl.when(lag == amount)
        def _():
            u = out_ref[...]
            for d in range(amount, 0, -1):
                u = spread(normalized(vec_mat(u, befores[d - 1][...])), out_ref)
            out_ref[...] = u

    loads[2].wait()
    loads[3].wait()
    incoming = out_ref[...]
    w_first = normalized(vec_mat(incoming, first_ref[...]))
    w_second = normalized(vec_mat(spread(w_first, incoming), second_ref[...]))
    out_ref[...] = jnp.concatenate(
        [w_first, w_second, jnp.zeros((incoming.shape[0] - 2, incoming.shape[1]), jnp.float32)],
        axis=0,
    )

    for d in range(1, stride + 1):
        @pl.when(d <= sends)
        def _():
            copies[d - 1].wait_send()


def chain(weights_own, block, befores, combined, prior, steps, stride, head):
    count = combined.shape[0]
    loaded = stride + 3
    return pl.pallas_call(
        functools.partial(chain_kernel, steps, stride, head),
        out_shape=jax.ShapeDtypeStruct((8, count), jnp.float32),
        in_specs=[pl.BlockSpec(memory_space=pl.ANY)] * 4
        + [pl.BlockSpec(memory_space=pltpu.VMEM)],
        out_specs=pl.BlockSpec(memory_space=pltpu.VMEM),
        scratch_shapes=[
            pltpu.VMEM((1, count), jnp.float32),
            pltpu.VMEM((1, count), jnp.float32),
            pltpu.SemaphoreType.DMA((stride,)),
            pltpu.SemaphoreType.DMA,
            pltpu.SemaphoreType.DMA((loaded,)),
        ]
        + [pltpu.VMEM((count, count), jnp.float32) for _ in range(loaded)],
        compiler_params=pltpu.CompilerParams(
            collective_id=0, has_side_effects=True, vmem_limit_bytes=48 * 1024 * 1024
        ),
    )(weights_own, block, befores, combined, prior)


def block_product(matrices):
    block = matrices[0]
    for matrix in matrices[1:]:
        block = jnp.dot(
            block, matrix, precision=lax.Precision.HIGH, preferred_element_type=jnp.float32
        )
    return block


def shards(states, ancestors, tracer_obs, jitter, fingerprints, tracer_scale, prior_weights):
    count = states.shape[2]
    own_rows = count // lax.axis_size("rows")
    row_start = lax.axis_index("rows") * own_rows
    steps = lax.axis_size("tm")
    stride = STRIDE
    head = min(HEAD, steps - 1)
    local = states.shape[0]
    dims = states.shape[1]
    tracers = tracer_obs.shape[1]
    me = lax.axis_index("tm")

    count_pad = jnp.zeros((local, count - tracers - 1), jnp.float32)
    extra = jnp.concatenate(
        [
            ancestors.astype(jnp.float32)[:, None, :],
            jnp.concatenate([tracer_obs, jitter[:, None], count_pad], axis=1)[:, None, :],
            jnp.zeros((local, 6, count), jnp.float32),
        ],
        axis=1,
    )
    packed = jnp.concatenate([states, extra], axis=1)

    def need(k):
        if k <= head:
            return 0
        phase = (k - head) % stride
        return stride - 1 if phase == 0 else phase - 1

    devices = range(steps)

    def sent(block, distance, wanted):
        route = [(i - distance, i) for i in devices if i - distance >= 0 and wanted(i)]
        return lax.ppermute(block, "tm", route)

    rim_own = sent(states[-1], 1, lambda i: True)

    core = lax.axis_index("rows") % 2
    half_rows = dims // 2
    packed_half = lax.dynamic_index_in_dim(packed, core, 0, keepdims=False)
    rim_half = lax.dynamic_slice_in_dim(states[-1], core * half_rows, half_rows, 0)
    fetched = [sent(packed_half, d, lambda i, d=d: need(i) >= d) for d in range(1, stride)]
    fetched += [sent(rim_half, e, lambda i, e=e: need(i) + 1 == e) for e in range(2, stride + 1)]
    bundle = jnp.concatenate(fetched, axis=0)
    pairs = [(r, r ^ 1) for r in range(lax.axis_size("rows"))]
    other = lax.ppermute(bundle, "rows", pairs)

    def batched(previous, current, parents, observed, mixing):
        return jax.vmap(transition, in_axes=(0, 0, 0, 0, 0, None, None))(
            jnp.stack(previous),
            jnp.stack(current),
            jnp.concatenate(parents).astype(jnp.int32),
            jnp.concatenate(observed),
            jnp.concatenate(mixing),
            fingerprints,
            tracer_scale,
        )

    def earlier(bundle, other, rim_own):
        first_half = jnp.where(core == 0, bundle, other)
        second_half = jnp.where(core == 0, other, bundle)
        rows_of = [f.shape[0] for f in fetched]
        offsets = [sum(rows_of[:i]) for i in range(len(rows_of) + 1)]

        def joined(i):
            lo, hi = offsets[i], offsets[i + 1]
            return jnp.concatenate([first_half[lo:hi], second_half[lo:hi]], axis=0)

        packs = [packed] + [joined(i).reshape(packed.shape) for i in range(stride - 1)]
        rim_parts = [joined(stride - 1 + i) for i in range(stride - 1)]
        rims = [rim_own] + [
            (packs[d + 1][-1, :dims, :] if d + 1 < stride else 0.0) + rim_parts[d - 1]
            for d in range(1, stride)
        ]
        previous = []
        current = []
        parents = []
        observed = []
        mixing = []
        for d in range(stride):
            block_states = packs[d][:, :dims, :]
            previous += [rims[d], block_states[0]]
            current += [block_states[0], block_states[1]]
            parents.append(packs[d][:, dims, :])
            observed.append(packs[d][:, dims + 1, :tracers])
            mixing.append(packs[d][:, dims + 1, tracers])
        weights_all = batched(previous, current, parents, observed, mixing)
        products = lax.dot_general(
            weights_all[0::2],
            weights_all[1::2],
            (((2,), (1,)), ((0,), (0,))),
            precision=lax.Precision.HIGH,
            preferred_element_type=jnp.float32,
        )
        combined = block_product([products[d] for d in range(stride - 1, -1, -1)])
        return weights_all[0:2], products[0], products[1:], combined

    def own_only(bundle, other, rim_own):
        weights_own = batched(
            [rim_own, states[0]],
            [states[0], states[1]],
            [ancestors],
            [tracer_obs],
            [jitter],
        )
        return (
            weights_own,
            block_product([weights_own[0], weights_own[1]]),
            jnp.zeros((stride - 1, count, count), jnp.float32),
            jnp.zeros((count, count), jnp.float32),
        )

    weights_own, block_own, befores, combined = lax.cond(
        me > head, earlier, own_only, bundle, other, rim_own
    )

    prior8 = jnp.broadcast_to(prior_weights[None, :], (8, count))
    weights = chain(weights_own, block_own, befores, combined, prior8, steps, stride, head)
    mine = lax.dynamic_slice_in_dim(weights[:local], row_start, own_rows, 1)
    return count * mine


def solution(mesh):
    return jax.shard_map(
        shards,
        mesh=mesh,
        in_specs=(P("tm", None, None), P("tm", None), P("tm", None), P("tm"), P(), P(), P()),
        out_specs=P("tm", "rows"),
        check_vma=False,
    )
```

```python
import functools

import jax
import jax.numpy as jnp
from jax import lax
from jax.experimental import pallas as pl
from jax.experimental.pallas import tpu as pltpu
from jax.sharding import PartitionSpec as P

MESH = pl.DeviceIdType.MESH
STRIDE = 3
HEAD = 12


def shifted(block, axis, distance):
    devices = range(lax.axis_size(axis))
    route = [(i - distance, i) for i in devices if i - distance in devices]
    return lax.ppermute(block, axis, route)


def transition(previous, current, parent_ids, observed, mixing, fingerprints, tracer_scale):
    count = current.shape[1]
    highest = lax.Precision.HIGHEST
    inner_prod = lax.dot_general(
        previous,
        current,
        (((0,), (0,)), ((), ())),
        precision=highest,
        preferred_element_type=jnp.float32,
    )
    distance = (
        jnp.sum(previous * previous, axis=0)[:, None]
        + jnp.sum(current * current, axis=0)[None, :]
        - 2.0 * inner_prod
    )
    kernel = jnp.exp(-2.0 * distance / current.shape[0])
    predicted = lax.dot_general(
        fingerprints,
        current,
        (((0,), (0,)), ((), ())),
        precision=highest,
        preferred_element_type=jnp.float32,
    )
    misfit = tracer_scale[:, None] * (observed[:, None] - predicted)
    likelihood = jnp.exp(-0.5 * jnp.sum(misfit * misfit, axis=0))
    likelihood = likelihood / jnp.max(likelihood)
    parent = (parent_ids[None, :] == jnp.arange(count, dtype=jnp.int32)[:, None]).astype(
        jnp.float32
    )
    return likelihood[None, :] * (parent + mixing * kernel)


def vec_mat(u_row, mat):
    n = mat.shape[0]
    u_col = jnp.transpose(jnp.broadcast_to(u_row[0:1, :], (128, n)))
    parts = []
    for g in range(n // 128):
        block = mat[:, g * 128:(g + 1) * 128]
        parts.append(jnp.sum(block * u_col, axis=0, keepdims=True))
    return jnp.concatenate(parts, axis=1)


def normalized(v):
    return v / jnp.sum(v)


def spread(v, like):
    return jnp.broadcast_to(v, like.shape)


def chain_kernel(steps, stride, head, *refs):
    weights_hbm, block_hbm, befores_hbm, combined_hbm, prior_ref = refs[:5]
    out_ref, recv_buf, send_buf, send_sem, recv_sem, load_sem = refs[5:11]
    local = refs[11:]
    me = lax.axis_index("tm")
    row = lax.axis_index("rows")
    last = steps - 1
    offset = me - head
    phase = jnp.maximum(offset, 0) % stride
    tail = me > head
    tail_node = jnp.logical_and(tail, phase == 0)
    fans = jnp.logical_or(me == head, tail_node)

    sources = [block_hbm, combined_hbm, weights_hbm.at[0], weights_hbm.at[1]]
    sources += [befores_hbm.at[d] for d in range(stride - 1)]
    loads = [
        pltpu.make_async_copy(sources[i], local[i], load_sem.at[i]) for i in range(len(sources))
    ]
    for load in loads:
        load.start()
    block_ref, combined_ref, first_ref, second_ref = local[:4]
    befores = local[4:]

    source_gap = jnp.where(me <= head, 1, jnp.where(phase == 0, stride, phase))
    sends = jnp.where(me < head, 1, jnp.where(fans, jnp.minimum(last - me, stride), 0))

    barrier = pltpu.get_barrier_semaphore()

    def greet(other):
        pl.semaphore_signal(barrier, 1, device_id=(other, row), device_id_type=MESH)

    @pl.when(me > 0)
    def _():
        greet(me - source_gap)

    for d in range(1, stride + 1):
        @pl.when(d <= sends)
        def _():
            greet(me + d)

    partners = sends + (me > 0).astype(jnp.int32)
    for amount in range(1, stride + 2):
        @pl.when(partners == amount)
        def _():
            pl.semaphore_wait(barrier, amount)

    def copy_to(d):
        return pltpu.make_async_remote_copy(
            src_ref=send_buf,
            dst_ref=recv_buf,
            send_sem=send_sem.at[d - 1],
            recv_sem=recv_sem,
            device_id=(jnp.minimum(me + d, last), row),
            device_id_type=MESH,
        )

    copies = [copy_to(d) for d in range(1, stride + 1)]

    def send_all(v):
        send_buf[...] = v
        for d in range(1, stride + 1):
            @pl.when(d <= sends)
            def _():
                copies[d - 1].start()

    loads[0].wait()
    loads[1].wait()

    @pl.when(me == 0)
    def _():
        out_ref[...] = spread(normalized(prior_ref[0:1, :]), out_ref)

    @pl.when(me > 0)
    def _():
        copies[0].wait_recv()
        out_ref[...] = spread(recv_buf[...], out_ref)

    @pl.when(me <= head)
    def _():
        send_all(normalized(vec_mat(out_ref[...], block_ref[...])))

    @pl.when(tail_node)
    def _():
        send_all(normalized(vec_mat(out_ref[...], combined_ref[...])))

    for load in loads[4:]:
        load.wait()
    lag = jnp.where(tail_node, stride - 1, jnp.where(tail, phase - 1, 0))
    for amount in range(1, stride):
        @pl.when(lag == amount)
        def _():
            u = out_ref[...]
            for d in range(amount, 0, -1):
                u = spread(normalized(vec_mat(u, befores[d - 1][...])), out_ref)
            out_ref[...] = u

    loads[2].wait()
    loads[3].wait()
    incoming = out_ref[...]
    w_first = normalized(vec_mat(incoming, first_ref[...]))
    w_second = normalized(vec_mat(spread(w_first, incoming), second_ref[...]))
    out_ref[...] = jnp.concatenate(
        [w_first, w_second, jnp.zeros((incoming.shape[0] - 2, incoming.shape[1]), jnp.float32)],
        axis=0,
    )

    for d in range(1, stride + 1):
        @pl.when(d <= sends)
        def _():
            copies[d - 1].wait_send()


def chain(weights_own, block, befores, combined, prior, steps, stride, head):
    count = combined.shape[0]
    loaded = stride + 3
    return pl.pallas_call(
        functools.partial(chain_kernel, steps, stride, head),
        out_shape=jax.ShapeDtypeStruct((8, count), jnp.float32),
        in_specs=[pl.BlockSpec(memory_space=pl.ANY)] * 4
        + [pl.BlockSpec(memory_space=pltpu.VMEM)],
        out_specs=pl.BlockSpec(memory_space=pltpu.VMEM),
        scratch_shapes=[
            pltpu.VMEM((1, count), jnp.float32),
            pltpu.VMEM((1, count), jnp.float32),
            pltpu.SemaphoreType.DMA((stride,)),
            pltpu.SemaphoreType.DMA,
            pltpu.SemaphoreType.DMA((loaded,)),
        ]
        + [pltpu.VMEM((count, count), jnp.float32) for _ in range(loaded)],
        compiler_params=pltpu.CompilerParams(
            collective_id=0, has_side_effects=True, vmem_limit_bytes=48 * 1024 * 1024
        ),
    )(weights_own, block, befores, combined, prior)


def block_product(matrices):
    block = matrices[0]
    for matrix in matrices[1:]:
        block = jnp.dot(
            block, matrix, precision=lax.Precision.HIGH, preferred_element_type=jnp.float32
        )
    return block


def shards(states, ancestors, tracer_obs, jitter, fingerprints, tracer_scale, prior_weights):
    count = states.shape[2]
    own_rows = count // lax.axis_size("rows")
    row_start = lax.axis_index("rows") * own_rows
    steps = lax.axis_size("tm")
    stride = STRIDE
    head = min(HEAD, steps - 1)
    local = states.shape[0]
    dims = states.shape[1]
    tracers = tracer_obs.shape[1]
    me = lax.axis_index("tm")

    count_pad = jnp.zeros((local, count - tracers - 1), jnp.float32)
    extra = jnp.concatenate(
        [
            ancestors.astype(jnp.float32)[:, None, :],
            jnp.concatenate([tracer_obs, jitter[:, None], count_pad], axis=1)[:, None, :],
            jnp.zeros((local, 6, count), jnp.float32),
        ],
        axis=1,
    )
    packed = jnp.concatenate([states, extra], axis=1)

    def need(k):
        if k <= head:
            return 0
        phase = (k - head) % stride
        return stride - 1 if phase == 0 else phase - 1

    devices = range(steps)

    def sent(block, distance, wanted):
        route = [(i - distance, i) for i in devices if i - distance >= 0 and wanted(i)]
        return lax.ppermute(block, "tm", route)

    rim_own = sent(states[-1], 1, lambda i: True)

    core = lax.axis_index("rows") % 2
    half_rows = dims // 2
    packed_half = lax.dynamic_index_in_dim(packed, core, 0, keepdims=False)
    rim_half = lax.dynamic_slice_in_dim(states[-1], core * half_rows, half_rows, 0)
    fetched = [sent(packed_half, d, lambda i, d=d: need(i) >= d) for d in range(1, stride)]
    fetched += [sent(rim_half, e, lambda i, e=e: need(i) + 1 == e) for e in range(2, stride + 1)]
    bundle = jnp.concatenate(fetched, axis=0)
    pairs = [(r, r ^ 1) for r in range(lax.axis_size("rows"))]
    other = lax.ppermute(bundle, "rows", pairs)

    def own_matrices():
        return jax.vmap(transition, in_axes=(0, 0, 0, 0, 0, None, None))(
            jnp.stack([rim_own, states[0]]),
            states,
            ancestors,
            tracer_obs,
            jitter,
            fingerprints,
            tracer_scale,
        )

    weights_own = own_matrices()
    block_own = block_product([weights_own[0], weights_own[1]])

    def earlier(bundle, other):
        first_half = jnp.where(core == 0, bundle, other)
        second_half = jnp.where(core == 0, other, bundle)
        rows_of = [f.shape[0] for f in fetched]
        offsets = [sum(rows_of[:i]) for i in range(len(rows_of) + 1)]

        def joined(i):
            lo, hi = offsets[i], offsets[i + 1]
            return jnp.concatenate([first_half[lo:hi], second_half[lo:hi]], axis=0)

        packs = [packed] + [joined(i).reshape(packed.shape) for i in range(stride - 1)]
        rim_parts = [joined(stride - 1 + i) for i in range(stride - 1)]
        rims = [None] + [
            (packs[d + 1][-1, :dims, :] if d + 1 < stride else 0.0) + rim_parts[d - 1]
            for d in range(1, stride)
        ]
        previous = []
        current = []
        parents = []
        observed = []
        mixing = []
        for d in range(1, stride):
            block_states = packs[d][:, :dims, :]
            previous += [rims[d], block_states[0]]
            current += [block_states[0], block_states[1]]
            parents.append(packs[d][:, dims, :])
            observed.append(packs[d][:, dims + 1, :tracers])
            mixing.append(packs[d][:, dims + 1, tracers])
        weights_all = jax.vmap(transition, in_axes=(0, 0, 0, 0, 0, None, None))(
            jnp.stack(previous),
            jnp.stack(current),
            jnp.concatenate(parents).astype(jnp.int32),
            jnp.concatenate(observed),
            jnp.concatenate(mixing),
            fingerprints,
            tracer_scale,
        )
        products = lax.dot_general(
            weights_all[0::2],
            weights_all[1::2],
            (((2,), (1,)), ((0,), (0,))),
            precision=lax.Precision.HIGH,
            preferred_element_type=jnp.float32,
        )
        combined = block_product([products[d] for d in range(stride - 2, -1, -1)] + [block_own])
        return products, combined

    def skipped(bundle, other):
        return (
            jnp.zeros((stride - 1, count, count), jnp.float32),
            jnp.zeros((count, count), jnp.float32),
        )

    befores, combined = lax.cond(me > head, earlier, skipped, bundle, other)

    prior8 = jnp.broadcast_to(prior_weights[None, :], (8, count))
    weights = chain(weights_own, block_own, befores, combined, prior8, steps, stride, head)
    mine = lax.dynamic_slice_in_dim(weights[:local], row_start, own_rows, 1)
    return count * mine


def solution(mesh):
    return jax.shard_map(
        shards,
        mesh=mesh,
        in_specs=(P("tm", None, None), P("tm", None), P("tm", None), P("tm"), P(), P(), P()),
        out_specs=P("tm", "rows"),
        check_vma=False,
    )
```

```python
import functools

import jax
import jax.numpy as jnp
from jax import lax
from jax.experimental import pallas as pl
from jax.experimental.pallas import tpu as pltpu
from jax.sharding import PartitionSpec as P

MESH = pl.DeviceIdType.MESH
STRIDE = 3
HEAD = 12


def shifted(block, axis, distance):
    devices = range(lax.axis_size(axis))
    route = [(i - distance, i) for i in devices if i - distance in devices]
    return lax.ppermute(block, axis, route)


def transition(previous, current, parent_ids, observed, mixing, fingerprints, tracer_scale):
    count = current.shape[1]
    highest = lax.Precision.HIGHEST
    inner_prod = lax.dot_general(
        previous,
        current,
        (((0,), (0,)), ((), ())),
        precision=highest,
        preferred_element_type=jnp.float32,
    )
    distance = (
        jnp.sum(previous * previous, axis=0)[:, None]
        + jnp.sum(current * current, axis=0)[None, :]
        - 2.0 * inner_prod
    )
    kernel = jnp.exp(-2.0 * distance / current.shape[0])
    predicted = lax.dot_general(
        fingerprints,
        current,
        (((0,), (0,)), ((), ())),
        precision=highest,
        preferred_element_type=jnp.float32,
    )
    misfit = tracer_scale[:, None] * (observed[:, None] - predicted)
    likelihood = jnp.exp(-0.5 * jnp.sum(misfit * misfit, axis=0))
    likelihood = likelihood / jnp.max(likelihood)
    parent = (parent_ids[None, :] == jnp.arange(count, dtype=jnp.int32)[:, None]).astype(
        jnp.float32
    )
    return likelihood[None, :] * (parent + mixing * kernel)


def vec_mat(u_row, mat):
    n = mat.shape[0]
    u_col = jnp.transpose(jnp.broadcast_to(u_row[0:1, :], (128, n)))
    parts = []
    for g in range(n // 128):
        block = mat[:, g * 128:(g + 1) * 128]
        parts.append(jnp.sum(block * u_col, axis=0, keepdims=True))
    return jnp.concatenate(parts, axis=1)


def normalized(v):
    return v / jnp.sum(v)


def spread(v, like):
    return jnp.broadcast_to(v, like.shape)


def chain_kernel(steps, stride, head, *refs):
    weights_hbm, block_hbm, befores_hbm, combined_hbm, prior_ref = refs[:5]
    out_ref, recv_buf, send_buf, send_sem, recv_sem, load_sem = refs[5:11]
    local = refs[11:]
    me = lax.axis_index("tm")
    row = lax.axis_index("rows")
    last = steps - 1
    offset = me - head
    phase = jnp.maximum(offset, 0) % stride
    tail = me > head
    tail_node = jnp.logical_and(tail, phase == 0)
    fans = jnp.logical_or(me == head, tail_node)

    sources = [block_hbm, combined_hbm, weights_hbm.at[0], weights_hbm.at[1]]
    sources += [befores_hbm.at[d] for d in range(stride - 1)]
    loads = [
        pltpu.make_async_copy(sources[i], local[i], load_sem.at[i]) for i in range(len(sources))
    ]
    for load in loads:
        load.start()
    block_ref, combined_ref, first_ref, second_ref = local[:4]
    befores = local[4:]

    source_gap = jnp.where(me <= head, 1, jnp.where(phase == 0, stride, phase))
    sends = jnp.where(me < head, 1, jnp.where(fans, jnp.minimum(last - me, stride), 0))

    barrier = pltpu.get_barrier_semaphore()

    def greet(other):
        pl.semaphore_signal(barrier, 1, device_id=(other, row), device_id_type=MESH)

    @pl.when(me > 0)
    def _():
        greet(me - source_gap)

    for d in range(1, stride + 1):
        @pl.when(d <= sends)
        def _():
            greet(me + d)

    partners = sends + (me > 0).astype(jnp.int32)
    for amount in range(1, stride + 2):
        @pl.when(partners == amount)
        def _():
            pl.semaphore_wait(barrier, amount)

    def copy_to(d):
        return pltpu.make_async_remote_copy(
            src_ref=send_buf,
            dst_ref=recv_buf,
            send_sem=send_sem.at[d - 1],
            recv_sem=recv_sem,
            device_id=(jnp.minimum(me + d, last), row),
            device_id_type=MESH,
        )

    copies = [copy_to(d) for d in range(1, stride + 1)]

    def send_all(v):
        send_buf[...] = v
        for d in range(1, stride + 1):
            @pl.when(d <= sends)
            def _():
                copies[d - 1].start()

    loads[0].wait()

    @pl.when(tail_node)
    def _():
        loads[1].wait()

    @pl.when(me == 0)
    def _():
        out_ref[...] = spread(normalized(prior_ref[0:1, :]), out_ref)

    @pl.when(me > 0)
    def _():
        copies[0].wait_recv()
        out_ref[...] = spread(recv_buf[...], out_ref)

    @pl.when(me <= head)
    def _():
        send_all(normalized(vec_mat(out_ref[...], block_ref[...])))

    @pl.when(tail_node)
    def _():
        send_all(normalized(vec_mat(out_ref[...], combined_ref[...])))

    @pl.when(jnp.logical_not(tail_node))
    def _():
        loads[1].wait()

    for load in loads[4:]:
        load.wait()
    lag = jnp.where(tail_node, stride - 1, jnp.where(tail, phase - 1, 0))
    for amount in range(1, stride):
        @pl.when(lag == amount)
        def _():
            u = out_ref[...]
            for d in range(amount, 0, -1):
                u = spread(normalized(vec_mat(u, befores[d - 1][...])), out_ref)
            out_ref[...] = u

    loads[2].wait()
    loads[3].wait()
    incoming = out_ref[...]
    w_first = normalized(vec_mat(incoming, first_ref[...]))
    w_second = normalized(vec_mat(spread(w_first, incoming), second_ref[...]))
    out_ref[...] = jnp.concatenate(
        [w_first, w_second, jnp.zeros((incoming.shape[0] - 2, incoming.shape[1]), jnp.float32)],
        axis=0,
    )

    for d in range(1, stride + 1):
        @pl.when(d <= sends)
        def _():
            copies[d - 1].wait_send()


def chain(weights_own, block, befores, combined, prior, steps, stride, head):
    count = combined.shape[0]
    loaded = stride + 3
    return pl.pallas_call(
        functools.partial(chain_kernel, steps, stride, head),
        out_shape=jax.ShapeDtypeStruct((8, count), jnp.float32),
        in_specs=[pl.BlockSpec(memory_space=pl.ANY)] * 4
        + [pl.BlockSpec(memory_space=pltpu.VMEM)],
        out_specs=pl.BlockSpec(memory_space=pltpu.VMEM),
        scratch_shapes=[
            pltpu.VMEM((1, count), jnp.float32),
            pltpu.VMEM((1, count), jnp.float32),
            pltpu.SemaphoreType.DMA((stride,)),
            pltpu.SemaphoreType.DMA,
            pltpu.SemaphoreType.DMA((loaded,)),
        ]
        + [pltpu.VMEM((count, count), jnp.float32) for _ in range(loaded)],
        compiler_params=pltpu.CompilerParams(
            collective_id=0, has_side_effects=True, vmem_limit_bytes=48 * 1024 * 1024
        ),
    )(weights_own, block, befores, combined, prior)


def block_product(matrices):
    block = matrices[0]
    for matrix in matrices[1:]:
        block = jnp.dot(
            block, matrix, precision=lax.Precision.HIGH, preferred_element_type=jnp.float32
        )
    return block


def shards(states, ancestors, tracer_obs, jitter, fingerprints, tracer_scale, prior_weights):
    count = states.shape[2]
    own_rows = count // lax.axis_size("rows")
    row_start = lax.axis_index("rows") * own_rows
    steps = lax.axis_size("tm")
    stride = STRIDE
    head = min(HEAD, steps - 1)
    local = states.shape[0]
    dims = states.shape[1]
    tracers = tracer_obs.shape[1]
    me = lax.axis_index("tm")

    count_pad = jnp.zeros((local, count - tracers - 1), jnp.float32)
    extra = jnp.concatenate(
        [
            ancestors.astype(jnp.float32)[:, None, :],
            jnp.concatenate([tracer_obs, jitter[:, None], count_pad], axis=1)[:, None, :],
            jnp.zeros((local, 6, count), jnp.float32),
        ],
        axis=1,
    )
    packed = jnp.concatenate([states, extra], axis=1)

    def need(k):
        if k <= head:
            return 0
        phase = (k - head) % stride
        return stride - 1 if phase == 0 else phase - 1

    devices = range(steps)

    def sent(block, distance, wanted):
        route = [(i - distance, i) for i in devices if i - distance >= 0 and wanted(i)]
        return lax.ppermute(block, "tm", route)

    rim_own = sent(states[-1], 1, lambda i: True)

    core = lax.axis_index("rows") % 2
    half_rows = dims // 2
    packed_half = lax.dynamic_index_in_dim(packed, core, 0, keepdims=False)
    rim_half = lax.dynamic_slice_in_dim(states[-1], core * half_rows, half_rows, 0)
    fetched = [sent(packed_half, d, lambda i, d=d: need(i) >= d) for d in range(1, stride)]
    fetched += [sent(rim_half, e, lambda i, e=e: need(i) + 1 == e) for e in range(2, stride + 1)]
    bundle = jnp.concatenate(fetched, axis=0)
    pairs = [(r, r ^ 1) for r in range(lax.axis_size("rows"))]

    def own_matrices():
        return jax.vmap(transition, in_axes=(0, 0, 0, 0, 0, None, None))(
            jnp.stack([rim_own, states[0]]),
            states,
            ancestors,
            tracer_obs,
            jitter,
            fingerprints,
            tracer_scale,
        )

    weights_own = own_matrices()
    block_own = block_product([weights_own[0], weights_own[1]])

    def earlier(bundle):
        other = lax.ppermute(bundle, "rows", pairs)
        first_half = jnp.where(core == 0, bundle, other)
        second_half = jnp.where(core == 0, other, bundle)
        rows_of = [f.shape[0] for f in fetched]
        offsets = [sum(rows_of[:i]) for i in range(len(rows_of) + 1)]

        def joined(i):
            lo, hi = offsets[i], offsets[i + 1]
            return jnp.concatenate([first_half[lo:hi], second_half[lo:hi]], axis=0)

        packs = [packed] + [joined(i).reshape(packed.shape) for i in range(stride - 1)]
        rim_parts = [joined(stride - 1 + i) for i in range(stride - 1)]
        rims = [None] + [
            (packs[d + 1][-1, :dims, :] if d + 1 < stride else 0.0) + rim_parts[d - 1]
            for d in range(1, stride)
        ]
        previous = []
        current = []
        parents = []
        observed = []
        mixing = []
        for d in range(1, stride):
            block_states = packs[d][:, :dims, :]
            previous += [rims[d], block_states[0]]
            current += [block_states[0], block_states[1]]
            parents.append(packs[d][:, dims, :])
            observed.append(packs[d][:, dims + 1, :tracers])
            mixing.append(packs[d][:, dims + 1, tracers])
        weights_all = jax.vmap(transition, in_axes=(0, 0, 0, 0, 0, None, None))(
            jnp.stack(previous),
            jnp.stack(current),
            jnp.concatenate(parents).astype(jnp.int32),
            jnp.concatenate(observed),
            jnp.concatenate(mixing),
            fingerprints,
            tracer_scale,
        )
        products = lax.dot_general(
            weights_all[0::2],
            weights_all[1::2],
            (((2,), (1,)), ((0,), (0,))),
            precision=lax.Precision.HIGH,
            preferred_element_type=jnp.float32,
        )
        combined = block_product([products[d] for d in range(stride - 2, -1, -1)] + [block_own])
        return products, combined

    def skipped(bundle):
        return (
            jnp.zeros((stride - 1, count, count), jnp.float32),
            jnp.zeros((count, count), jnp.float32),
        )

    befores, combined = lax.cond(me > head, earlier, skipped, bundle)

    prior8 = jnp.broadcast_to(prior_weights[None, :], (8, count))
    weights = chain(weights_own, block_own, befores, combined, prior8, steps, stride, head)
    mine = lax.dynamic_slice_in_dim(weights[:local], row_start, own_rows, 1)
    return count * mine


def solution(mesh):
    return jax.shard_map(
        shards,
        mesh=mesh,
        in_specs=(P("tm", None, None), P("tm", None), P("tm", None), P("tm"), P(), P(), P()),
        out_specs=P("tm", "rows"),
        check_vma=False,
    )
```

```python
import functools

import jax
import jax.numpy as jnp
from jax import lax
from jax.experimental import pallas as pl
from jax.experimental.pallas import tpu as pltpu
from jax.sharding import PartitionSpec as P

MESH = pl.DeviceIdType.MESH
STRIDE = 3
HEAD = 12


def shifted(block, axis, distance):
    devices = range(lax.axis_size(axis))
    route = [(i - distance, i) for i in devices if i - distance in devices]
    return lax.ppermute(block, axis, route)


def transition(previous, current, parent_ids, observed, mixing, fingerprints, tracer_scale):
    count = current.shape[1]
    highest = lax.Precision.HIGHEST
    inner_prod = lax.dot_general(
        previous,
        current,
        (((0,), (0,)), ((), ())),
        precision=highest,
        preferred_element_type=jnp.float32,
    )
    distance = (
        jnp.sum(previous * previous, axis=0)[:, None]
        + jnp.sum(current * current, axis=0)[None, :]
        - 2.0 * inner_prod
    )
    kernel = jnp.exp(-2.0 * distance / current.shape[0])
    predicted = lax.dot_general(
        fingerprints,
        current,
        (((0,), (0,)), ((), ())),
        precision=highest,
        preferred_element_type=jnp.float32,
    )
    misfit = tracer_scale[:, None] * (observed[:, None] - predicted)
    likelihood = jnp.exp(-0.5 * jnp.sum(misfit * misfit, axis=0))
    likelihood = likelihood / jnp.max(likelihood)
    parent = (parent_ids[None, :] == jnp.arange(count, dtype=jnp.int32)[:, None]).astype(
        jnp.float32
    )
    return likelihood[None, :] * (parent + mixing * kernel)


def vec_mat(u_row, mat):
    n = mat.shape[0]
    u_col = jnp.transpose(jnp.broadcast_to(u_row[0:1, :], (128, n)))
    parts = []
    for g in range(n // 128):
        block = mat[:, g * 128:(g + 1) * 128]
        parts.append(jnp.sum(block * u_col, axis=0, keepdims=True))
    return jnp.concatenate(parts, axis=1)


def normalized(v):
    return v / jnp.sum(v)


def spread(v, like):
    return jnp.broadcast_to(v, like.shape)


def chain_kernel(steps, stride, head, *refs):
    weights_hbm, block_hbm, befores_hbm, combined_hbm, prior_ref = refs[:5]
    out_ref, recv_buf, send_buf, send_sem, recv_sem, load_sem = refs[5:11]
    local = refs[11:]
    me = lax.axis_index("tm")
    row = lax.axis_index("rows")
    last = steps - 1
    offset = me - head
    phase = jnp.maximum(offset, 0) % stride
    tail = me > head
    tail_node = jnp.logical_and(tail, phase == 0)
    fans = jnp.logical_or(me == head, tail_node)

    sources = [block_hbm, combined_hbm, weights_hbm.at[0], weights_hbm.at[1]]
    sources += [befores_hbm.at[d] for d in range(stride - 1)]
    loads = [
        pltpu.make_async_copy(sources[i], local[i], load_sem.at[i]) for i in range(len(sources))
    ]
    for load in loads:
        load.start()
    block_ref, combined_ref, first_ref, second_ref = local[:4]
    befores = local[4:]

    source_gap = jnp.where(me <= head, 1, jnp.where(phase == 0, stride, phase))
    sends = jnp.where(me < head, 1, jnp.where(fans, jnp.minimum(last - me, stride), 0))

    barrier = pltpu.get_barrier_semaphore()

    def greet(other):
        pl.semaphore_signal(barrier, 1, device_id=(other, row), device_id_type=MESH)

    @pl.when(me > 0)
    def _():
        greet(me - source_gap)

    for d in range(1, stride + 1):
        @pl.when(d <= sends)
        def _():
            greet(me + d)

    partners = sends + (me > 0).astype(jnp.int32)
    for amount in range(1, stride + 2):
        @pl.when(partners == amount)
        def _():
            pl.semaphore_wait(barrier, amount)

    def copy_to(d):
        return pltpu.make_async_remote_copy(
            src_ref=send_buf,
            dst_ref=recv_buf,
            send_sem=send_sem.at[d - 1],
            recv_sem=recv_sem,
            device_id=(jnp.minimum(me + d, last), row),
            device_id_type=MESH,
        )

    copies = [copy_to(d) for d in range(1, stride + 1)]

    def send_all(v):
        send_buf[...] = v
        for d in range(1, stride + 1):
            @pl.when(d <= sends)
            def _():
                copies[d - 1].start()

    loads[0].wait()
    loads[1].wait()

    @pl.when(me == 0)
    def _():
        out_ref[...] = spread(normalized(prior_ref[0:1, :]), out_ref)

    @pl.when(me > 0)
    def _():
        copies[0].wait_recv()
        out_ref[...] = spread(recv_buf[...], out_ref)

    @pl.when(me <= head)
    def _():
        send_all(normalized(vec_mat(out_ref[...], block_ref[...])))

    @pl.when(tail_node)
    def _():
        send_all(normalized(vec_mat(out_ref[...], combined_ref[...])))

    for load in loads[4:]:
        load.wait()
    lag = jnp.where(tail_node, stride - 1, jnp.where(tail, phase - 1, 0))
    for amount in range(1, stride):
        @pl.when(lag == amount)
        def _():
            u = out_ref[...]
            for d in range(amount, 0, -1):
                u = spread(normalized(vec_mat(u, befores[d - 1][...])), out_ref)
            out_ref[...] = u

    loads[2].wait()
    loads[3].wait()
    incoming = out_ref[...]
    w_first = normalized(vec_mat(incoming, first_ref[...]))
    w_second = normalized(vec_mat(spread(w_first, incoming), second_ref[...]))
    out_ref[...] = jnp.concatenate(
        [w_first, w_second, jnp.zeros((incoming.shape[0] - 2, incoming.shape[1]), jnp.float32)],
        axis=0,
    )

    for d in range(1, stride + 1):
        @pl.when(d <= sends)
        def _():
            copies[d - 1].wait_send()


def chain(weights_own, block, befores, combined, prior, steps, stride, head):
    count = combined.shape[0]
    loaded = stride + 3
    return pl.pallas_call(
        functools.partial(chain_kernel, steps, stride, head),
        out_shape=jax.ShapeDtypeStruct((8, count), jnp.float32),
        in_specs=[pl.BlockSpec(memory_space=pl.ANY)] * 4
        + [pl.BlockSpec(memory_space=pltpu.VMEM)],
        out_specs=pl.BlockSpec(memory_space=pltpu.VMEM),
        scratch_shapes=[
            pltpu.VMEM((1, count), jnp.float32),
            pltpu.VMEM((1, count), jnp.float32),
            pltpu.SemaphoreType.DMA((stride,)),
            pltpu.SemaphoreType.DMA,
            pltpu.SemaphoreType.DMA((loaded,)),
        ]
        + [pltpu.VMEM((count, count), jnp.float32) for _ in range(loaded)],
        compiler_params=pltpu.CompilerParams(
            collective_id=0, has_side_effects=True, vmem_limit_bytes=48 * 1024 * 1024
        ),
    )(weights_own, block, befores, combined, prior)


def block_product(matrices):
    block = matrices[0]
    for matrix in matrices[1:]:
        block = jnp.dot(
            block, matrix, precision=lax.Precision.HIGH, preferred_element_type=jnp.float32
        )
    return block


def shards(states, ancestors, tracer_obs, jitter, fingerprints, tracer_scale, prior_weights):
    count = states.shape[2]
    own_rows = count // lax.axis_size("rows")
    row_start = lax.axis_index("rows") * own_rows
    steps = lax.axis_size("tm")
    stride = STRIDE
    head = min(HEAD, steps - 1)
    local = states.shape[0]
    dims = states.shape[1]
    tracers = tracer_obs.shape[1]
    me = lax.axis_index("tm")

    count_pad = jnp.zeros((local, count - tracers - 1), jnp.float32)
    extra = jnp.concatenate(
        [
            ancestors.astype(jnp.float32)[:, None, :],
            jnp.concatenate([tracer_obs, jitter[:, None], count_pad], axis=1)[:, None, :],
            jnp.zeros((local, 6, count), jnp.float32),
        ],
        axis=1,
    )
    packed = jnp.concatenate([states, extra], axis=1)

    def need(k):
        if k <= head:
            return 0
        phase = (k - head) % stride
        return stride - 1 if phase == 0 else phase - 1

    devices = range(steps)

    def sent(block, distance, wanted):
        route = [(i - distance, i) for i in devices if i - distance >= 0 and wanted(i)]
        return lax.ppermute(block, "tm", route)

    rim_own = sent(states[-1], 1, lambda i: True)

    def own_matrices():
        return jax.vmap(transition, in_axes=(0, 0, 0, 0, 0, None, None))(
            jnp.stack([rim_own, states[0]]),
            states,
            ancestors,
            tracer_obs,
            jitter,
            fingerprints,
            tracer_scale,
        )

    weights_own = own_matrices()
    block_own = block_product([weights_own[0], weights_own[1]])

    core = lax.axis_index("rows") % 2
    half_rows = dims // 2
    packed_half = lax.dynamic_index_in_dim(packed, core, 0, keepdims=False)
    rim_half = lax.dynamic_slice_in_dim(states[-1], core * half_rows, half_rows, 0)
    weights_own, block_own, packed_half, rim_half = lax.optimization_barrier(
        (weights_own, block_own, packed_half, rim_half)
    )
    fetched = [sent(packed_half, d, lambda i, d=d: need(i) >= d) for d in range(1, stride)]
    fetched += [sent(rim_half, e, lambda i, e=e: need(i) + 1 == e) for e in range(2, stride + 1)]
    bundle = jnp.concatenate(fetched, axis=0)
    pairs = [(r, r ^ 1) for r in range(lax.axis_size("rows"))]
    other = lax.ppermute(bundle, "rows", pairs)

    def earlier(bundle, other):
        first_half = jnp.where(core == 0, bundle, other)
        second_half = jnp.where(core == 0, other, bundle)
        rows_of = [f.shape[0] for f in fetched]
        offsets = [sum(rows_of[:i]) for i in range(len(rows_of) + 1)]

        def joined(i):
            lo, hi = offsets[i], offsets[i + 1]
            return jnp.concatenate([first_half[lo:hi], second_half[lo:hi]], axis=0)

        packs = [packed] + [joined(i).reshape(packed.shape) for i in range(stride - 1)]
        rim_parts = [joined(stride - 1 + i) for i in range(stride - 1)]
        rims = [None] + [
            (packs[d + 1][-1, :dims, :] if d + 1 < stride else 0.0) + rim_parts[d - 1]
            for d in range(1, stride)
        ]
        previous = []
        current = []
        parents = []
        observed = []
        mixing = []
        for d in range(1, stride):
            block_states = packs[d][:, :dims, :]
            previous += [rims[d], block_states[0]]
            current += [block_states[0], block_states[1]]
            parents.append(packs[d][:, dims, :])
            observed.append(packs[d][:, dims + 1, :tracers])
            mixing.append(packs[d][:, dims + 1, tracers])
        weights_all = jax.vmap(transition, in_axes=(0, 0, 0, 0, 0, None, None))(
            jnp.stack(previous),
            jnp.stack(current),
            jnp.concatenate(parents).astype(jnp.int32),
            jnp.concatenate(observed),
            jnp.concatenate(mixing),
            fingerprints,
            tracer_scale,
        )
        products = lax.dot_general(
            weights_all[0::2],
            weights_all[1::2],
            (((2,), (1,)), ((0,), (0,))),
            precision=lax.Precision.HIGH,
            preferred_element_type=jnp.float32,
        )
        combined = block_product([products[d] for d in range(stride - 2, -1, -1)] + [block_own])
        return products, combined

    def skipped(bundle, other):
        return (
            jnp.zeros((stride - 1, count, count), jnp.float32),
            jnp.zeros((count, count), jnp.float32),
        )

    befores, combined = lax.cond(me > head, earlier, skipped, bundle, other)

    prior8 = jnp.broadcast_to(prior_weights[None, :], (8, count))
    weights = chain(weights_own, block_own, befores, combined, prior8, steps, stride, head)
    mine = lax.dynamic_slice_in_dim(weights[:local], row_start, own_rows, 1)
    return count * mine


def solution(mesh):
    return jax.shard_map(
        shards,
        mesh=mesh,
        in_specs=(P("tm", None, None), P("tm", None), P("tm", None), P("tm"), P(), P(), P()),
        out_specs=P("tm", "rows"),
        check_vma=False,
    )
```

```python
import functools

import jax
import jax.numpy as jnp
from jax import lax
from jax.experimental import pallas as pl
from jax.experimental.pallas import tpu as pltpu
from jax.sharding import PartitionSpec as P

MESH = pl.DeviceIdType.MESH
STRIDE = 3
HEAD = 12


def shifted(block, axis, distance):
    devices = range(lax.axis_size(axis))
    route = [(i - distance, i) for i in devices if i - distance in devices]
    return lax.ppermute(block, axis, route)


def transition(previous, current, parent_ids, observed, mixing, fingerprints, tracer_scale):
    count = current.shape[1]
    highest = lax.Precision.HIGHEST
    inner_prod = lax.dot_general(
        previous,
        current,
        (((0,), (0,)), ((), ())),
        precision=highest,
        preferred_element_type=jnp.float32,
    )
    distance = (
        jnp.sum(previous * previous, axis=0)[:, None]
        + jnp.sum(current * current, axis=0)[None, :]
        - 2.0 * inner_prod
    )
    kernel = jnp.exp(-2.0 * distance / current.shape[0])
    predicted = lax.dot_general(
        fingerprints,
        current,
        (((0,), (0,)), ((), ())),
        precision=highest,
        preferred_element_type=jnp.float32,
    )
    misfit = tracer_scale[:, None] * (observed[:, None] - predicted)
    likelihood = jnp.exp(-0.5 * jnp.sum(misfit * misfit, axis=0))
    likelihood = likelihood / jnp.max(likelihood)
    parent = (parent_ids[None, :] == jnp.arange(count, dtype=jnp.int32)[:, None]).astype(
        jnp.float32
    )
    return likelihood[None, :] * (parent + mixing * kernel)


def vec_mat(u_row, mat):
    n = mat.shape[0]
    u_col = jnp.transpose(jnp.broadcast_to(u_row[0:1, :], (128, n)))
    parts = []
    for g in range(n // 128):
        block = mat[:, g * 128:(g + 1) * 128]
        parts.append(jnp.sum(block * u_col, axis=0, keepdims=True))
    return jnp.concatenate(parts, axis=1)


def normalized(v):
    return v / jnp.sum(v)


def spread(v, like):
    return jnp.broadcast_to(v, like.shape)


def chain_kernel(steps, stride, head, *refs):
    weights_hbm, block_hbm, befores_hbm, combined_hbm, prior_ref = refs[:5]
    out_ref, recv_buf, send_buf, send_sem, recv_sem, load_sem = refs[5:11]
    local = refs[11:]
    me = lax.axis_index("tm")
    row = lax.axis_index("rows")
    last = steps - 1
    offset = me - head
    phase = jnp.maximum(offset, 0) % stride
    tail = me > head
    tail_node = jnp.logical_and(tail, phase == 0)
    fans = jnp.logical_or(me == head, tail_node)

    sources = [block_hbm, combined_hbm, weights_hbm.at[0], weights_hbm.at[1]]
    sources += [befores_hbm.at[d] for d in range(stride - 1)]
    loads = [
        pltpu.make_async_copy(sources[i], local[i], load_sem.at[i]) for i in range(len(sources))
    ]
    for load in loads:
        load.start()
    block_ref, combined_ref, first_ref, second_ref = local[:4]
    befores = local[4:]

    source_gap = jnp.where(me <= head, 1, jnp.where(phase == 0, stride, phase))
    sends = jnp.where(me < head, 1, jnp.where(fans, jnp.minimum(last - me, stride), 0))

    barrier = pltpu.get_barrier_semaphore()

    def greet(other):
        pl.semaphore_signal(barrier, 1, device_id=(other, row), device_id_type=MESH)

    @pl.when(me > 0)
    def _():
        greet(me - source_gap)

    for d in range(1, stride + 1):
        @pl.when(d <= sends)
        def _():
            greet(me + d)

    partners = sends + (me > 0).astype(jnp.int32)
    for amount in range(1, stride + 2):
        @pl.when(partners == amount)
        def _():
            pl.semaphore_wait(barrier, amount)

    def copy_to(d):
        return pltpu.make_async_remote_copy(
            src_ref=send_buf,
            dst_ref=recv_buf,
            send_sem=send_sem.at[d - 1],
            recv_sem=recv_sem,
            device_id=(jnp.minimum(me + d, last), row),
            device_id_type=MESH,
        )

    copies = [copy_to(d) for d in range(1, stride + 1)]

    def send_all(v):
        send_buf[...] = v
        for d in range(1, stride + 1):
            @pl.when(d <= sends)
            def _():
                copies[d - 1].start()

    loads[0].wait()
    loads[1].wait()

    @pl.when(me == 0)
    def _():
        out_ref[...] = spread(normalized(prior_ref[0:1, :]), out_ref)

    @pl.when(me > 0)
    def _():
        copies[0].wait_recv()
        out_ref[...] = spread(recv_buf[...], out_ref)

    @pl.when(me <= head)
    def _():
        send_all(normalized(vec_mat(out_ref[...], block_ref[...])))

    @pl.when(tail_node)
    def _():
        send_all(normalized(vec_mat(out_ref[...], combined_ref[...])))

    for load in loads[4:]:
        load.wait()
    lag = jnp.where(tail_node, stride - 1, jnp.where(tail, phase - 1, 0))
    for amount in range(1, stride):
        @pl.when(lag == amount)
        def _():
            u = out_ref[...]
            for d in range(amount, 0, -1):
                u = spread(normalized(vec_mat(u, befores[d - 1][...])), out_ref)
            out_ref[...] = u

    loads[2].wait()
    loads[3].wait()
    incoming = out_ref[...]
    w_first = normalized(vec_mat(incoming, first_ref[...]))
    w_second = normalized(vec_mat(spread(w_first, incoming), second_ref[...]))
    out_ref[...] = jnp.concatenate(
        [w_first, w_second, jnp.zeros((incoming.shape[0] - 2, incoming.shape[1]), jnp.float32)],
        axis=0,
    )

    for d in range(1, stride + 1):
        @pl.when(d <= sends)
        def _():
            copies[d - 1].wait_send()


def chain(weights_own, block, befores, combined, prior, steps, stride, head):
    count = combined.shape[0]
    loaded = stride + 3
    return pl.pallas_call(
        functools.partial(chain_kernel, steps, stride, head),
        out_shape=jax.ShapeDtypeStruct((8, count), jnp.float32),
        in_specs=[pl.BlockSpec(memory_space=pl.ANY)] * 4
        + [pl.BlockSpec(memory_space=pltpu.VMEM)],
        out_specs=pl.BlockSpec(memory_space=pltpu.VMEM),
        scratch_shapes=[
            pltpu.VMEM((1, count), jnp.float32),
            pltpu.VMEM((1, count), jnp.float32),
            pltpu.SemaphoreType.DMA((stride,)),
            pltpu.SemaphoreType.DMA,
            pltpu.SemaphoreType.DMA((loaded,)),
        ]
        + [pltpu.VMEM((count, count), jnp.float32) for _ in range(loaded)],
        compiler_params=pltpu.CompilerParams(
            collective_id=0, has_side_effects=True, vmem_limit_bytes=48 * 1024 * 1024
        ),
    )(weights_own, block, befores, combined, prior)


def block_product(matrices):
    block = matrices[0]
    for matrix in matrices[1:]:
        block = jnp.dot(
            block, matrix, precision=lax.Precision.HIGH, preferred_element_type=jnp.float32
        )
    return block


def shards(states, ancestors, tracer_obs, jitter, fingerprints, tracer_scale, prior_weights):
    count = states.shape[2]
    own_rows = count // lax.axis_size("rows")
    row_start = lax.axis_index("rows") * own_rows
    steps = lax.axis_size("tm")
    stride = STRIDE
    head = min(HEAD, steps - 1)
    local = states.shape[0]
    dims = states.shape[1]
    tracers = tracer_obs.shape[1]
    me = lax.axis_index("tm")

    count_pad = jnp.zeros((local, count - tracers - 1), jnp.float32)
    extra = jnp.concatenate(
        [
            ancestors.astype(jnp.float32)[:, None, :],
            jnp.concatenate([tracer_obs, jitter[:, None], count_pad], axis=1)[:, None, :],
            jnp.zeros((local, 6, count), jnp.float32),
        ],
        axis=1,
    )
    packed = jnp.concatenate([states, extra], axis=1)

    def need(k):
        if k <= head:
            return 0
        phase = (k - head) % stride
        return stride - 1 if phase == 0 else phase - 1

    devices = range(steps)

    def sent(block, distance, wanted):
        route = [(i - distance, i) for i in devices if i - distance >= 0 and wanted(i)]
        return lax.ppermute(block, "tm", route)

    rim_own = sent(states[-1], 1, lambda i: True)

    core = lax.axis_index("rows") % 2
    half_rows = dims // 2
    packed_half = lax.dynamic_index_in_dim(packed, core, 0, keepdims=False)
    rim_half = lax.dynamic_slice_in_dim(states[-1], core * half_rows, half_rows, 0)
    fetched = [sent(packed_half, d, lambda i: need(i) >= 1) for d in range(1, stride)]
    fetched += [sent(rim_half, stride, lambda i: need(i) == stride - 1)]
    bundle = jnp.concatenate(fetched, axis=0)
    pairs = [(r, r ^ 1) for r in range(lax.axis_size("rows"))]
    other = lax.ppermute(bundle, "rows", pairs)

    def own_matrices():
        return jax.vmap(transition, in_axes=(0, 0, 0, 0, 0, None, None))(
            jnp.stack([rim_own, states[0]]),
            states,
            ancestors,
            tracer_obs,
            jitter,
            fingerprints,
            tracer_scale,
        )

    weights_own = own_matrices()
    block_own = block_product([weights_own[0], weights_own[1]])

    def earlier(bundle, other):
        first_half = jnp.where(core == 0, bundle, other)
        second_half = jnp.where(core == 0, other, bundle)
        rows_of = [f.shape[0] for f in fetched]
        offsets = [sum(rows_of[:i]) for i in range(len(rows_of) + 1)]

        def joined(i):
            lo, hi = offsets[i], offsets[i + 1]
            return jnp.concatenate([first_half[lo:hi], second_half[lo:hi]], axis=0)

        packs = [packed] + [joined(i).reshape(packed.shape) for i in range(stride - 1)]
        rims = [None] + [packs[d + 1][-1, :dims, :] for d in range(1, stride - 1)]
        rims.append(joined(stride - 1))
        previous = []
        current = []
        parents = []
        observed = []
        mixing = []
        for d in range(1, stride):
            block_states = packs[d][:, :dims, :]
            previous += [rims[d], block_states[0]]
            current += [block_states[0], block_states[1]]
            parents.append(packs[d][:, dims, :])
            observed.append(packs[d][:, dims + 1, :tracers])
            mixing.append(packs[d][:, dims + 1, tracers])
        weights_all = jax.vmap(transition, in_axes=(0, 0, 0, 0, 0, None, None))(
            jnp.stack(previous),
            jnp.stack(current),
            jnp.concatenate(parents).astype(jnp.int32),
            jnp.concatenate(observed),
            jnp.concatenate(mixing),
            fingerprints,
            tracer_scale,
        )
        products = lax.dot_general(
            weights_all[0::2],
            weights_all[1::2],
            (((2,), (1,)), ((0,), (0,))),
            precision=lax.Precision.HIGH,
            preferred_element_type=jnp.float32,
        )
        combined = block_product([products[d] for d in range(stride - 2, -1, -1)] + [block_own])
        return products, combined

    def skipped(bundle, other):
        return (
            jnp.zeros((stride - 1, count, count), jnp.float32),
            jnp.zeros((count, count), jnp.float32),
        )

    befores, combined = lax.cond(me > head, earlier, skipped, bundle, other)

    prior8 = jnp.broadcast_to(prior_weights[None, :], (8, count))
    weights = chain(weights_own, block_own, befores, combined, prior8, steps, stride, head)
    mine = lax.dynamic_slice_in_dim(weights[:local], row_start, own_rows, 1)
    return count * mine


def solution(mesh):
    return jax.shard_map(
        shards,
        mesh=mesh,
        in_specs=(P("tm", None, None), P("tm", None), P("tm", None), P("tm"), P(), P(), P()),
        out_specs=P("tm", "rows"),
        check_vma=False,
    )
```

```python
import functools

import jax
import jax.numpy as jnp
from jax import lax
from jax.experimental import pallas as pl
from jax.experimental.pallas import tpu as pltpu
from jax.sharding import PartitionSpec as P

MESH = pl.DeviceIdType.MESH
STRIDE = 3
HEAD = 12


def shifted(block, axis, distance):
    devices = range(lax.axis_size(axis))
    route = [(i - distance, i) for i in devices if i - distance in devices]
    return lax.ppermute(block, axis, route)


def transition(previous, current, parent_ids, observed, mixing, fingerprints, tracer_scale):
    count = current.shape[1]
    highest = lax.Precision.HIGHEST
    inner_prod = lax.dot_general(
        previous,
        current,
        (((0,), (0,)), ((), ())),
        precision=highest,
        preferred_element_type=jnp.float32,
    )
    distance = (
        jnp.sum(previous * previous, axis=0)[:, None]
        + jnp.sum(current * current, axis=0)[None, :]
        - 2.0 * inner_prod
    )
    kernel = jnp.exp(-2.0 * distance / current.shape[0])
    predicted = lax.dot_general(
        fingerprints,
        current,
        (((0,), (0,)), ((), ())),
        precision=highest,
        preferred_element_type=jnp.float32,
    )
    misfit = tracer_scale[:, None] * (observed[:, None] - predicted)
    likelihood = jnp.exp(-0.5 * jnp.sum(misfit * misfit, axis=0))
    likelihood = likelihood / jnp.max(likelihood)
    parent = (parent_ids[None, :] == jnp.arange(count, dtype=jnp.int32)[:, None]).astype(
        jnp.float32
    )
    return likelihood[None, :] * (parent + mixing * kernel)


def vec_mat(u_row, mat):
    n = mat.shape[0]
    u_col = jnp.transpose(jnp.broadcast_to(u_row[0:1, :], (128, n)))
    parts = []
    for g in range(n // 128):
        block = mat[:, g * 128:(g + 1) * 128]
        parts.append(jnp.sum(block * u_col, axis=0, keepdims=True))
    return jnp.concatenate(parts, axis=1)


def normalized(v):
    return v / jnp.sum(v)


def spread(v, like):
    return jnp.broadcast_to(v, like.shape)


def chain_kernel(steps, stride, head, *refs):
    weights_hbm, block_hbm, befores_hbm, combined_hbm, prior_ref = refs[:5]
    out_ref, recv_buf, send_buf, send_sem, recv_sem, load_sem = refs[5:11]
    local = refs[11:]
    me = lax.axis_index("tm")
    row = lax.axis_index("rows")
    last = steps - 1
    offset = me - head
    phase = jnp.maximum(offset, 0) % stride
    tail = me > head
    tail_node = jnp.logical_and(tail, phase == 0)
    fans = jnp.logical_or(me == head, tail_node)

    sources = [block_hbm, combined_hbm, weights_hbm.at[0], weights_hbm.at[1]]
    sources += [befores_hbm.at[d] for d in range(stride - 1)]
    loads = [
        pltpu.make_async_copy(sources[i], local[i], load_sem.at[i]) for i in range(len(sources))
    ]
    for load in loads:
        load.start()
    block_ref, combined_ref, first_ref, second_ref = local[:4]
    befores = local[4:]

    source_gap = jnp.where(me <= head, 1, jnp.where(phase == 0, stride, phase))
    sends = jnp.where(me < head, 1, jnp.where(fans, jnp.minimum(last - me, stride), 0))

    barrier = pltpu.get_barrier_semaphore()

    def greet(other):
        pl.semaphore_signal(barrier, 1, device_id=(other, row), device_id_type=MESH)

    @pl.when(me > 0)
    def _():
        greet(me - source_gap)

    for d in range(1, stride + 1):
        @pl.when(d <= sends)
        def _():
            greet(me + d)

    partners = sends + (me > 0).astype(jnp.int32)
    for amount in range(1, stride + 2):
        @pl.when(partners == amount)
        def _():
            pl.semaphore_wait(barrier, amount)

    def copy_to(d):
        return pltpu.make_async_remote_copy(
            src_ref=send_buf,
            dst_ref=recv_buf,
            send_sem=send_sem.at[d - 1],
            recv_sem=recv_sem,
            device_id=(jnp.minimum(me + d, last), row),
            device_id_type=MESH,
        )

    copies = [copy_to(d) for d in range(1, stride + 1)]

    def send_all(v):
        send_buf[...] = v
        for d in range(stride, 0, -1):
            @pl.when(d <= sends)
            def _():
                copies[d - 1].start()

    loads[0].wait()
    loads[1].wait()

    @pl.when(me == 0)
    def _():
        out_ref[...] = spread(normalized(prior_ref[0:1, :]), out_ref)

    @pl.when(me > 0)
    def _():
        copies[0].wait_recv()
        out_ref[...] = spread(recv_buf[...], out_ref)

    @pl.when(me <= head)
    def _():
        send_all(normalized(vec_mat(out_ref[...], block_ref[...])))

    @pl.when(tail_node)
    def _():
        send_all(normalized(vec_mat(out_ref[...], combined_ref[...])))

    for load in loads[4:]:
        load.wait()
    lag = jnp.where(tail_node, stride - 1, jnp.where(tail, phase - 1, 0))
    for amount in range(1, stride):
        @pl.when(lag == amount)
        def _():
            u = out_ref[...]
            for d in range(amount, 0, -1):
                u = spread(normalized(vec_mat(u, befores[d - 1][...])), out_ref)
            out_ref[...] = u

    loads[2].wait()
    loads[3].wait()
    incoming = out_ref[...]
    w_first = normalized(vec_mat(incoming, first_ref[...]))
    w_second = normalized(vec_mat(spread(w_first, incoming), second_ref[...]))
    out_ref[...] = jnp.concatenate(
        [w_first, w_second, jnp.zeros((incoming.shape[0] - 2, incoming.shape[1]), jnp.float32)],
        axis=0,
    )

    for d in range(1, stride + 1):
        @pl.when(d <= sends)
        def _():
            copies[d - 1].wait_send()


def chain(weights_own, block, befores, combined, prior, steps, stride, head):
    count = combined.shape[0]
    loaded = stride + 3
    return pl.pallas_call(
        functools.partial(chain_kernel, steps, stride, head),
        out_shape=jax.ShapeDtypeStruct((8, count), jnp.float32),
        in_specs=[pl.BlockSpec(memory_space=pl.ANY)] * 4
        + [pl.BlockSpec(memory_space=pltpu.VMEM)],
        out_specs=pl.BlockSpec(memory_space=pltpu.VMEM),
        scratch_shapes=[
            pltpu.VMEM((1, count), jnp.float32),
            pltpu.VMEM((1, count), jnp.float32),
            pltpu.SemaphoreType.DMA((stride,)),
            pltpu.SemaphoreType.DMA,
            pltpu.SemaphoreType.DMA((loaded,)),
        ]
        + [pltpu.VMEM((count, count), jnp.float32) for _ in range(loaded)],
        compiler_params=pltpu.CompilerParams(
            collective_id=0, has_side_effects=True, vmem_limit_bytes=48 * 1024 * 1024
        ),
    )(weights_own, block, befores, combined, prior)


def block_product(matrices):
    block = matrices[0]
    for matrix in matrices[1:]:
        block = jnp.dot(
            block, matrix, precision=lax.Precision.HIGH, preferred_element_type=jnp.float32
        )
    return block


def shards(states, ancestors, tracer_obs, jitter, fingerprints, tracer_scale, prior_weights):
    count = states.shape[2]
    own_rows = count // lax.axis_size("rows")
    row_start = lax.axis_index("rows") * own_rows
    steps = lax.axis_size("tm")
    stride = STRIDE
    head = min(HEAD, steps - 1)
    local = states.shape[0]
    dims = states.shape[1]
    tracers = tracer_obs.shape[1]
    me = lax.axis_index("tm")

    count_pad = jnp.zeros((local, count - tracers - 1), jnp.float32)
    extra = jnp.concatenate(
        [
            ancestors.astype(jnp.float32)[:, None, :],
            jnp.concatenate([tracer_obs, jitter[:, None], count_pad], axis=1)[:, None, :],
            jnp.zeros((local, 6, count), jnp.float32),
        ],
        axis=1,
    )
    packed = jnp.concatenate([states, extra], axis=1)

    def need(k):
        if k <= head:
            return 0
        phase = (k - head) % stride
        return stride - 1 if phase == 0 else phase - 1

    devices = range(steps)

    def sent(block, distance, wanted):
        route = [(i - distance, i) for i in devices if i - distance >= 0 and wanted(i)]
        return lax.ppermute(block, "tm", route)

    rim_own = sent(states[-1], 1, lambda i: True)

    core = lax.axis_index("rows") % 2
    half_rows = dims // 2
    packed_half = lax.dynamic_index_in_dim(packed, core, 0, keepdims=False)
    rim_half = lax.dynamic_slice_in_dim(states[-1], core * half_rows, half_rows, 0)
    fetched = [sent(packed_half, d, lambda i, d=d: need(i) >= d) for d in range(1, stride)]
    fetched += [sent(rim_half, e, lambda i, e=e: need(i) + 1 == e) for e in range(2, stride + 1)]
    bundle = jnp.concatenate(fetched, axis=0)
    pairs = [(r, r ^ 1) for r in range(lax.axis_size("rows"))]
    other = lax.ppermute(bundle, "rows", pairs)

    def own_matrices():
        return jax.vmap(transition, in_axes=(0, 0, 0, 0, 0, None, None))(
            jnp.stack([rim_own, states[0]]),
            states,
            ancestors,
            tracer_obs,
            jitter,
            fingerprints,
            tracer_scale,
        )

    weights_own = own_matrices()
    block_own = block_product([weights_own[0], weights_own[1]])

    def earlier(bundle, other):
        first_half = jnp.where(core == 0, bundle, other)
        second_half = jnp.where(core == 0, other, bundle)
        rows_of = [f.shape[0] for f in fetched]
        offsets = [sum(rows_of[:i]) for i in range(len(rows_of) + 1)]

        def joined(i):
            lo, hi = offsets[i], offsets[i + 1]
            return jnp.concatenate([first_half[lo:hi], second_half[lo:hi]], axis=0)

        packs = [packed] + [joined(i).reshape(packed.shape) for i in range(stride - 1)]
        rim_parts = [joined(stride - 1 + i) for i in range(stride - 1)]
        rims = [None] + [
            (packs[d + 1][-1, :dims, :] if d + 1 < stride else 0.0) + rim_parts[d - 1]
            for d in range(1, stride)
        ]
        previous = []
        current = []
        parents = []
        observed = []
        mixing = []
        for d in range(1, stride):
            block_states = packs[d][:, :dims, :]
            previous += [rims[d], block_states[0]]
            current += [block_states[0], block_states[1]]
            parents.append(packs[d][:, dims, :])
            observed.append(packs[d][:, dims + 1, :tracers])
            mixing.append(packs[d][:, dims + 1, tracers])
        weights_all = jax.vmap(transition, in_axes=(0, 0, 0, 0, 0, None, None))(
            jnp.stack(previous),
            jnp.stack(current),
            jnp.concatenate(parents).astype(jnp.int32),
            jnp.concatenate(observed),
            jnp.concatenate(mixing),
            fingerprints,
            tracer_scale,
        )
        products = lax.dot_general(
            weights_all[0::2],
            weights_all[1::2],
            (((2,), (1,)), ((0,), (0,))),
            precision=lax.Precision.HIGH,
            preferred_element_type=jnp.float32,
        )
        combined = block_product([products[d] for d in range(stride - 2, -1, -1)] + [block_own])
        return products, combined

    def skipped(bundle, other):
        return (
            jnp.zeros((stride - 1, count, count), jnp.float32),
            jnp.zeros((count, count), jnp.float32),
        )

    befores, combined = lax.cond(me > head, earlier, skipped, bundle, other)

    prior8 = jnp.broadcast_to(prior_weights[None, :], (8, count))
    weights = chain(weights_own, block_own, befores, combined, prior8, steps, stride, head)
    mine = lax.dynamic_slice_in_dim(weights[:local], row_start, own_rows, 1)
    return count * mine


def solution(mesh):
    return jax.shard_map(
        shards,
        mesh=mesh,
        in_specs=(P("tm", None, None), P("tm", None), P("tm", None), P("tm"), P(), P(), P()),
        out_specs=P("tm", "rows"),
        check_vma=False,
    )
```

```python
import functools

import jax
import jax.numpy as jnp
from jax import lax
from jax.experimental import pallas as pl
from jax.experimental.pallas import tpu as pltpu
from jax.sharding import PartitionSpec as P

MESH = pl.DeviceIdType.MESH
STRIDE = 3
HEAD = 11


def shifted(block, axis, distance):
    devices = range(lax.axis_size(axis))
    route = [(i - distance, i) for i in devices if i - distance in devices]
    return lax.ppermute(block, axis, route)


def transition(previous, current, parent_ids, observed, mixing, fingerprints, tracer_scale):
    count = current.shape[1]
    highest = lax.Precision.HIGHEST
    inner_prod = lax.dot_general(
        previous,
        current,
        (((0,), (0,)), ((), ())),
        precision=highest,
        preferred_element_type=jnp.float32,
    )
    distance = (
        jnp.sum(previous * previous, axis=0)[:, None]
        + jnp.sum(current * current, axis=0)[None, :]
        - 2.0 * inner_prod
    )
    kernel = jnp.exp(-2.0 * distance / current.shape[0])
    predicted = lax.dot_general(
        fingerprints,
        current,
        (((0,), (0,)), ((), ())),
        precision=highest,
        preferred_element_type=jnp.float32,
    )
    misfit = tracer_scale[:, None] * (observed[:, None] - predicted)
    likelihood = jnp.exp(-0.5 * jnp.sum(misfit * misfit, axis=0))
    likelihood = likelihood / jnp.max(likelihood)
    parent = (parent_ids[None, :] == jnp.arange(count, dtype=jnp.int32)[:, None]).astype(
        jnp.float32
    )
    return likelihood[None, :] * (parent + mixing * kernel)


def vec_mat(u_row, mat):
    n = mat.shape[0]
    u_col = jnp.transpose(jnp.broadcast_to(u_row[0:1, :], (128, n)))
    parts = []
    for g in range(n // 128):
        block = mat[:, g * 128:(g + 1) * 128]
        parts.append(jnp.sum(block * u_col, axis=0, keepdims=True))
    return jnp.concatenate(parts, axis=1)


def normalized(v):
    return v / jnp.sum(v)


def spread(v, like):
    return jnp.broadcast_to(v, like.shape)


def chain_kernel(steps, stride, head, *refs):
    weights_hbm, block_hbm, befores_hbm, combined_hbm, prior_ref = refs[:5]
    out_ref, recv_buf, send_buf, send_sem, recv_sem, load_sem = refs[5:11]
    local = refs[11:]
    me = lax.axis_index("tm")
    row = lax.axis_index("rows")
    last = steps - 1
    offset = me - head
    phase = jnp.maximum(offset, 0) % stride
    tail = me > head
    tail_node = jnp.logical_and(tail, phase == 0)
    fans = jnp.logical_or(me == head, tail_node)

    sources = [block_hbm, combined_hbm, weights_hbm.at[0], weights_hbm.at[1]]
    sources += [befores_hbm.at[d] for d in range(stride - 1)]
    loads = [
        pltpu.make_async_copy(sources[i], local[i], load_sem.at[i]) for i in range(len(sources))
    ]
    for load in loads:
        load.start()
    block_ref, combined_ref, first_ref, second_ref = local[:4]
    befores = local[4:]

    source_gap = jnp.where(me <= head, 1, jnp.where(phase == 0, stride, phase))
    sends = jnp.where(me < head, 1, jnp.where(fans, jnp.minimum(last - me, stride), 0))

    barrier = pltpu.get_barrier_semaphore()

    def greet(other):
        pl.semaphore_signal(barrier, 1, device_id=(other, row), device_id_type=MESH)

    @pl.when(me > 0)
    def _():
        greet(me - source_gap)

    for d in range(1, stride + 1):
        @pl.when(d <= sends)
        def _():
            greet(me + d)

    partners = sends + (me > 0).astype(jnp.int32)
    for amount in range(1, stride + 2):
        @pl.when(partners == amount)
        def _():
            pl.semaphore_wait(barrier, amount)

    def copy_to(d):
        return pltpu.make_async_remote_copy(
            src_ref=send_buf,
            dst_ref=recv_buf,
            send_sem=send_sem.at[d - 1],
            recv_sem=recv_sem,
            device_id=(jnp.minimum(me + d, last), row),
            device_id_type=MESH,
        )

    copies = [copy_to(d) for d in range(1, stride + 1)]

    def send_all(v):
        send_buf[...] = v
        for d in range(stride, 0, -1):
            @pl.when(d <= sends)
            def _():
                copies[d - 1].start()

    loads[0].wait()
    loads[1].wait()

    @pl.when(me == 0)
    def _():
        out_ref[...] = spread(normalized(prior_ref[0:1, :]), out_ref)

    @pl.when(me > 0)
    def _():
        copies[0].wait_recv()
        out_ref[...] = spread(recv_buf[...], out_ref)

    @pl.when(me <= head)
    def _():
        send_all(normalized(vec_mat(out_ref[...], block_ref[...])))

    @pl.when(tail_node)
    def _():
        send_all(normalized(vec_mat(out_ref[...], combined_ref[...])))

    for load in loads[4:]:
        load.wait()
    lag = jnp.where(tail_node, stride - 1, jnp.where(tail, phase - 1, 0))
    for amount in range(1, stride):
        @pl.when(lag == amount)
        def _():
            u = out_ref[...]
            for d in range(amount, 0, -1):
                u = spread(normalized(vec_mat(u, befores[d - 1][...])), out_ref)
            out_ref[...] = u

    loads[2].wait()
    loads[3].wait()
    incoming = out_ref[...]
    w_first = normalized(vec_mat(incoming, first_ref[...]))
    w_second = normalized(vec_mat(spread(w_first, incoming), second_ref[...]))
    out_ref[...] = jnp.concatenate(
        [w_first, w_second, jnp.zeros((incoming.shape[0] - 2, incoming.shape[1]), jnp.float32)],
        axis=0,
    )

    for d in range(1, stride + 1):
        @pl.when(d <= sends)
        def _():
            copies[d - 1].wait_send()


def chain(weights_own, block, befores, combined, prior, steps, stride, head):
    count = combined.shape[0]
    loaded = stride + 3
    return pl.pallas_call(
        functools.partial(chain_kernel, steps, stride, head),
        out_shape=jax.ShapeDtypeStruct((8, count), jnp.float32),
        in_specs=[pl.BlockSpec(memory_space=pl.ANY)] * 4
        + [pl.BlockSpec(memory_space=pltpu.VMEM)],
        out_specs=pl.BlockSpec(memory_space=pltpu.VMEM),
        scratch_shapes=[
            pltpu.VMEM((1, count), jnp.float32),
            pltpu.VMEM((1, count), jnp.float32),
            pltpu.SemaphoreType.DMA((stride,)),
            pltpu.SemaphoreType.DMA,
            pltpu.SemaphoreType.DMA((loaded,)),
        ]
        + [pltpu.VMEM((count, count), jnp.float32) for _ in range(loaded)],
        compiler_params=pltpu.CompilerParams(
            collective_id=0, has_side_effects=True, vmem_limit_bytes=48 * 1024 * 1024
        ),
    )(weights_own, block, befores, combined, prior)


def block_product(matrices):
    block = matrices[0]
    for matrix in matrices[1:]:
        block = jnp.dot(
            block, matrix, precision=lax.Precision.HIGH, preferred_element_type=jnp.float32
        )
    return block


def shards(states, ancestors, tracer_obs, jitter, fingerprints, tracer_scale, prior_weights):
    count = states.shape[2]
    own_rows = count // lax.axis_size("rows")
    row_start = lax.axis_index("rows") * own_rows
    steps = lax.axis_size("tm")
    stride = STRIDE
    head = min(HEAD, steps - 1)
    local = states.shape[0]
    dims = states.shape[1]
    tracers = tracer_obs.shape[1]
    me = lax.axis_index("tm")

    count_pad = jnp.zeros((local, count - tracers - 1), jnp.float32)
    extra = jnp.concatenate(
        [
            ancestors.astype(jnp.float32)[:, None, :],
            jnp.concatenate([tracer_obs, jitter[:, None], count_pad], axis=1)[:, None, :],
            jnp.zeros((local, 6, count), jnp.float32),
        ],
        axis=1,
    )
    packed = jnp.concatenate([states, extra], axis=1)

    def need(k):
        if k <= head:
            return 0
        phase = (k - head) % stride
        return stride - 1 if phase == 0 else phase - 1

    devices = range(steps)

    def sent(block, distance, wanted):
        route = [(i - distance, i) for i in devices if i - distance >= 0 and wanted(i)]
        return lax.ppermute(block, "tm", route)

    rim_own = sent(states[-1], 1, lambda i: True)

    core = lax.axis_index("rows") % 2
    half_rows = dims // 2
    packed_half = lax.dynamic_index_in_dim(packed, core, 0, keepdims=False)
    rim_half = lax.dynamic_slice_in_dim(states[-1], core * half_rows, half_rows, 0)
    fetched = [sent(packed_half, d, lambda i, d=d: need(i) >= d) for d in range(1, stride)]
    fetched += [sent(rim_half, e, lambda i, e=e: need(i) + 1 == e) for e in range(2, stride + 1)]
    bundle = jnp.concatenate(fetched, axis=0)
    pairs = [(r, r ^ 1) for r in range(lax.axis_size("rows"))]
    other = lax.ppermute(bundle, "rows", pairs)

    def own_matrices():
        return jax.vmap(transition, in_axes=(0, 0, 0, 0, 0, None, None))(
            jnp.stack([rim_own, states[0]]),
            states,
            ancestors,
            tracer_obs,
            jitter,
            fingerprints,
            tracer_scale,
        )

    weights_own = own_matrices()
    block_own = block_product([weights_own[0], weights_own[1]])

    def earlier(bundle, other):
        first_half = jnp.where(core == 0, bundle, other)
        second_half = jnp.where(core == 0, other, bundle)
        rows_of = [f.shape[0] for f in fetched]
        offsets = [sum(rows_of[:i]) for i in range(len(rows_of) + 1)]

        def joined(i):
            lo, hi = offsets[i], offsets[i + 1]
            return jnp.concatenate([first_half[lo:hi], second_half[lo:hi]], axis=0)

        packs = [packed] + [joined(i).reshape(packed.shape) for i in range(stride - 1)]
        rim_parts = [joined(stride - 1 + i) for i in range(stride - 1)]
        rims = [None] + [
            (packs[d + 1][-1, :dims, :] if d + 1 < stride else 0.0) + rim_parts[d - 1]
            for d in range(1, stride)
        ]
        previous = []
        current = []
        parents = []
        observed = []
        mixing = []
        for d in range(1, stride):
            block_states = packs[d][:, :dims, :]
            previous += [rims[d], block_states[0]]
            current += [block_states[0], block_states[1]]
            parents.append(packs[d][:, dims, :])
            observed.append(packs[d][:, dims + 1, :tracers])
            mixing.append(packs[d][:, dims + 1, tracers])
        weights_all = jax.vmap(transition, in_axes=(0, 0, 0, 0, 0, None, None))(
            jnp.stack(previous),
            jnp.stack(current),
            jnp.concatenate(parents).astype(jnp.int32),
            jnp.concatenate(observed),
            jnp.concatenate(mixing),
            fingerprints,
            tracer_scale,
        )
        products = lax.dot_general(
            weights_all[0::2],
            weights_all[1::2],
            (((2,), (1,)), ((0,), (0,))),
            precision=lax.Precision.HIGH,
            preferred_element_type=jnp.float32,
        )
        combined = block_product([products[d] for d in range(stride - 2, -1, -1)] + [block_own])
        return products, combined

    def skipped(bundle, other):
        return (
            jnp.zeros((stride - 1, count, count), jnp.float32),
            jnp.zeros((count, count), jnp.float32),
        )

    befores, combined = lax.cond(me > head, earlier, skipped, bundle, other)

    prior8 = jnp.broadcast_to(prior_weights[None, :], (8, count))
    weights = chain(weights_own, block_own, befores, combined, prior8, steps, stride, head)
    mine = lax.dynamic_slice_in_dim(weights[:local], row_start, own_rows, 1)
    return count * mine


def solution(mesh):
    return jax.shard_map(
        shards,
        mesh=mesh,
        in_specs=(P("tm", None, None), P("tm", None), P("tm", None), P("tm"), P(), P(), P()),
        out_specs=P("tm", "rows"),
        check_vma=False,
    )
```

```python
import functools

import jax
import jax.numpy as jnp
from jax import lax
from jax.experimental import pallas as pl
from jax.experimental.pallas import tpu as pltpu
from jax.sharding import PartitionSpec as P

MESH = pl.DeviceIdType.MESH
STRIDE = 3
HEAD = 12


def shifted(block, axis, distance):
    devices = range(lax.axis_size(axis))
    route = [(i - distance, i) for i in devices if i - distance in devices]
    return lax.ppermute(block, axis, route)


def transition(previous, current, parent_ids, observed, mixing, fingerprints, tracer_scale):
    count = current.shape[1]
    highest = lax.Precision.HIGHEST
    inner_prod = lax.dot_general(
        previous,
        current,
        (((0,), (0,)), ((), ())),
        precision=highest,
        preferred_element_type=jnp.float32,
    )
    distance = (
        jnp.sum(previous * previous, axis=0)[:, None]
        + jnp.sum(current * current, axis=0)[None, :]
        - 2.0 * inner_prod
    )
    kernel = jnp.exp(-2.0 * distance / current.shape[0])
    predicted = lax.dot_general(
        fingerprints,
        current,
        (((0,), (0,)), ((), ())),
        precision=highest,
        preferred_element_type=jnp.float32,
    )
    misfit = tracer_scale[:, None] * (observed[:, None] - predicted)
    likelihood = jnp.exp(-0.5 * jnp.sum(misfit * misfit, axis=0))
    likelihood = likelihood / jnp.max(likelihood)
    parent = (parent_ids[None, :] == jnp.arange(count, dtype=jnp.int32)[:, None]).astype(
        jnp.float32
    )
    return likelihood[None, :] * (parent + mixing * kernel)


def vec_mat(u_row, mat):
    n = mat.shape[0]
    u_col = jnp.transpose(jnp.broadcast_to(u_row[0:1, :], (128, n)))
    parts = []
    for g in range(n // 128):
        block = mat[:, g * 128:(g + 1) * 128]
        parts.append(jnp.sum(block * u_col, axis=0, keepdims=True))
    return jnp.concatenate(parts, axis=1)


def normalized(v):
    return v / jnp.sum(v)


def spread(v, like):
    return jnp.broadcast_to(v, like.shape)


def chain_kernel(steps, stride, head, *refs):
    weights_hbm, block_hbm, befores_hbm, combined_hbm, prior_ref = refs[:5]
    out_ref, recv_buf, send_buf, send_sem, recv_sem, load_sem = refs[5:11]
    local = refs[11:]
    me = lax.axis_index("tm")
    row = lax.axis_index("rows")
    last = steps - 1
    offset = me - head
    phase = jnp.maximum(offset, 0) % stride
    tail = me > head
    tail_node = jnp.logical_and(tail, phase == 0)
    fans = jnp.logical_or(me == head, tail_node)

    sources = [block_hbm, combined_hbm, weights_hbm.at[0], weights_hbm.at[1]]
    sources += [befores_hbm.at[d] for d in range(stride - 1)]
    loads = [
        pltpu.make_async_copy(sources[i], local[i], load_sem.at[i]) for i in range(len(sources))
    ]
    for load in loads:
        load.start()
    block_ref, combined_ref, first_ref, second_ref = local[:4]
    befores = local[4:]

    source_gap = jnp.where(me <= head, 1, jnp.where(phase == 0, stride, phase))
    sends = jnp.where(me < head, 1, jnp.where(fans, jnp.minimum(last - me, stride), 0))

    barrier = pltpu.get_barrier_semaphore()

    def greet(other):
        pl.semaphore_signal(barrier, 1, device_id=(other, row), device_id_type=MESH)

    @pl.when(me > 0)
    def _():
        greet(me - source_gap)

    for d in range(1, stride + 1):
        @pl.when(d <= sends)
        def _():
            greet(me + d)

    partners = sends + (me > 0).astype(jnp.int32)
    for amount in range(1, stride + 2):
        @pl.when(partners == amount)
        def _():
            pl.semaphore_wait(barrier, amount)

    def copy_to(d):
        return pltpu.make_async_remote_copy(
            src_ref=send_buf,
            dst_ref=recv_buf,
            send_sem=send_sem.at[d - 1],
            recv_sem=recv_sem,
            device_id=(jnp.minimum(me + d, last), row),
            device_id_type=MESH,
        )

    copies = [copy_to(d) for d in range(1, stride + 1)]

    def send_all(v):
        send_buf[...] = v
        for d in range(stride, 0, -1):
            @pl.when(d <= sends)
            def _():
                copies[d - 1].start()

    loads[0].wait()

    @pl.when(tail_node)
    def _():
        loads[1].wait()

    @pl.when(me == 0)
    def _():
        out_ref[...] = spread(normalized(prior_ref[0:1, :]), out_ref)

    @pl.when(me > 0)
    def _():
        copies[0].wait_recv()
        out_ref[...] = spread(recv_buf[...], out_ref)

    @pl.when(me <= head)
    def _():
        send_all(normalized(vec_mat(out_ref[...], block_ref[...])))

    @pl.when(tail_node)
    def _():
        send_all(normalized(vec_mat(out_ref[...], combined_ref[...])))

    @pl.when(jnp.logical_not(tail_node))
    def _():
        loads[1].wait()

    for load in loads[4:]:
        load.wait()
    lag = jnp.where(tail_node, stride - 1, jnp.where(tail, phase - 1, 0))
    for amount in range(1, stride):
        @pl.when(lag == amount)
        def _():
            u = out_ref[...]
            for d in range(amount, 0, -1):
                u = spread(normalized(vec_mat(u, befores[d - 1][...])), out_ref)
            out_ref[...] = u

    loads[2].wait()
    loads[3].wait()
    incoming = out_ref[...]
    w_first = normalized(vec_mat(incoming, first_ref[...]))
    w_second = normalized(vec_mat(spread(w_first, incoming), second_ref[...]))
    out_ref[...] = jnp.concatenate(
        [w_first, w_second, jnp.zeros((incoming.shape[0] - 2, incoming.shape[1]), jnp.float32)],
        axis=0,
    )

    for d in range(1, stride + 1):
        @pl.when(d <= sends)
        def _():
            copies[d - 1].wait_send()


def chain(weights_own, block, befores, combined, prior, steps, stride, head):
    count = combined.shape[0]
    loaded = stride + 3
    return pl.pallas_call(
        functools.partial(chain_kernel, steps, stride, head),
        out_shape=jax.ShapeDtypeStruct((8, count), jnp.float32),
        in_specs=[pl.BlockSpec(memory_space=pl.ANY)] * 4
        + [pl.BlockSpec(memory_space=pltpu.VMEM)],
        out_specs=pl.BlockSpec(memory_space=pltpu.VMEM),
        scratch_shapes=[
            pltpu.VMEM((1, count), jnp.float32),
            pltpu.VMEM((1, count), jnp.float32),
            pltpu.SemaphoreType.DMA((stride,)),
            pltpu.SemaphoreType.DMA,
            pltpu.SemaphoreType.DMA((loaded,)),
        ]
        + [pltpu.VMEM((count, count), jnp.float32) for _ in range(loaded)],
        compiler_params=pltpu.CompilerParams(
            collective_id=0, has_side_effects=True, vmem_limit_bytes=48 * 1024 * 1024
        ),
    )(weights_own, block, befores, combined, prior)


def block_product(matrices):
    block = matrices[0]
    for matrix in matrices[1:]:
        block = jnp.dot(
            block, matrix, precision=lax.Precision.HIGH, preferred_element_type=jnp.float32
        )
    return block


def shards(states, ancestors, tracer_obs, jitter, fingerprints, tracer_scale, prior_weights):
    count = states.shape[2]
    own_rows = count // lax.axis_size("rows")
    row_start = lax.axis_index("rows") * own_rows
    steps = lax.axis_size("tm")
    stride = STRIDE
    head = min(HEAD, steps - 1)
    local = states.shape[0]
    dims = states.shape[1]
    tracers = tracer_obs.shape[1]
    me = lax.axis_index("tm")

    count_pad = jnp.zeros((local, count - tracers - 1), jnp.float32)
    extra = jnp.concatenate(
        [
            ancestors.astype(jnp.float32)[:, None, :],
            jnp.concatenate([tracer_obs, jitter[:, None], count_pad], axis=1)[:, None, :],
            jnp.zeros((local, 6, count), jnp.float32),
        ],
        axis=1,
    )
    packed = jnp.concatenate([states, extra], axis=1)

    def need(k):
        if k <= head:
            return 0
        phase = (k - head) % stride
        return stride - 1 if phase == 0 else phase - 1

    devices = range(steps)

    def sent(block, distance, wanted):
        route = [(i - distance, i) for i in devices if i - distance >= 0 and wanted(i)]
        return lax.ppermute(block, "tm", route)

    rim_own = sent(states[-1], 1, lambda i: True)

    core = lax.axis_index("rows") % 2
    half_rows = dims // 2
    packed_half = lax.dynamic_index_in_dim(packed, core, 0, keepdims=False)
    rim_half = lax.dynamic_slice_in_dim(states[-1], core * half_rows, half_rows, 0)
    fetched = [sent(packed_half, d, lambda i, d=d: need(i) >= d) for d in range(1, stride)]
    fetched += [sent(rim_half, e, lambda i, e=e: need(i) + 1 == e) for e in range(2, stride + 1)]
    bundle = jnp.concatenate(fetched, axis=0)
    pairs = [(r, r ^ 1) for r in range(lax.axis_size("rows"))]
    other = lax.ppermute(bundle, "rows", pairs)

    def own_matrices():
        return jax.vmap(transition, in_axes=(0, 0, 0, 0, 0, None, None))(
            jnp.stack([rim_own, states[0]]),
            states,
            ancestors,
            tracer_obs,
            jitter,
            fingerprints,
            tracer_scale,
        )

    weights_own = own_matrices()
    block_own = block_product([weights_own[0], weights_own[1]])

    def earlier(bundle, other):
        first_half = jnp.where(core == 0, bundle, other)
        second_half = jnp.where(core == 0, other, bundle)
        rows_of = [f.shape[0] for f in fetched]
        offsets = [sum(rows_of[:i]) for i in range(len(rows_of) + 1)]

        def joined(i):
            lo, hi = offsets[i], offsets[i + 1]
            return jnp.concatenate([first_half[lo:hi], second_half[lo:hi]], axis=0)

        packs = [packed] + [joined(i).reshape(packed.shape) for i in range(stride - 1)]
        rim_parts = [joined(stride - 1 + i) for i in range(stride - 1)]
        rims = [None] + [
            (packs[d + 1][-1, :dims, :] if d + 1 < stride else 0.0) + rim_parts[d - 1]
            for d in range(1, stride)
        ]
        previous = []
        current = []
        parents = []
        observed = []
        mixing = []
        for d in range(1, stride):
            block_states = packs[d][:, :dims, :]
            previous += [rims[d], block_states[0]]
            current += [block_states[0], block_states[1]]
            parents.append(packs[d][:, dims, :])
            observed.append(packs[d][:, dims + 1, :tracers])
            mixing.append(packs[d][:, dims + 1, tracers])
        weights_all = jax.vmap(transition, in_axes=(0, 0, 0, 0, 0, None, None))(
            jnp.stack(previous),
            jnp.stack(current),
            jnp.concatenate(parents).astype(jnp.int32),
            jnp.concatenate(observed),
            jnp.concatenate(mixing),
            fingerprints,
            tracer_scale,
        )
        products = lax.dot_general(
            weights_all[0::2],
            weights_all[1::2],
            (((2,), (1,)), ((0,), (0,))),
            precision=lax.Precision.HIGH,
            preferred_element_type=jnp.float32,
        )
        combined = block_product([products[d] for d in range(stride - 2, -1, -1)] + [block_own])
        return products, combined

    def skipped(bundle, other):
        return (
            jnp.zeros((stride - 1, count, count), jnp.float32),
            jnp.zeros((count, count), jnp.float32),
        )

    befores, combined = lax.cond(me > head, earlier, skipped, bundle, other)

    prior8 = jnp.broadcast_to(prior_weights[None, :], (8, count))
    weights = chain(weights_own, block_own, befores, combined, prior8, steps, stride, head)
    mine = lax.dynamic_slice_in_dim(weights[:local], row_start, own_rows, 1)
    return count * mine


def solution(mesh):
    return jax.shard_map(
        shards,
        mesh=mesh,
        in_specs=(P("tm", None, None), P("tm", None), P("tm", None), P("tm"), P(), P(), P()),
        out_specs=P("tm", "rows"),
        check_vma=False,
    )
```

```python
import functools

import jax
import jax.numpy as jnp
from jax import lax
from jax.experimental import pallas as pl
from jax.experimental.pallas import tpu as pltpu
from jax.sharding import PartitionSpec as P

MESH = pl.DeviceIdType.MESH
STRIDE = 3
HEAD = 12


def shifted(block, axis, distance):
    devices = range(lax.axis_size(axis))
    route = [(i - distance, i) for i in devices if i - distance in devices]
    return lax.ppermute(block, axis, route)


def transition(previous, current, parent_ids, observed, mixing, fingerprints, tracer_scale):
    count = current.shape[1]
    highest = lax.Precision.HIGHEST
    inner_prod = lax.dot_general(
        previous,
        current,
        (((0,), (0,)), ((), ())),
        precision=highest,
        preferred_element_type=jnp.float32,
    )
    distance = (
        jnp.sum(previous * previous, axis=0)[:, None]
        + jnp.sum(current * current, axis=0)[None, :]
        - 2.0 * inner_prod
    )
    kernel = jnp.exp(-2.0 * distance / current.shape[0])
    predicted = lax.dot_general(
        fingerprints,
        current,
        (((0,), (0,)), ((), ())),
        precision=highest,
        preferred_element_type=jnp.float32,
    )
    misfit = tracer_scale[:, None] * (observed[:, None] - predicted)
    likelihood = jnp.exp(-0.5 * jnp.sum(misfit * misfit, axis=0))
    likelihood = likelihood / jnp.max(likelihood)
    parent = (parent_ids[None, :] == jnp.arange(count, dtype=jnp.int32)[:, None]).astype(
        jnp.float32
    )
    return likelihood[None, :] * (parent + mixing * kernel)


def vec_mat(u_row, mat):
    n = mat.shape[0]
    u_col = jnp.transpose(jnp.broadcast_to(u_row[0:1, :], (128, n)))
    parts = []
    for g in range(n // 128):
        block = mat[:, g * 128:(g + 1) * 128]
        parts.append(jnp.sum(block * u_col, axis=0, keepdims=True))
    return jnp.concatenate(parts, axis=1)


def normalized(v):
    return v / jnp.sum(v)


def spread(v, like):
    return jnp.broadcast_to(v, like.shape)


def chain_kernel(steps, stride, head, *refs):
    weights_hbm, block_hbm, befores_hbm, combined_hbm, prior_ref = refs[:5]
    out_ref, recv_buf, send_buf, send_sem, recv_sem, load_sem = refs[5:11]
    local = refs[11:]
    me = lax.axis_index("tm")
    row = lax.axis_index("rows")
    last = steps - 1
    offset = me - head
    phase = jnp.maximum(offset, 0) % stride
    tail = me > head
    tail_node = jnp.logical_and(tail, phase == 0)
    fans = jnp.logical_or(me == head, tail_node)

    sources = [block_hbm, combined_hbm, weights_hbm.at[0], weights_hbm.at[1]]
    sources += [befores_hbm.at[d] for d in range(stride - 1)]
    loads = [
        pltpu.make_async_copy(sources[i], local[i], load_sem.at[i]) for i in range(len(sources))
    ]
    for load in loads:
        load.start()
    block_ref, combined_ref, first_ref, second_ref = local[:4]
    befores = local[4:]

    source_gap = jnp.where(me <= head, 1, jnp.where(phase == 0, stride, phase))
    sends = jnp.where(me < head, 1, jnp.where(fans, jnp.minimum(last - me, stride), 0))

    barrier = pltpu.get_barrier_semaphore()

    def greet(other):
        pl.semaphore_signal(barrier, 1, device_id=(other, row), device_id_type=MESH)

    @pl.when(me > 0)
    def _():
        greet(me - source_gap)

    for d in range(1, stride + 1):
        @pl.when(d <= sends)
        def _():
            greet(me + d)

    partners = sends + (me > 0).astype(jnp.int32)
    for amount in range(1, stride + 2):
        @pl.when(partners == amount)
        def _():
            pl.semaphore_wait(barrier, amount)

    def copy_to(d):
        return pltpu.make_async_remote_copy(
            src_ref=send_buf,
            dst_ref=recv_buf,
            send_sem=send_sem.at[d - 1],
            recv_sem=recv_sem,
            device_id=(jnp.minimum(me + d, last), row),
            device_id_type=MESH,
        )

    copies = [copy_to(d) for d in range(1, stride + 1)]

    def send_all(v):
        send_buf[...] = v
        for d in range(stride, 0, -1):
            @pl.when(d <= sends)
            def _():
                copies[d - 1].start()

    loads[0].wait()

    @pl.when(tail_node)
    def _():
        loads[1].wait()

    @pl.when(me == 0)
    def _():
        out_ref[...] = spread(normalized(prior_ref[0:1, :]), out_ref)

    @pl.when(jnp.logical_and(me > 0, me <= head))
    def _():
        copies[0].wait_recv()
        received = recv_buf[...]
        send_all(normalized(vec_mat(received, block_ref[...])))
        out_ref[...] = spread(received, out_ref)

    @pl.when(me == 0)
    def _():
        send_all(normalized(vec_mat(out_ref[...], block_ref[...])))

    @pl.when(tail_node)
    def _():
        copies[0].wait_recv()
        received = recv_buf[...]
        send_all(normalized(vec_mat(received, combined_ref[...])))
        out_ref[...] = spread(received, out_ref)

    @pl.when(jnp.logical_and(tail, jnp.logical_not(tail_node)))
    def _():
        copies[0].wait_recv()
        out_ref[...] = spread(recv_buf[...], out_ref)

    @pl.when(jnp.logical_not(tail_node))
    def _():
        loads[1].wait()

    for load in loads[4:]:
        load.wait()
    lag = jnp.where(tail_node, stride - 1, jnp.where(tail, phase - 1, 0))
    for amount in range(1, stride):
        @pl.when(lag == amount)
        def _():
            u = out_ref[...]
            for d in range(amount, 0, -1):
                u = spread(normalized(vec_mat(u, befores[d - 1][...])), out_ref)
            out_ref[...] = u

    loads[2].wait()
    loads[3].wait()
    incoming = out_ref[...]
    w_first = normalized(vec_mat(incoming, first_ref[...]))
    w_second = normalized(vec_mat(spread(w_first, incoming), second_ref[...]))
    out_ref[...] = jnp.concatenate(
        [w_first, w_second, jnp.zeros((incoming.shape[0] - 2, incoming.shape[1]), jnp.float32)],
        axis=0,
    )

    for d in range(1, stride + 1):
        @pl.when(d <= sends)
        def _():
            copies[d - 1].wait_send()


def chain(weights_own, block, befores, combined, prior, steps, stride, head):
    count = combined.shape[0]
    loaded = stride + 3
    return pl.pallas_call(
        functools.partial(chain_kernel, steps, stride, head),
        out_shape=jax.ShapeDtypeStruct((8, count), jnp.float32),
        in_specs=[pl.BlockSpec(memory_space=pl.ANY)] * 4
        + [pl.BlockSpec(memory_space=pltpu.VMEM)],
        out_specs=pl.BlockSpec(memory_space=pltpu.VMEM),
        scratch_shapes=[
            pltpu.VMEM((1, count), jnp.float32),
            pltpu.VMEM((1, count), jnp.float32),
            pltpu.SemaphoreType.DMA((stride,)),
            pltpu.SemaphoreType.DMA,
            pltpu.SemaphoreType.DMA((loaded,)),
        ]
        + [pltpu.VMEM((count, count), jnp.float32) for _ in range(loaded)],
        compiler_params=pltpu.CompilerParams(
            collective_id=0, has_side_effects=True, vmem_limit_bytes=48 * 1024 * 1024
        ),
    )(weights_own, block, befores, combined, prior)


def block_product(matrices):
    block = matrices[0]
    for matrix in matrices[1:]:
        block = jnp.dot(
            block, matrix, precision=lax.Precision.HIGH, preferred_element_type=jnp.float32
        )
    return block


def shards(states, ancestors, tracer_obs, jitter, fingerprints, tracer_scale, prior_weights):
    count = states.shape[2]
    own_rows = count // lax.axis_size("rows")
    row_start = lax.axis_index("rows") * own_rows
    steps = lax.axis_size("tm")
    stride = STRIDE
    head = min(HEAD, steps - 1)
    local = states.shape[0]
    dims = states.shape[1]
    tracers = tracer_obs.shape[1]
    me = lax.axis_index("tm")

    count_pad = jnp.zeros((local, count - tracers - 1), jnp.float32)
    extra = jnp.concatenate(
        [
            ancestors.astype(jnp.float32)[:, None, :],
            jnp.concatenate([tracer_obs, jitter[:, None], count_pad], axis=1)[:, None, :],
            jnp.zeros((local, 6, count), jnp.float32),
        ],
        axis=1,
    )
    packed = jnp.concatenate([states, extra], axis=1)

    def need(k):
        if k <= head:
            return 0
        phase = (k - head) % stride
        return stride - 1 if phase == 0 else phase - 1

    devices = range(steps)

    def sent(block, distance, wanted):
        route = [(i - distance, i) for i in devices if i - distance >= 0 and wanted(i)]
        return lax.ppermute(block, "tm", route)

    rim_own = sent(states[-1], 1, lambda i: True)

    core = lax.axis_index("rows") % 2
    half_rows = dims // 2
    packed_half = lax.dynamic_index_in_dim(packed, core, 0, keepdims=False)
    rim_half = lax.dynamic_slice_in_dim(states[-1], core * half_rows, half_rows, 0)
    fetched = [sent(packed_half, d, lambda i, d=d: need(i) >= d) for d in range(1, stride)]
    fetched += [sent(rim_half, e, lambda i, e=e: need(i) + 1 == e) for e in range(2, stride + 1)]
    bundle = jnp.concatenate(fetched, axis=0)
    pairs = [(r, r ^ 1) for r in range(lax.axis_size("rows"))]
    other = lax.ppermute(bundle, "rows", pairs)

    def own_matrices():
        return jax.vmap(transition, in_axes=(0, 0, 0, 0, 0, None, None))(
            jnp.stack([rim_own, states[0]]),
            states,
            ancestors,
            tracer_obs,
            jitter,
            fingerprints,
            tracer_scale,
        )

    weights_own = own_matrices()
    block_own = block_product([weights_own[0], weights_own[1]])

    def earlier(bundle, other):
        first_half = jnp.where(core == 0, bundle, other)
        second_half = jnp.where(core == 0, other, bundle)
        rows_of = [f.shape[0] for f in fetched]
        offsets = [sum(rows_of[:i]) for i in range(len(rows_of) + 1)]

        def joined(i):
            lo, hi = offsets[i], offsets[i + 1]
            return jnp.concatenate([first_half[lo:hi], second_half[lo:hi]], axis=0)

        packs = [packed] + [joined(i).reshape(packed.shape) for i in range(stride - 1)]
        rim_parts = [joined(stride - 1 + i) for i in range(stride - 1)]
        rims = [None] + [
            (packs[d + 1][-1, :dims, :] if d + 1 < stride else 0.0) + rim_parts[d - 1]
            for d in range(1, stride)
        ]
        previous = []
        current = []
        parents = []
        observed = []
        mixing = []
        for d in range(1, stride):
            block_states = packs[d][:, :dims, :]
            previous += [rims[d], block_states[0]]
            current += [block_states[0], block_states[1]]
            parents.append(packs[d][:, dims, :])
            observed.append(packs[d][:, dims + 1, :tracers])
            mixing.append(packs[d][:, dims + 1, tracers])
        weights_all = jax.vmap(transition, in_axes=(0, 0, 0, 0, 0, None, None))(
            jnp.stack(previous),
            jnp.stack(current),
            jnp.concatenate(parents).astype(jnp.int32),
            jnp.concatenate(observed),
            jnp.concatenate(mixing),
            fingerprints,
            tracer_scale,
        )
        products = lax.dot_general(
            weights_all[0::2],
            weights_all[1::2],
            (((2,), (1,)), ((0,), (0,))),
            precision=lax.Precision.HIGH,
            preferred_element_type=jnp.float32,
        )
        combined = block_product([products[d] for d in range(stride - 2, -1, -1)] + [block_own])
        return products, combined

    def skipped(bundle, other):
        return (
            jnp.zeros((stride - 1, count, count), jnp.float32),
            jnp.zeros((count, count), jnp.float32),
        )

    befores, combined = lax.cond(me > head, earlier, skipped, bundle, other)

    prior8 = jnp.broadcast_to(prior_weights[None, :], (8, count))
    weights = chain(weights_own, block_own, befores, combined, prior8, steps, stride, head)
    mine = lax.dynamic_slice_in_dim(weights[:local], row_start, own_rows, 1)
    return count * mine


def solution(mesh):
    return jax.shard_map(
        shards,
        mesh=mesh,
        in_specs=(P("tm", None, None), P("tm", None), P("tm", None), P("tm"), P(), P(), P()),
        out_specs=P("tm", "rows"),
        check_vma=False,
    )
```

```python
import functools

import jax
import jax.numpy as jnp
from jax import lax
from jax.experimental import pallas as pl
from jax.experimental.pallas import tpu as pltpu
from jax.sharding import PartitionSpec as P

MESH = pl.DeviceIdType.MESH
STRIDE = 3
HEAD = 12


def shifted(block, axis, distance):
    devices = range(lax.axis_size(axis))
    route = [(i - distance, i) for i in devices if i - distance in devices]
    return lax.ppermute(block, axis, route)


def transition(previous, current, parent_ids, observed, mixing, fingerprints, tracer_scale):
    count = current.shape[1]
    highest = lax.Precision.HIGHEST
    inner_prod = lax.dot_general(
        previous,
        current,
        (((0,), (0,)), ((), ())),
        precision=highest,
        preferred_element_type=jnp.float32,
    )
    distance = (
        jnp.sum(previous * previous, axis=0)[:, None]
        + jnp.sum(current * current, axis=0)[None, :]
        - 2.0 * inner_prod
    )
    kernel = jnp.exp(-2.0 * distance / current.shape[0])
    predicted = lax.dot_general(
        fingerprints,
        current,
        (((0,), (0,)), ((), ())),
        precision=highest,
        preferred_element_type=jnp.float32,
    )
    misfit = tracer_scale[:, None] * (observed[:, None] - predicted)
    likelihood = jnp.exp(-0.5 * jnp.sum(misfit * misfit, axis=0))
    likelihood = likelihood / jnp.max(likelihood)
    parent = (parent_ids[None, :] == jnp.arange(count, dtype=jnp.int32)[:, None]).astype(
        jnp.float32
    )
    return likelihood[None, :] * (parent + mixing * kernel)


def vec_mat(u_row, mat):
    n = mat.shape[0]
    u_col = jnp.transpose(jnp.broadcast_to(u_row[0:1, :], (128, n)))
    parts = []
    for g in range(n // 128):
        block = mat[:, g * 128:(g + 1) * 128]
        parts.append(jnp.sum(block * u_col, axis=0, keepdims=True))
    return jnp.concatenate(parts, axis=1)


def normalized(v):
    return v / jnp.sum(v)


def spread(v, like):
    return jnp.broadcast_to(v, like.shape)


def chain_kernel(steps, stride, head, *refs):
    weights_hbm, block_hbm, befores_hbm, combined_hbm, prior_ref = refs[:5]
    out_ref, recv_buf, send_buf, send_sem, recv_sem, load_sem = refs[5:11]
    local = refs[11:]
    me = lax.axis_index("tm")
    row = lax.axis_index("rows")
    last = steps - 1
    offset = me - head
    phase = jnp.maximum(offset, 0) % stride
    tail = me > head
    tail_node = jnp.logical_and(tail, phase == 0)
    fans = jnp.logical_or(me == head, tail_node)

    sources = [block_hbm, combined_hbm, weights_hbm.at[0], weights_hbm.at[1]]
    sources += [befores_hbm.at[d] for d in range(stride - 1)]
    loads = [
        pltpu.make_async_copy(sources[i], local[i], load_sem.at[i]) for i in range(len(sources))
    ]
    for load in loads:
        load.start()
    block_ref, combined_ref, first_ref, second_ref = local[:4]
    befores = local[4:]

    source_gap = jnp.where(me <= head, 1, jnp.where(phase == 0, stride, phase))
    sends = jnp.where(me < head, 1, jnp.where(fans, jnp.minimum(last - me, stride), 0))

    barrier = pltpu.get_barrier_semaphore()

    def greet(other):
        pl.semaphore_signal(barrier, 1, device_id=(other, row), device_id_type=MESH)

    @pl.when(me > 0)
    def _():
        greet(me - source_gap)

    for d in range(1, stride + 1):
        @pl.when(d <= sends)
        def _():
            greet(me + d)

    partners = sends + (me > 0).astype(jnp.int32)
    for amount in range(1, stride + 2):
        @pl.when(partners == amount)
        def _():
            pl.semaphore_wait(barrier, amount)

    def copy_to(d):
        return pltpu.make_async_remote_copy(
            src_ref=send_buf,
            dst_ref=recv_buf,
            send_sem=send_sem.at[d - 1],
            recv_sem=recv_sem,
            device_id=(jnp.minimum(me + d, last), row),
            device_id_type=MESH,
        )

    copies = [copy_to(d) for d in range(1, stride + 1)]

    def send_all(v):
        send_buf[...] = v
        for d in range(stride, 0, -1):
            @pl.when(d <= sends)
            def _():
                copies[d - 1].start()

    loads[0].wait()

    @pl.when(tail_node)
    def _():
        loads[1].wait()

    @pl.when(me == 0)
    def _():
        out_ref[...] = spread(normalized(prior_ref[0:1, :]), out_ref)

    @pl.when(me > 0)
    def _():
        copies[0].wait_recv()
        out_ref[...] = spread(recv_buf[...], out_ref)

    @pl.when(me <= head)
    def _():
        send_all(normalized(vec_mat(out_ref[...], block_ref[...])))

    @pl.when(tail_node)
    def _():
        send_all(normalized(vec_mat(out_ref[...], combined_ref[...])))

    @pl.when(jnp.logical_not(tail_node))
    def _():
        loads[1].wait()

    for load in loads[4:]:
        load.wait()
    lag = jnp.where(tail_node, stride - 1, jnp.where(tail, phase - 1, 0))
    for amount in range(1, stride):
        @pl.when(lag == amount)
        def _():
            u = out_ref[...]
            for d in range(amount, 0, -1):
                u = spread(normalized(vec_mat(u, befores[d - 1][...])), out_ref)
            out_ref[...] = u

    loads[2].wait()
    loads[3].wait()
    incoming = out_ref[...]
    w_first = normalized(vec_mat(incoming, first_ref[...]))
    w_second = normalized(vec_mat(spread(w_first, incoming), second_ref[...]))
    out_ref[...] = jnp.concatenate(
        [w_first, w_second, jnp.zeros((incoming.shape[0] - 2, incoming.shape[1]), jnp.float32)],
        axis=0,
    )

    for d in range(1, stride + 1):
        @pl.when(d <= sends)
        def _():
            copies[d - 1].wait_send()


def chain(weights_own, block, befores, combined, prior, steps, stride, head):
    count = combined.shape[0]
    loaded = stride + 3
    return pl.pallas_call(
        functools.partial(chain_kernel, steps, stride, head),
        out_shape=jax.ShapeDtypeStruct((8, count), jnp.float32),
        in_specs=[pl.BlockSpec(memory_space=pl.ANY)] * 4
        + [pl.BlockSpec(memory_space=pltpu.VMEM)],
        out_specs=pl.BlockSpec(memory_space=pltpu.VMEM),
        scratch_shapes=[
            pltpu.VMEM((1, count), jnp.float32),
            pltpu.VMEM((1, count), jnp.float32),
            pltpu.SemaphoreType.DMA((stride,)),
            pltpu.SemaphoreType.DMA,
            pltpu.SemaphoreType.DMA((loaded,)),
        ]
        + [pltpu.VMEM((count, count), jnp.float32) for _ in range(loaded)],
        compiler_params=pltpu.CompilerParams(
            collective_id=0, has_side_effects=True, vmem_limit_bytes=48 * 1024 * 1024
        ),
    )(weights_own, block, befores, combined, prior)


def block_product(matrices):
    block = matrices[0]
    for matrix in matrices[1:]:
        block = jnp.dot(
            block, matrix, precision=lax.Precision.HIGH, preferred_element_type=jnp.float32
        )
    return block


def shards(states, ancestors, tracer_obs, jitter, fingerprints, tracer_scale, prior_weights):
    count = states.shape[2]
    own_rows = count // lax.axis_size("rows")
    row_start = lax.axis_index("rows") * own_rows
    steps = lax.axis_size("tm")
    stride = STRIDE
    head = min(HEAD, steps - 1)
    local = states.shape[0]
    dims = states.shape[1]
    tracers = tracer_obs.shape[1]
    me = lax.axis_index("tm")

    count_pad = jnp.zeros((local, count - tracers - 1), jnp.float32)
    extra = jnp.concatenate(
        [
            ancestors.astype(jnp.float32)[:, None, :],
            jnp.concatenate([tracer_obs, jitter[:, None], count_pad], axis=1)[:, None, :],
            jnp.zeros((local, 6, count), jnp.float32),
        ],
        axis=1,
    )
    packed = jnp.concatenate([states, extra], axis=1)

    def need(k):
        if k <= head:
            return 0
        phase = (k - head) % stride
        return stride - 1 if phase == 0 else phase - 1

    devices = range(steps)

    def sent(block, distance, wanted):
        route = [(i - distance, i) for i in devices if i - distance >= 0 and wanted(i)]
        return lax.ppermute(block, "tm", route)

    rim_own = sent(states[-1], 1, lambda i: True)

    core = lax.axis_index("rows") % 2
    half_rows = dims // 2
    packed_half = lax.dynamic_index_in_dim(packed, core, 0, keepdims=False)
    rim_half = lax.dynamic_slice_in_dim(states[-1], core * half_rows, half_rows, 0)
    fetched = [sent(packed_half, d, lambda i, d=d: need(i) >= d) for d in range(1, stride)]
    fetched += [sent(rim_half, e, lambda i, e=e: need(i) + 1 == e) for e in range(2, stride + 1)]
    bundle = jnp.concatenate(fetched, axis=0)
    pairs = [(r, r ^ 1) for r in range(lax.axis_size("rows"))]
    other = lax.ppermute(bundle, "rows", pairs)

    def own_matrices():
        return jax.vmap(transition, in_axes=(0, 0, 0, 0, 0, None, None))(
            jnp.stack([rim_own, states[0]]),
            states,
            ancestors,
            tracer_obs,
            jitter,
            fingerprints,
            tracer_scale,
        )

    weights_own = own_matrices()
    block_own = block_product([weights_own[0], weights_own[1]])

    def earlier(bundle, other):
        first_half = jnp.where(core == 0, bundle, other)
        second_half = jnp.where(core == 0, other, bundle)
        rows_of = [f.shape[0] for f in fetched]
        offsets = [sum(rows_of[:i]) for i in range(len(rows_of) + 1)]

        def joined(i):
            lo, hi = offsets[i], offsets[i + 1]
            return jnp.concatenate([first_half[lo:hi], second_half[lo:hi]], axis=0)

        packs = [packed] + [joined(i).reshape(packed.shape) for i in range(stride - 1)]
        rim_parts = [joined(stride - 1 + i) for i in range(stride - 1)]
        rims = [None] + [
            (packs[d + 1][-1, :dims, :] if d + 1 < stride else 0.0) + rim_parts[d - 1]
            for d in range(1, stride)
        ]
        previous = []
        current = []
        parents = []
        observed = []
        mixing = []
        for d in range(1, stride):
            block_states = packs[d][:, :dims, :]
            previous += [rims[d], block_states[0]]
            current += [block_states[0], block_states[1]]
            parents.append(packs[d][:, dims, :])
            observed.append(packs[d][:, dims + 1, :tracers])
            mixing.append(packs[d][:, dims + 1, tracers])
        weights_all = jax.vmap(transition, in_axes=(0, 0, 0, 0, 0, None, None))(
            jnp.stack(previous),
            jnp.stack(current),
            jnp.concatenate(parents).astype(jnp.int32),
            jnp.concatenate(observed),
            jnp.concatenate(mixing),
            fingerprints,
            tracer_scale,
        )
        products = lax.dot_general(
            weights_all[0::2],
            weights_all[1::2],
            (((2,), (1,)), ((0,), (0,))),
            precision=lax.Precision.HIGH,
            preferred_element_type=jnp.float32,
        )
        combined = block_product([products[d] for d in range(stride - 2, -1, -1)] + [block_own])
        return products, combined

    def skipped(bundle, other, weights_own, block_own):
        return weights_own, block_own

    def tail_branch(bundle, other, weights_own, block_own):
        return earlier(bundle, other)

    befores, combined = lax.cond(
        me > head, tail_branch, skipped, bundle, other, weights_own, block_own
    )

    prior8 = jnp.broadcast_to(prior_weights[None, :], (8, count))
    weights = chain(weights_own, block_own, befores, combined, prior8, steps, stride, head)
    mine = lax.dynamic_slice_in_dim(weights[:local], row_start, own_rows, 1)
    return count * mine


def solution(mesh):
    return jax.shard_map(
        shards,
        mesh=mesh,
        in_specs=(P("tm", None, None), P("tm", None), P("tm", None), P("tm"), P(), P(), P()),
        out_specs=P("tm", "rows"),
        check_vma=False,
    )
```
